32 devices in a mesh: groups: 2 (over y), qry: 4 (over x, core), ref: 4 (over z).
Axes of the slice: x: 2, y: 2, z: 4, core: 2. Of those that a mesh axis runs over, the one named last changes fastest.
Arguments:
- query_feats: bfloat16 [1024, 9, 3840], P(('groups', 'qry')), parts along dimension 0, may hold values from -6 to 6
- ref_feats: bfloat16 [256, 4, 9, 3840], P(('groups', 'ref'), 'qry'), parts along dimension 0, may hold values from -6 to 6
- pair_table: int32 [8, 4], P('groups'), parts along dimension 0, may hold values from 0 to 1, as said below
- lengths: int32 [4], P('groups'), parts along dimension 0, may hold values from 1 to 96, 128 in all
- query_len: int32 [2], P('groups'), parts along dimension 0, may hold values from 64 to 128
- conv1_weight: float32 [3, 3, 32], replicated, may hold values from -2 to 2
- conv1_bias: float32 [32], replicated, may hold values from -3 to 3
- conv2_weight: bfloat16 [3, 3, 64, 32], replicated, may hold values from -0.375 to 0.375
- conv2_bias: float32 [64], replicated, may hold values from -3 to 3
- conv3_weight: bfloat16 [3, 3, 128, 64], replicated, may hold values from -0.25 to 0.25
- conv3_bias: float32 [128], replicated, may hold values from -3 to 3
- conv4_weight: bfloat16 [128], replicated, may hold values from -0.5 to 0.5
- conv4_bias: float32 [1], replicated, may hold values from -3 to 3
Outputs:
- score_map: float32 [256, 128], P(('groups', 'qry'), 'ref'), parts along dimension 0
- video_scores: float32 [4], P('groups'), parts along dimension 0
The draws below stay inside these ranges and needn't reach their ends.
There are 2 independent parts, one for each index of `groups`. The reference program is written for one: setup_inputs(seed, part) draws one part's arguments, and reference() takes and returns one part's arrays. A program takes and returns all parts, laid end to end along the dimension named above; an argument that names none is the same for every part. Nothing has to cross between parts.
Inputs may be any that keep to these rules, and one draw needn't show every extreme that they name: `pair_table`: in each row, at most 1 of the 1 tiles in the block of one index of ref are 1, and some such block holds exactly 1 in every draw.
All inputs are finite; a program needn't handle non-finite values.
Results may differ from the reference program's by a relative error of at most 0.01.
Values may be sent and summed in bfloat16 or wider, within the bound.
No kernel may reach another device: no remote copies, remote signals or barrier semaphores. Data moves between devices by JAX's collectives and lax.ppermute only.
A program may use at most 128 MiB of HBM per device.

```python
import math
import jax
import jax.numpy as jnp
import numpy as np
from jax import lax

D = 3840
REGIONS = 9
FT = 128
C1 = 32
C2 = 64
C3 = 128
MOST = 1
RTD = 1
QT = 4
RT = 4
NQ = 512
NR = 512
VIDEOS = 2
N_REF = 4


def draw_pair_table(key, part):
    subkeys = jax.random.split(jax.random.fold_in(key, 17), 4)
    counts = jax.random.randint(subkeys[0], (QT, N_REF), 0, MOST + 1)
    pick_row = jax.random.randint(subkeys[1], (), 0, QT)
    pick_col = jax.random.randint(subkeys[2], (), 0, N_REF)
    forced = (jnp.arange(QT)[:, None] == pick_row) & (jnp.arange(N_REF)[None, :] == pick_col)
    counts = jnp.where(forced, MOST, counts)
    scores = jax.random.randint(subkeys[3], (QT, N_REF, RTD), 0, 1 << 20) * RTD + jnp.arange(RTD)
    ordering = jnp.argsort(scores, axis=-1, stable=True)
    placing = jnp.argsort(ordering, axis=-1, stable=True)
    return (placing < counts[..., None]).astype(jnp.int32).reshape(QT, RT)


def block_levels(own_key, shape, cuts, least, high):
    def one(axis_at, shards_of):
        heights = jax.random.uniform(jax.random.fold_in(jax.random.fold_in(own_key, 6), axis_at), (shards_of,), jnp.float32, least / len(cuts), high / len(cuts))
        return jnp.repeat(jnp.exp(heights), shape[axis_at] // shards_of).reshape((-1,) + (1,) * (len(shape) - axis_at - 1))

    level = one(*cuts[0])
    for cut in cuts[1:]:
        level = level * one(*cut)
    return level


def split_up(number_of, total, bound, slope):
    loads = [(1 << 20) // math.isqrt(standing ** slope) + 1 for standing in range(2, number_of + 1)]
    spare, holding = total - bound - (number_of - 1), [1] * (number_of - 1)
    while spare > 0:
        movable = [i for i in range(number_of - 1) if holding[i] < bound]
        pool, left = sum([loads[i] for i in movable]), spare
        for i in movable:
            addition = min(bound - holding[i], max(1, left * loads[i] // pool), spare)
            holding[i] = holding[i] + addition
            spare = spare - addition
    return np.array([bound] + holding)


def uneven_parts(key, number_of, total, most, slope):
    if number_of == 2:
        one = jax.random.randint(key, (), max(1, total - most), min(most, total - 1) + 1)
        return jnp.stack([one, total - one])
    sizes = jnp.asarray(split_up(number_of, total, most, slope), jnp.int32)
    pairs = (number_of - 1) // 2
    giver, receiver = sizes[1:1 + 2 * pairs:2], sizes[2:2 + 2 * pairs:2]
    slack = jnp.minimum(giver - 1, most - receiver)
    moved = jax.random.randint(jax.random.fold_in(key, 1), (pairs,), 0, 1 << 20) % (slack + 1)
    sizes = sizes.at[1:1 + 2 * pairs:2].set(giver - moved).at[2:2 + 2 * pairs:2].set(receiver + moved)
    return sizes[jax.random.permutation(jax.random.fold_in(key, 2), number_of)]


def gaussian(own_key, shape, scale, most, shards=(), kind=jnp.bfloat16):
    entries = jax.random.normal(own_key, shape, jnp.float32) * scale
    if len(shards) > 0:
        entries = block_levels(own_key, shape, shards, -0.22, 0.18) * entries
    return jnp.clip(entries, min=-most, max=most).astype(kind)


def setup_inputs(seed: int = 0, part: int = 0) -> dict:
    streams_of = jax.random.split(jax.random.key(seed), 14)
    own_keys = jax.random.split(jax.random.fold_in(streams_of[13], part), 14)
    return {
        "query_feats": gaussian(own_keys[0], (NQ, REGIONS, D), 1.0, 6.0, ((0, 4),)),
        "ref_feats": gaussian(own_keys[1], (NR // QT, QT, REGIONS, D), 1.0, 6.0, ((0, 4), (1, 4))),
        "pair_table": draw_pair_table(jax.random.fold_in(jax.random.fold_in(streams_of[13], part), 71), part),
        "lengths": uneven_parts(own_keys[3], VIDEOS, NR // 4, 3 * FT // 4, 1).astype(jnp.int32),
        "query_len": jax.random.randint(own_keys[4], (1,), NQ // 8, NQ // 4 + 1).astype(jnp.int32),
        "conv1_weight": gaussian(streams_of[5], (3, 3, C1), 9 ** -0.5, 2.0, (), jnp.float32),
        "conv1_bias": gaussian(streams_of[6], (C1,), 0.5, 3.0, (), jnp.float32),
        "conv2_weight": gaussian(streams_of[7], (3, 3, C2, C1), (9 * C1) ** -0.5, 0.375),
        "conv2_bias": gaussian(streams_of[8], (C2,), 0.5, 3.0, (), jnp.float32),
        "conv3_weight": gaussian(streams_of[9], (3, 3, C3, C2), (9 * C2) ** -0.5, 0.25),
        "conv3_bias": gaussian(streams_of[10], (C3,), 0.5, 3.0, (), jnp.float32),
        "conv4_weight": gaussian(streams_of[11], (C3,), C3 ** -0.5, 0.5),
        "conv4_bias": gaussian(streams_of[12], (1,), 0.5, 3.0, (), jnp.float32),
    }


def slot_table(mask, most):
    width = mask.shape[-1]
    ranking = (jnp.cumsum(mask, axis=-1) - 1).astype(jnp.int32)
    slot_ids = jnp.arange(most, dtype=jnp.int32)
    chosen = (mask[..., None, :] == 1) & (ranking[..., None, :] == slot_ids[:, None])
    picked = lax.optimization_barrier(jnp.sum(jnp.where(chosen, jnp.arange(width, dtype=jnp.int32), 0), axis=-1)).astype(jnp.int32)
    return (chosen, picked)

def frame_sims(query_mat, ref_mat, regions):
    products = lax.dot_general(query_mat, ref_mat, (((1,), (1,)), ((), ())), preferred_element_type=jnp.float32, precision=lax.Precision.HIGHEST)
    frames = query_mat.shape[0] // regions
    others = ref_mat.shape[0] // regions
    best = lax.optimization_barrier(jnp.max(products.reshape(frames, regions, others, regions), axis=3))
    return lax.optimization_barrier(jnp.sum(best, axis=1)) * (1.0 / (regions * math.sqrt(query_mat.shape[1])))

def conv_layer(padded, weights, bias, block_rows, use_relu, use_pool):
    channels = padded.shape[0]
    height = padded.shape[1] - 2
    width = padded.shape[2] - 2
    block_rows = math.gcd(height, block_rows)
    outputs = weights.shape[0]

    def one_block(position):
        window = lax.dynamic_slice_in_dim(padded, position * block_rows, block_rows + 2, 1)
        stacked = jnp.concatenate([window[:, shift_row:shift_row + block_rows, shift_col:shift_col + width] for shift_row in range(3) for shift_col in range(3)], axis=0)
        result = jnp.dot(weights, stacked.reshape(9 * channels, block_rows * width), preferred_element_type=jnp.float32, precision=lax.Precision.HIGHEST)
        result = (result + bias[:, None]).reshape(outputs, block_rows, width)
        if use_relu:
            result = jnp.maximum(result, 0.0)
        if use_pool:
            result = lax.optimization_barrier(jnp.max(result.reshape(outputs, block_rows // 2, 2, width // 2, 2), axis=(2, 4)))
        return result
    blocks = lax.map(one_block, jnp.arange(height // block_rows, dtype=jnp.int32))
    return jnp.transpose(blocks, (1, 0, 2, 3)).reshape(outputs, -1, blocks.shape[-1])

def rounded(values):
    return lax.optimization_barrier(values.astype(jnp.bfloat16)).astype(jnp.float32)

def padded_map(values):
    return jnp.pad(values, ((0, 0), (1, 1), (1, 1)))

def weight_matrix(weight):
    return jnp.transpose(weight, (2, 0, 1, 3)).reshape(weight.shape[2], -1).astype(jnp.float32)

def reference(query_feats, ref_feats, pair_table, lengths, query_len, conv1_weight, conv1_bias, conv2_weight, conv2_bias, conv3_weight, conv3_bias, conv4_weight, conv4_bias):
    queries = query_feats.astype(jnp.float32).reshape(QT, FT * REGIONS, D)
    references = ref_feats.astype(jnp.float32).reshape(RT, FT * REGIONS, D)
    chosen, picked = slot_table(pair_table.reshape(QT, N_REF, RTD), MOST)

    def tile_block(position):
        qry_index = position // N_REF
        ref_index = position % N_REF
        query_mat = queries[qry_index]

        def one_slot(slot_id):
            return frame_sims(query_mat, references[ref_index * RTD + picked[qry_index, ref_index, slot_id]], REGIONS)
        sims = lax.map(one_slot, jnp.arange(MOST, dtype=jnp.int32))
        placed = jnp.einsum('st,sqf->qtf', chosen[qry_index, ref_index].astype(jnp.float32), sims, precision=lax.Precision.HIGHEST)
        return placed.reshape(FT, RTD * FT)
    blocks = lax.map(tile_block, jnp.arange(QT * N_REF, dtype=jnp.int32))
    sim_map = blocks.reshape(QT, N_REF, FT, RTD * FT).transpose(0, 2, 1, 3).reshape(1, NQ, NR)
    first_weights = conv1_weight.astype(jnp.float32).transpose(2, 0, 1).reshape(C1, 9)
    first = rounded(conv_layer(padded_map(sim_map), first_weights, conv1_bias, 32, True, True))
    second = rounded(conv_layer(padded_map(first), weight_matrix(conv2_weight), conv2_bias, 16, True, True))
    third = rounded(conv_layer(padded_map(second), weight_matrix(conv3_weight), conv3_bias, 16, True, False))
    last_weights = conv4_weight.astype(jnp.float32).reshape(1, C3)
    score_map = jnp.dot(last_weights, third.reshape(C3, -1), preferred_element_type=jnp.float32, precision=lax.Precision.HIGHEST).reshape(NQ // 4, NR // 4) + conv4_bias[0]
    ends = jnp.cumsum(lengths).astype(jnp.int32)
    starts = ends - lengths
    column = jnp.arange(NR // 4, dtype=jnp.int32)
    member = (column[:, None] >= starts[None, :]) & (column[:, None] < ends[None, :])
    peaks = lax.optimization_barrier(jnp.max(jnp.where(member[None], score_map[:, :, None], -jnp.inf), axis=1))
    row_ids = jnp.arange(NQ // 4, dtype=jnp.int32)
    totals = lax.optimization_barrier(jnp.sum(jnp.where((row_ids < query_len[0])[:, None], peaks, 0.0), axis=0))
    return (score_map, totals / query_len[0].astype(jnp.float32))
```

```python
import functools
import math

import jax
import jax.numpy as jnp
import numpy as np
from jax import lax
from jax.experimental import pallas as pl
from jax.experimental.pallas import tpu as pltpu
from jax.sharding import PartitionSpec as P

PIECE = 8
PHASES = 4
HALO = 2
JP = 48
GROUP = 3
WINDOW = PHASES * GROUP + 2
BF = jnp.bfloat16
F32 = jnp.float32


def shift(array, axis, pairs):
    return lax.ppermute(array, axis, pairs)


def sims_kernel(scale, regions, counts, pos_ref, table_ref, query_ref, *refs):
    pieces, outs = refs[: len(counts)], refs[len(counts) :]
    step = pl.program_id(0)
    width = query_ref.shape[0]
    active = table_ref[pos_ref[0], pos_ref[1]] == 1
    factor = jnp.where(active, scale, 0.0).astype(F32)
    for count, piece, out in zip(counts, pieces, outs):
        products = lax.dot_general(
            piece[...],
            query_ref[...].reshape(-1, query_ref.shape[2]),
            (((1,), (1,)), ((), ())),
            preferred_element_type=F32,
        )
        best = products[0:count]
        for other in range(1, regions):
            best = jnp.maximum(best, products[other * count : (other + 1) * count])
        frames = query_ref.shape[1]
        total = best[:, 0:frames]
        for other in range(1, width):
            total = total + best[:, other * frames : (other + 1) * frames]
        total = total * factor

        @pl.when(step == 0)
        def _():
            out[...] = total

        @pl.when(step > 0)
        def _():
            out[...] += total


def similarities(query, pieces, position, table):
    regions, frames, channels = query.shape
    counts = [piece.shape[0] // regions for piece in pieces]
    width = 3 if regions % 3 == 0 else 1
    scale = 1.0 / (regions * math.sqrt(channels))
    rows = sum(piece.shape[0] for piece in pieces)
    return pl.pallas_call(
        functools.partial(sims_kernel, scale, regions, counts),
        grid=(regions // width,),
        in_specs=[
            pl.BlockSpec(memory_space=pltpu.SMEM),
            pl.BlockSpec(memory_space=pltpu.SMEM),
            pl.BlockSpec((width, frames, channels), lambda i: (i, 0, 0)),
        ]
        + [pl.BlockSpec(piece.shape, lambda i: (0, 0)) for piece in pieces],
        out_specs=[pl.BlockSpec((count, frames), lambda i: (0, 0)) for count in counts],
        out_shape=[jax.ShapeDtypeStruct((count, frames), F32) for count in counts],
        cost_estimate=pl.CostEstimate(
            flops=2 * rows * regions * frames * channels,
            bytes_accessed=2 * channels * (rows + regions * frames),
            transcendentals=0,
        ),
        name="similarities",
    )(position, table, query, *pieces)


def network_kernel(
    map_rows,
    map_cols,
    pos_ref,
    len_ref,
    own_ref,
    left_ref,
    right_ref,
    top_ref,
    bottom_ref,
    w1_ref,
    b1_ref,
    w2_ref,
    b2_ref,
    w3_ref,
    b3_ref,
    w4_ref,
    b4_ref,
    score_ref,
    peak_ref,
    sims_ref,
    y_ref,
    first_ref,
    lhs2_ref,
    second_ref,
    lhs3_ref,
    flat_ref,
):
    block = own_ref.shape[1]
    frames = own_ref.shape[2]
    cells = block + 2 * HALO
    groups = cells // GROUP
    row0 = pos_ref[0] * block
    col0 = pos_ref[1] * block
    videos = len_ref.shape[0]

    lanes = sims_ref.shape[2]
    edge = top_ref.shape[2]
    sims_ref[...] = jnp.zeros_like(sims_ref)
    sims_ref[:, 3 : 3 + block, 0:frames] = own_ref[...]
    sims_ref[:, 1:3, 0:frames] = left_ref[...]
    sims_ref[:, 3 + block : 5 + block, 0:frames] = right_ref[...]
    sims_ref[:, 1 : 1 + cells, frames : frames + edge] = bottom_ref[...]
    sims_ref[:, 1 : 1 + cells, lanes - edge : lanes] = top_ref[...]

    sources = [(PHASES - 1, 0)] + [(phase, 1) for phase in range(PHASES)] + [(0, 2)]
    bases = [sims_ref[phase, at : at + JP, :] for phase, at in sources]
    zero = jnp.zeros((JP, 128 - len(sources) * WINDOW), F32)
    reach = PHASES * HALO + 1
    for group in range(groups):
        low = PHASES * GROUP * group - reach
        parts = []
        for base in bases:
            if low < 0:
                parts.append(base[:, lanes + low : lanes])
                parts.append(base[:, 0 : low + WINDOW])
            else:
                parts.append(base[:, low : low + WINDOW])
        window = jnp.concatenate(parts + [zero], axis=1)
        high = window.astype(BF)
        rest = (window - high.astype(F32)).astype(BF)
        y_ref[group * JP : (group + 1) * JP, 0:128] = high
        y_ref[group * JP : (group + 1) * JP, 128:256] = rest
        y_ref[group * JP : (group + 1) * JP, 256:384] = high

    cell = lax.broadcasted_iota(jnp.int32, (JP, 128), 0)
    lane = lax.broadcasted_iota(jnp.int32, (JP, 128), 1)

    def inside(halo):
        at = cell + (col0 - halo)
        return jnp.where((at >= 0) & (at < map_cols), 1.0, 0.0).astype(F32)

    def row_flag(at):
        return jnp.where((at >= 0) & (at < map_rows), 1.0, 0.0).astype(F32)

    cols_first = inside(HALO)
    for member in range(GROUP):
        result = jnp.dot(
            y_ref[...], w1_ref[:, member * 512 : (member + 1) * 512], preferred_element_type=F32
        )
        pooled = jnp.maximum(
            jnp.maximum(result[:, 0:128], result[:, 128:256]),
            jnp.maximum(result[:, 256:384], result[:, 384:512]),
        )
        pooled = jnp.maximum(pooled + b1_ref[...], 0.0)
        for group in range(groups):
            at = group * GROUP + member
            keep = cols_first * row_flag(row0 + at - HALO)
            first_ref[at] = (pooled[group * JP : (group + 1) * JP] * keep).astype(BF).astype(F32)

    upper = lane < 64
    left = (lane // 32) % 2 == 0
    rows2 = block + 2
    for at in range(rows2):
        centre = first_ref[at + 1]
        across = jnp.where(upper, first_ref[at + 2], first_ref[at])
        for index, value in enumerate((centre, across)):
            here = pltpu.roll(value, JP - 1, 0)
            beside = jnp.where(left, pltpu.roll(value, JP - 2, 0), value)
            lhs2_ref[at * JP : (at + 1) * JP, index * 256 : index * 256 + 128] = here.astype(BF)
            lhs2_ref[at * JP : (at + 1) * JP, index * 256 + 128 : index * 256 + 256] = (
                beside.astype(BF)
            )
    result = jnp.dot(lhs2_ref[...], w2_ref[...], preferred_element_type=F32)
    pooled = jnp.maximum(result[:, 0:128], result[:, 128:256])
    pooled = jnp.maximum(pooled, pltpu.roll(pooled, 64, 1))
    pooled = jnp.maximum(pooled + b2_ref[...], 0.0)
    cols_second = inside(1)
    for at in range(rows2):
        keep = cols_second * row_flag(row0 + at - 1)
        second_ref[at] = (pooled[at * JP : (at + 1) * JP] * keep).astype(BF).astype(F32)

    upper = lane[0:block] < 64
    for at in range(block):
        row = slice(at * block, (at + 1) * block)
        for down in range(3):
            value = second_ref[at + down]
            pair = jnp.where(upper, value[0:block], value[1 : 1 + block])
            lhs3_ref[row, down * 128 : (down + 1) * 128] = pair.astype(BF)
        pair = jnp.where(
            upper, second_ref[at, 2 : 2 + block, :], second_ref[at + 1, 2 : 2 + block, :]
        )
        lhs3_ref[row, 384:512] = pair.astype(BF)
        lhs3_ref[row, 512:640] = second_ref[at + 2, 2 : 2 + block, :].astype(BF)
    third = jnp.dot(lhs3_ref[...], w3_ref[...], preferred_element_type=F32)
    third = jnp.maximum(third + b3_ref[...], 0.0).astype(BF)
    flat = lax.dot_general(
        w4_ref[...], third, (((1,), (1,)), ((), ())), preferred_element_type=F32
    )
    flat_ref[...] = flat[0:8] + b4_ref[0]
    for at in range(block):
        score_ref[at : at + 1, :] = flat_ref[0:1, at * block : (at + 1) * block]

    score = score_ref[...]
    column = col0 + lax.broadcasted_iota(jnp.int32, (block, block), 1)
    slot = lax.broadcasted_iota(jnp.int32, (block, videos), 1)
    start = jnp.int32(0)
    peaks = jnp.zeros((block, videos), F32)
    for video in range(videos):
        end = start + len_ref[video]
        member = (column >= start) & (column < end)
        best = jnp.max(jnp.where(member, score, -jnp.inf), axis=1, keepdims=True)
        peaks = jnp.where(slot == video, best, peaks)
        start = end
    peak_ref[...] = peaks


def network(position, lengths, own, left, right, top, bottom, weights, map_rows, map_cols):
    block = own.shape[1]
    frames = own.shape[2]
    cells = block + 2 * HALO
    videos = lengths.shape[0]
    smem = pl.BlockSpec(memory_space=pltpu.SMEM)
    vmem = pl.BlockSpec(memory_space=pltpu.VMEM)
    w1, b1, w2, b2, w3, b3, w4, b4 = weights
    return pl.pallas_call(
        functools.partial(network_kernel, map_rows, map_cols),
        in_specs=[smem, smem] + [vmem] * 5 + [vmem] * 7 + [smem],
        out_specs=[vmem, vmem],
        out_shape=[
            jax.ShapeDtypeStruct((block, block), F32),
            jax.ShapeDtypeStruct((block, videos), F32),
        ],
        scratch_shapes=[
            pltpu.VMEM((PHASES, JP + 8, 2 * frames), F32),
            pltpu.VMEM((cells // GROUP * JP, 384), BF),
            pltpu.VMEM((cells, JP, 128), F32),
            pltpu.VMEM(((block + 2) * JP, 512), BF),
            pltpu.VMEM((block + 2, JP, 128), F32),
            pltpu.VMEM((block * block, 640), BF),
            pltpu.VMEM((8, block * block), F32),
        ],
        cost_estimate=pl.CostEstimate(
            flops=2_000_000_000, bytes_accessed=4_000_000, transcendentals=0
        ),
        name="network",
    )(position, lengths, own, left, right, top, bottom, w1, b1, w2, b2, w3, b3, w4, b4)


def network_weights(w1, b1, w2, b2, w3, b3, w4, b4):
    c1, c2, c3 = w1.shape[2], w2.shape[2], w3.shape[2]
    rows = np.arange(6 * WINDOW)
    member, pr, pc, sr, sc, _ = np.unravel_index(
        np.arange(GROUP * 16 * c1), (GROUP, 2, 2, 2, 2, c1)
    )
    down = jnp.asarray(rows % WINDOW, jnp.int32)[:, None] - jnp.asarray(
        PHASES * member + 2 * sr + pr, jnp.int32
    )
    along = jnp.asarray(rows // WINDOW, jnp.int32)[:, None] - jnp.asarray(2 * sc + pc, jnp.int32)
    tiled = jnp.tile(w1.astype(F32), (1, 1, GROUP * 16))
    dense = jnp.zeros((6 * WINDOW, GROUP * 16 * c1), F32)
    for di in range(3):
        for dj in range(3):
            dense = jnp.where((down == di) & (along == dj), tiled[di, dj][None, :], dense)
    dense = jnp.pad(dense, ((0, 128 - 6 * WINDOW), (0, 0)))
    high = lax.reduce_precision(dense, 8, 7)
    rest = (dense - high).astype(BF)
    high = high.astype(BF)
    first = jnp.concatenate([high, high, rest], axis=0)
    taps = jnp.transpose(w2, (0, 1, 3, 2))
    nothing = jnp.zeros((c1, c2), w2.dtype)
    reach = ((0, 1), (2, -1))
    columns = []
    for qr in range(2):
        for qc in range(2):
            column = []
            for row_kind in range(2):
                for col_kind in range(2):
                    for sr in range(2):
                        for sc in range(2):
                            di = reach[row_kind][sr] - qr + 1
                            dj = reach[col_kind][sc] - qc + 1
                            fits = 0 <= di <= 2 and 0 <= dj <= 2
                            column.append(taps[di, dj] if fits else nothing)
            columns.append(jnp.concatenate(column, axis=0))
    second = jnp.concatenate(columns, axis=1)
    taps = jnp.transpose(w3, (0, 1, 3, 2))
    order = [(0, 0), (0, 1), (1, 0), (1, 1), (2, 0), (2, 1), (0, 2), (1, 2), (2, 2)]
    third = jnp.concatenate(
        [taps[di, dj] for di, dj in order] + [jnp.zeros((c2, c3), w3.dtype)], axis=0
    )
    fourth = jnp.broadcast_to(w4[None], (16, c3))
    return (
        first,
        jnp.tile(b1, 128 // c1)[None],
        second,
        jnp.tile(b2, 128 // c2)[None],
        third,
        b3[None],
        fourth,
        b4,
    )


def body(
    query_feats,
    ref_feats,
    pair_table,
    lengths,
    query_len,
    conv1_weight,
    conv1_bias,
    conv2_weight,
    conv2_bias,
    conv3_weight,
    conv3_bias,
    conv4_weight,
    conv4_bias,
):
    qry_index = lax.axis_index("qry")
    ref_index = lax.axis_index("ref")
    senders = lax.axis_size("qry")
    blocks = lax.axis_size("ref")
    position = jnp.stack([qry_index, ref_index]).astype(jnp.int32)
    frames, regions, channels = query_feats.shape
    rows = ref_feats.shape[0]
    query = jnp.transpose(query_feats, (1, 0, 2))
    own = jnp.transpose(ref_feats[:, 0], (1, 0, 2))
    chips = senders // 2
    count = rows // PIECE
    order = [0, count - 1] + list(range(1, count - 1)) if count > 1 else [0]
    pieces = [
        own[:, at * PIECE : (at + 1) * PIECE].reshape(regions * PIECE, channels) for at in order
    ]
    across = [
        [(i, (i - 2 * step) % senders) for i in range(senders)] for step in range(1, chips)
    ]
    beside = [(i, i ^ 1) for i in range(senders)]

    whole = own.reshape(regions * rows, channels)
    found = [[shift(piece, "qry", pairs) for piece in pieces] for pairs in across]
    sibling = shift(whole, "qry", beside)
    tile = [similarities(query, [whole], position, pair_table)[0]]
    tile.append(similarities(query, [sibling], position, pair_table)[0])
    for group in found:
        here, there = [None] * count, [None] * count
        for at, piece in zip(order, group):
            other = shift(piece, "qry", beside)
            here[at], there[at] = similarities(query, [piece, other], position, pair_table)
        tile.append(jnp.concatenate(here, axis=0))
        tile.append(jnp.concatenate(there, axis=0))
    relative = jnp.stack(tile)
    sender = jnp.arange(senders, dtype=jnp.int32)
    step = (sender // 2 - qry_index // 2) % chips
    source = 2 * step + (sender % 2) ^ (qry_index % 2)
    ordered = relative[source]
    sims = (
        ordered.reshape(senders // PHASES, PHASES, rows, frames)
        .transpose(1, 2, 0, 3)
        .reshape(PHASES, frames // PHASES, frames)
    )
    up = [(i, i + 1) for i in range(blocks - 1)]
    down = [(b, a) for a, b in up]
    left = shift(sims[:, -HALO:], "ref", up)
    right = shift(sims[:, :HALO], "ref", down)
    wide = jnp.concatenate([left, sims, right], axis=1)
    up = [(i, i + 1) for i in range(senders - 1)]
    down = [(b, a) for a, b in up]
    top = shift(wide[:, :, frames - 8 :], "qry", up)
    bottom = shift(wide[:, :, :8], "qry", down)
    weights = network_weights(
        conv1_weight,
        conv1_bias,
        conv2_weight,
        conv2_bias,
        conv3_weight,
        conv3_bias,
        conv4_weight,
        conv4_bias,
    )
    block = frames // PHASES
    score_map, peaks = network(
        position, lengths, sims, left, right, top, bottom, weights, block * senders, block * blocks
    )
    best = peaks
    for step in range(1, blocks):
        pairs = [(i, (i + step) % blocks) for i in range(blocks)]
        best = jnp.maximum(best, shift(peaks, "ref", pairs))
    row_ids = qry_index * block + jnp.arange(block, dtype=jnp.int32)
    partial = jnp.sum(jnp.where((row_ids < query_len[0])[:, None], best, 0.0), axis=0)
    total = partial
    for step in range(1, senders):
        pairs = [(i, (i + step) % senders) for i in range(senders)]
        total = total + shift(partial, "qry", pairs)
    return (score_map, total / query_len[0].astype(F32))


def solution(mesh):
    placed = (
        P(("groups", "qry"), None, None),
        P(("groups", "ref"), "qry", None, None),
        P("groups", None),
        P("groups"),
        P("groups"),
    ) + (P(),) * 8
    return jax.shard_map(
        body,
        mesh=mesh,
        in_specs=placed,
        out_specs=(P(("groups", "qry"), "ref"), P("groups")),
        check_vma=False,
    )
```

```python
import functools
import math

import jax
import jax.numpy as jnp
from jax import lax
from jax.experimental import pallas as pl
from jax.experimental.pallas import tpu as pltpu
from jax.sharding import PartitionSpec as P


GRANT = 20 * 1024 * 1024
PIECE = 8
PHASES = 4
HALO = 2
EDGE = 8
GROUP = 3
WINDOW = PHASES * GROUP + 2
BF = jnp.bfloat16
F32 = jnp.float32


def in_hbm(array):
    return pltpu.with_memory_space_constraint(array, pltpu.HBM)


def shift(array, axis, pairs):
    return lax.ppermute(array, axis, pairs)


def cut_kernel(order, source_ref, *refs):
    outs, sems = refs[:-1], refs[-1]
    copies = []
    for index, (at, out) in enumerate(zip(order, outs)):
        piece = source_ref.at[:, pl.ds(at * PIECE, PIECE), :]
        copies.append(pltpu.make_async_copy(piece, out, sems.at[index]))
    for copy in copies:
        copy.start()
    for copy in copies:
        copy.wait()


def cut(source, order):
    regions, _, channels = source.shape
    shape = (regions, PIECE, channels)
    pieces = pl.pallas_call(
        functools.partial(cut_kernel, order),
        in_specs=[pl.BlockSpec(memory_space=pltpu.HBM)],
        out_specs=[pl.BlockSpec(memory_space=pltpu.VMEM) for _ in order],
        out_shape=[jax.ShapeDtypeStruct(shape, source.dtype) for _ in order],
        scratch_shapes=[pltpu.SemaphoreType.DMA((len(order),))],
        compiler_params=pltpu.CompilerParams(vmem_limit_bytes=GRANT),
        cost_estimate=pl.CostEstimate(
            flops=0, bytes_accessed=4 * source.size, transcendentals=0
        ),
        name="cut",
    )(in_hbm(source))
    return [piece.reshape(regions * PIECE, channels) for piece in pieces]


def write_edges(pos_ref, arrays, core_ref, chip_ref):
    total = jnp.concatenate(arrays, axis=0)
    frames = total.shape[1]
    eights = [total[at : at + 8] for at in range(0, total.shape[0], 8)]
    first = jnp.concatenate([eight[:, 0:EDGE] for eight in eights], axis=1)
    last = jnp.concatenate([eight[:, frames - EDGE : frames] for eight in eights], axis=1)
    even = pos_ref[0] % 2 == 0
    core_ref[...] = jnp.where(even, last, first)
    chip_ref[...] = jnp.where(even, first, last)


def edge_shapes(columns):
    return [jax.ShapeDtypeStruct((8, columns // 8 * EDGE), F32)] * 2


def edges_kernel(pos_ref, *refs):
    write_edges(pos_ref, [ref[...] for ref in refs[:-2]], *refs[-2:])


def edge_rows(position, sources):
    smem = pl.BlockSpec(memory_space=pltpu.SMEM)
    vmem = pl.BlockSpec(memory_space=pltpu.VMEM)
    return pl.pallas_call(
        edges_kernel,
        in_specs=[smem] + [vmem for _ in sources],
        out_specs=[vmem, vmem],
        out_shape=edge_shapes(sum(source.shape[0] for source in sources)),
        name="edges",
    )(position, *sources)


def sims_kernel(scale, spans, others, fetch, pos_ref, table_ref, query_ref, *refs):
    pieces, refs = refs[: len(spans)], refs[len(spans) :]
    done, refs = refs[:others], refs[others:]
    out_ref = refs[0]
    if fetch:
        rows_ref, sems = refs[-2], refs[-1]
    regions, frames, channels = query_ref.shape
    width = 3 if regions % 3 == 0 else 1
    if fetch:
        copies, arriving = [], []
        start = 0
        for index, (span, piece) in enumerate(zip(spans, pieces)):
            rows = pl.ds(start, span * regions)
            copies.append(pltpu.make_async_copy(piece, rows_ref.at[rows, :], sems.at[index]))
            start += span * regions
        for copy in copies:
            copy.start()
        for step in range(regions // width):
            block = pl.ds(step * width, width)
            arriving.append(
                pltpu.make_async_copy(
                    query_ref.at[block], refs[1].at[block], sems.at[len(spans) + step]
                )
            )
        for copy in arriving:
            copy.start()
        query_ref = refs[1]
        for copy in copies:
            copy.wait()

    total = None
    for step in range(regions // width):
        if fetch:
            arriving[step].wait()
        rows = (
            rows_ref[...]
            if fetch
            else jnp.concatenate([piece[...] for piece in pieces], axis=0)
        )
        products = lax.dot_general(
            rows,
            query_ref[step * width : (step + 1) * width].reshape(-1, channels),
            (((1,), (1,)), ((), ())),
            preferred_element_type=F32,
        )
        parts = []
        start = 0
        for span in spans:
            best = products[start : start + span]
            for other in range(1, regions):
                best = jnp.maximum(
                    best, products[start + other * span : start + (other + 1) * span]
                )
            part = best[:, 0:frames]
            for other in range(1, width):
                part = part + best[:, other * frames : (other + 1) * frames]
            parts.append(part)
            start += span * regions
        part = jnp.concatenate(parts, axis=0)
        total = part if total is None else total + part
    active = table_ref[pos_ref[0], pos_ref[1]] == 1
    total = total * jnp.where(active, scale, 0.0).astype(F32)
    out_ref[...] = total
    if done:
        write_edges(pos_ref, [ref[...] for ref in done] + [total], *refs[1:3])


def similarities(query, pieces, position, table, done=(), fetch=False):
    regions, frames, channels = query.shape
    spans = [piece.shape[0] // regions for piece in pieces]
    scale = 1.0 / (regions * math.sqrt(channels))
    rows = sum(spans)
    shapes = [jax.ShapeDtypeStruct((rows, frames), F32)]
    if done:
        shapes += edge_shapes(rows + sum(array.shape[0] for array in done))
    steps = 0
    if fetch:
        shapes.append(pltpu.VMEM(query.shape, query.dtype))
        steps = regions
    smem = pl.BlockSpec(memory_space=pltpu.SMEM)
    vmem = pl.BlockSpec(memory_space=pltpu.VMEM)
    return pl.pallas_call(
        functools.partial(sims_kernel, scale, spans, len(done), fetch),
        in_specs=[smem, smem, pl.BlockSpec(memory_space=pltpu.HBM) if fetch else vmem]
        + [pl.BlockSpec(memory_space=pltpu.HBM) if fetch else vmem for _ in pieces]
        + [vmem for _ in done],
        out_specs=[vmem for _ in shapes],
        out_shape=shapes,
        scratch_shapes=[
            pltpu.VMEM((rows * regions, channels), BF),
            pltpu.SemaphoreType.DMA((len(pieces) + steps,)),
        ]
        if fetch
        else [],
        compiler_params=pltpu.CompilerParams(vmem_limit_bytes=GRANT),
        cost_estimate=pl.CostEstimate(
            flops=2 * rows * regions * regions * frames * channels,
            bytes_accessed=2 * channels * regions * rows,
            transcendentals=0,
        ),
        name="similarities",
    )(position, table, *(map(in_hbm, (query, *pieces)) if fetch else (query, *pieces)), *done)


def convolve(sims_ref, weights, scratch, score_ref, pos_ref, block, limits, padding):
    w1_ref, b1_ref, w2_ref, b2_ref, w3_ref, b3_ref, w4_ref, b4_ref = weights
    y_ref, first_ref, lhs2_ref, second_ref, lhs3_ref = scratch
    map_rows, map_cols = limits
    jf, js, jt = padding
    rows1 = block + 2 * HALO
    groups = rows1 // GROUP
    row0 = pos_ref[0] * block
    col0 = pos_ref[1] * block
    lanes = sims_ref.shape[2]

    sources = [(PHASES - 1, 0)] + [(phase, 1) for phase in range(PHASES)] + [(0, 2)]
    bases = [sims_ref[phase, at : at + jf, :] for phase, at in sources]
    terms = len(sources) * WINDOW
    zero = jnp.zeros((jf, 128 - terms), F32)
    reach = PHASES * HALO + 1
    lane = lax.broadcasted_iota(jnp.int32, (jf, 128), 1)
    for group in range(groups):
        low = PHASES * GROUP * group - reach
        parts = []
        for base in bases:
            if low < 0:
                parts.append(base[:, lanes + low : lanes])
                parts.append(base[:, 0 : low + WINDOW])
            else:
                parts.append(base[:, low : low + WINDOW])
        window = jnp.concatenate(parts + [zero], axis=1)
        high = window.astype(BF).astype(F32)
        rest = pltpu.roll(window - high, terms, 1)
        again = pltpu.roll(high, 2 * terms - 128, 1)
        row = slice(group * jf, (group + 1) * jf)
        y_ref[row, 0:128] = jnp.where(lane < terms, high, rest).astype(BF)
        y_ref[row, 128:256] = jnp.where(lane < 2 * terms - 128, rest, again).astype(BF)

    cell = lax.broadcasted_iota(jnp.int32, (jf, 128), 0)

    def inside(halo, count):
        at = cell[0:count] + (col0 - halo)
        return jnp.where((at >= 0) & (at < map_cols), 1.0, 0.0).astype(F32)

    def row_flag(at):
        return jnp.where((at >= 0) & (at < map_rows), 1.0, 0.0).astype(F32)

    keep_cols = inside(HALO, jf)
    for member in range(GROUP):
        result = jnp.dot(
            y_ref[0 : groups * jf, :],
            w1_ref[:, member * 512 : (member + 1) * 512],
            preferred_element_type=F32,
        )
        pooled = jnp.maximum(
            jnp.maximum(result[:, 0:128], result[:, 128:256]),
            jnp.maximum(result[:, 256:384], result[:, 384:512]),
        )
        pooled = jnp.maximum(pooled + b1_ref[...], 0.0)
        for group in range(groups):
            at = group * GROUP + member
            keep = keep_cols * row_flag(row0 + at - HALO)
            first_ref[at, 0:jf, :] = (
                (pooled[group * jf : (group + 1) * jf] * keep).astype(BF).astype(F32)
            )

    upper = lane < 64
    left = (lane // 32) % 2 == 0
    rows2 = block + 2
    for at in range(rows2):
        centre = first_ref[at + 1, 0:jf, :]
        across = jnp.where(upper, first_ref[at + 2, 0:jf, :], first_ref[at, 0:jf, :])
        row = slice(at * js, (at + 1) * js)
        for index, value in enumerate((centre, across)):
            here = pltpu.roll(value, jf - 1, 0)
            beside = jnp.where(left, pltpu.roll(value, jf - 2, 0), value)
            lhs2_ref[row, index * 256 : index * 256 + 128] = here[0:js].astype(BF)
            lhs2_ref[row, index * 256 + 128 : index * 256 + 256] = beside[0:js].astype(BF)
    result = jnp.dot(lhs2_ref[0 : rows2 * js, :], w2_ref[...], preferred_element_type=F32)
    pooled = jnp.maximum(result[:, 0:128], result[:, 128:256])
    pooled = jnp.maximum(pooled, pltpu.roll(pooled, 64, 1))
    pooled = jnp.maximum(pooled + b2_ref[...], 0.0)
    keep_cols = inside(1, js)
    for at in range(rows2):
        keep = keep_cols * row_flag(row0 + at - 1)
        second_ref[at, 0:js, :] = (pooled[at * js : (at + 1) * js] * keep).astype(BF).astype(F32)
        if js < jt + 8:
            second_ref[at, js : jt + 8, :] = jnp.zeros((jt + 8 - js, 128), F32)

    upper = upper[0:jt]
    for at in range(block // 2):
        row = slice(at * jt, (at + 1) * jt)
        rows = [second_ref.at[2 * at + down] for down in range(4)]
        for down in range(4):
            pair = jnp.where(upper, rows[down][0:jt, :], rows[down][1 : 1 + jt, :])
            lhs3_ref[row, down * 128 : (down + 1) * 128] = pair.astype(BF)
        for half in range(2):
            pair = jnp.where(
                upper, rows[2 * half][2 : 2 + jt, :], rows[2 * half + 1][2 : 2 + jt, :]
            )
            lhs3_ref[row, (4 + half) * 128 : (5 + half) * 128] = pair.astype(BF)
    third = jnp.dot(lhs3_ref[...], w3_ref[...], preferred_element_type=F32)
    third = jnp.maximum(third + b3_ref[...], 0.0).astype(BF)
    flat = lax.dot_general(
        w4_ref[...], third, (((1,), (1,)), ((), ())), preferred_element_type=F32
    )
    flat = flat[0:8] + b4_ref[0]
    for at in range(block // 2):
        score_ref[2 * at : 2 * at + 2, :] = flat[0:2, at * jt : at * jt + block]


def pad_cells(cells):
    js = -(-(cells + 2) // 8) * 8
    return (max(-(-(cells + 4) // 8) * 8, js), js, -(-cells // 16) * 16)


def convolve_scratch(block, padding):
    jf, js, jt = padding
    rows1 = block + 2 * HALO
    return [
        pltpu.VMEM((rows1 // GROUP * jf, 256), BF),
        pltpu.VMEM((rows1, jf, 128), F32),
        pltpu.VMEM(((block + 2) * js, 512), BF),
        pltpu.VMEM((block + 2, max(js, jt + 8), 128), F32),
        pltpu.VMEM((block // 2 * jt, 768), BF),
    ]


def place(pos_ref, sims_ref, sources, segments):
    for source, row, size, shard, cell in segments:
        if source < len(sources):
            rows = slice(3 + cell, 3 + cell + size)
            sims_ref[pos_ref[2 + shard], rows, 0 : sources[source].shape[1]] = sources[source][
                row : row + size, :
            ]


def place_edges(pos_ref, sims_ref, starts, segments, table, edge_ref, side):
    for source, row, size, shard, cell in segments:
        for at in range(0, size, 8):
            start = starts[source] + row + at
            count = min(8, size - at)
            lane = start // 8 * EDGE
            sims_ref[pos_ref[table + shard], 3 + cell + at : 3 + cell + at + count, side] = edge_ref[
                start % 8 : start % 8 + count, lane : lane + EDGE
            ]


def assemble_kernel(segments, pos_ref, *refs):
    sources, sims_ref = refs[:-1], refs[-1]
    sims_ref[...] = jnp.zeros_like(sims_ref)
    place(pos_ref, sims_ref, sources, segments)


def assembled(position, sources, segments, block):
    smem = pl.BlockSpec(memory_space=pltpu.SMEM)
    vmem = pl.BlockSpec(memory_space=pltpu.VMEM)
    frames = sources[0].shape[1]
    return pl.pallas_call(
        functools.partial(assemble_kernel, segments),
        in_specs=[smem] + [vmem for _ in sources],
        out_specs=vmem,
        out_shape=jax.ShapeDtypeStruct((PHASES, block + 24, 2 * frames), F32),
        compiler_params=pltpu.CompilerParams(vmem_limit_bytes=GRANT),
        cost_estimate=pl.CostEstimate(flops=0, bytes_accessed=500_000, transcendentals=0),
        name="assemble",
    )(position, *sources)


def network_kernel(limits, padding, starts, segments, pos_ref, len_ref, base_ref, *refs):
    (late_ref, core_ref, chip_ref), refs = refs[:3], refs[3:]
    weights, (score_ref, peak_ref, sims_ref), scratch = refs[:8], refs[8:11], refs[11:]
    block = score_ref.shape[0]
    last = len(starts) - 1
    place(
        pos_ref, sims_ref, [late_ref], [(0, *rest) for source, *rest in segments if source == last]
    )
    lanes = sims_ref.shape[2]
    above, below = slice(lanes - EDGE, lanes), slice(lanes // 2, lanes // 2 + EDGE)

    def edges(core_side, chip_side):
        place_edges(pos_ref, sims_ref, starts, segments, 6, core_ref, core_side)
        place_edges(pos_ref, sims_ref, starts, segments, 10, chip_ref, chip_side)

    pl.when(pos_ref[0] % 2 == 0)(lambda: edges(below, above))
    pl.when(pos_ref[0] % 2 == 1)(lambda: edges(above, below))
    convolve(sims_ref, weights, scratch, score_ref, pos_ref, block, limits, padding)

    score = score_ref[...]
    videos = len_ref.shape[0]
    column = pos_ref[1] * block + lax.broadcasted_iota(jnp.int32, (block, block), 1)
    slot = lax.broadcasted_iota(jnp.int32, (block, 128), 1)
    start = jnp.int32(0)
    peaks = jnp.zeros((block, 128), F32)
    for video in range(videos):
        end = start + len_ref[video]
        member = (column >= start) & (column < end)
        best = jnp.max(jnp.where(member, score, -jnp.inf), axis=1, keepdims=True)
        peaks = jnp.where(slot == video, best, peaks)
        start = end
    peak_ref[...] = jnp.transpose(peaks)[0:videos]


def network(position, lengths, base, late, edges, starts, segments, weights, block, limits):
    smem = pl.BlockSpec(memory_space=pltpu.SMEM)
    vmem = pl.BlockSpec(memory_space=pltpu.VMEM)
    padding = pad_cells(block)
    arrays = [base, late, *edges]
    score, peaks, _ = pl.pallas_call(
        functools.partial(network_kernel, limits, padding, starts, segments),
        in_specs=[smem, smem] + [vmem] * len(arrays) + [vmem] * 7 + [smem],
        out_specs=[vmem, vmem, vmem],
        out_shape=[
            jax.ShapeDtypeStruct((block, block), F32),
            jax.ShapeDtypeStruct((lengths.shape[0], block), F32),
            jax.ShapeDtypeStruct(base.shape, F32),
        ],
        scratch_shapes=convolve_scratch(block, padding),
        input_output_aliases={2: 2},
        cost_estimate=pl.CostEstimate(
            flops=6_000_000_000, bytes_accessed=4_000_000, transcendentals=0
        ),
        compiler_params=pltpu.CompilerParams(vmem_limit_bytes=GRANT),
        name="network",
    )(position, lengths, *arrays, *weights)
    return score, peaks


def weights_kernel(w1_ref, b1_ref, w2_ref, b2_ref, w3_ref, b3_ref, w4_ref, *outs):
    f1_ref, o1_ref, f2_ref, o2_ref, f3_ref, o3_ref, f4_ref = outs
    c1, c2, c3 = w1_ref.shape[2], w2_ref.shape[3], w3_ref.shape[3]
    rows = lax.broadcasted_iota(jnp.int32, (256, 16 * c1), 0)
    lane = lax.broadcasted_iota(jnp.int32, (256, 16 * c1), 1) // c1
    terms = 6 * WINDOW
    third = rows >= 2 * terms
    valid = rows < 3 * terms
    rows = rows - jnp.where(third, 2 * terms, jnp.where(rows >= terms, terms, 0))
    along = jnp.zeros_like(rows)
    for offset in range(1, 6):
        along = along + jnp.where(rows >= offset * WINDOW, 1, 0)
    down = rows - along * WINDOW - 2 * ((lane // 2) % 2) - lane // 8
    along = along - 2 * (lane % 2) - (lane // 4) % 2
    taps = []
    for di in range(3):
        for dj in range(3):
            tap = jnp.concatenate([w1_ref[di, dj : dj + 1, :]] * (128 // c1), axis=1)
            taps.append(jnp.concatenate([tap] * (16 * c1 // 128), axis=1))
    for member in range(GROUP):
        dense = jnp.zeros(rows.shape, F32)
        for di in range(3):
            for dj in range(3):
                here = (down == di + PHASES * member) & (along == dj) & valid
                dense = jnp.where(here, taps[3 * di + dj], dense)
        high = dense.astype(BF).astype(F32)
        at = slice(member * 16 * c1, (member + 1) * 16 * c1)
        f1_ref[:, at] = jnp.where(third, dense - high, high).astype(BF)
    o1_ref[...] = jnp.concatenate([b1_ref[...]] * (128 // c1), axis=1)
    o2_ref[...] = jnp.concatenate([b2_ref[...]] * (128 // c2), axis=1)
    f2_ref[...] = jnp.zeros_like(f2_ref)
    reach = ((0, 1), (2, -1))
    for index in range(16):
        row_kind, col_kind, sr, sc = (index >> 3) & 1, (index >> 2) & 1, (index >> 1) & 1, index & 1
        for phase in range(4):
            di = reach[row_kind][sr] - phase // 2 + 1
            dj = reach[col_kind][sc] - phase % 2 + 1
            if 0 <= di <= 2 and 0 <= dj <= 2:
                f2_ref[index * c1 : (index + 1) * c1, phase * c2 : (phase + 1) * c2] = w2_ref[
                    di, dj
                ]
    f3_ref[...] = jnp.zeros_like(f3_ref)
    order = [(row, col) for row in range(4) for col in range(2)] + [(row, 2) for row in range(4)]
    for index, (row, dj) in enumerate(order):
        for output in range(2):
            if 0 <= row - output <= 2:
                f3_ref[index * c2 : (index + 1) * c2, output * c3 : (output + 1) * c3] = w3_ref[
                    row - output, dj
                ]
    o3_ref[...] = jnp.concatenate([b3_ref[...]] * 2, axis=1)
    fourth = jnp.concatenate([w4_ref[...].astype(F32)] * 2, axis=1)
    half = lax.broadcasted_iota(jnp.int32, f4_ref.shape, 1) // c3
    output = lax.broadcasted_iota(jnp.int32, f4_ref.shape, 0)
    f4_ref[...] = jnp.where(half == output, fourth, 0.0).astype(BF)


def network_weights(w1, b1, w2, b2, w3, b3, w4, b4):
    c1, c2, c3 = w1.shape[2], w2.shape[2], w3.shape[2]
    shapes = [
        ((256, GROUP * 16 * c1), BF),
        ((1, 128), F32),
        ((16 * c1, 4 * c2), BF),
        ((1, 128), F32),
        ((12 * c2, 2 * c3), BF),
        ((1, 2 * c3), F32),
        ((16, 2 * c3), BF),
    ]
    f1, o1, f2, o2, f3, o3, f4 = pl.pallas_call(
        weights_kernel,
        out_shape=[jax.ShapeDtypeStruct(shape, dtype) for shape, dtype in shapes],
        cost_estimate=pl.CostEstimate(flops=100_000_000, bytes_accessed=4_000_000, transcendentals=0),
        compiler_params=pltpu.CompilerParams(vmem_limit_bytes=GRANT),
        name="weights",
    )(
        w1,
        b1[None],
        jnp.transpose(w2, (0, 1, 3, 2)),
        b2[None],
        jnp.transpose(w3, (0, 1, 3, 2)),
        b3[None],
        w4[None],
    )
    return (f1, o1, f2, o2, f3, o3, f4, b4)


def body(
    query_feats,
    ref_feats,
    pair_table,
    lengths,
    query_len,
    conv1_weight,
    conv1_bias,
    conv2_weight,
    conv2_bias,
    conv3_weight,
    conv3_bias,
    conv4_weight,
    conv4_bias,
):
    qry_index = lax.axis_index("qry")
    ref_index = lax.axis_index("ref")
    senders = lax.axis_size("qry")
    blocks = lax.axis_size("ref")
    frames, regions, channels = query_feats.shape
    rows = ref_feats.shape[0]
    block = frames // PHASES
    limits = (block * senders, block * blocks)
    count = rows // PIECE
    split = count >= 3 and senders == PHASES
    odd = qry_index % 2
    nearest = (qry_index + 2 * odd - 1) % senders
    entries = [qry_index, ref_index]
    for place in (qry_index, qry_index ^ 1, nearest):
        entries += [place ^ flip if split else flip for flip in range(PHASES)]
    position = jnp.stack([jnp.asarray(entry, jnp.int32) for entry in entries])
    query = jnp.transpose(query_feats, (1, 0, 2))
    own = jnp.transpose(ref_feats[:, 0], (1, 0, 2))
    chips = senders // 2
    across = [
        [(i, (i - 2 * step) % senders) for i in range(senders)] for step in range(1, chips)
    ]
    beside = [(i, i ^ 1) for i in range(senders)]

    if split:
        late = count // 2
        middle = [at for at in range(1, count - 1) if at != late]
        groups = [[0], [count - 1]] + [[at] for at in middle] + [[late]]
    else:
        groups = [list(range(count))]

    order = [at for group in groups for at in group]
    (piece,) = cut(own, order[:1])
    source, piece = lax.optimization_barrier((own, piece))
    whole = source.reshape(regions * rows, channels)
    cuts = [piece]
    if len(order) > 1:
        cuts += cut(source, order[1:])
    found = []
    for pairs in across:
        trips = []
        for piece in cuts:
            trips.append(shift(piece, "qry", pairs))
        found.append(trips)
    sibling = shift(whole, "qry", beside)
    weights = network_weights(
        conv1_weight,
        conv1_bias,
        conv2_weight,
        conv2_bias,
        conv3_weight,
        conv3_bias,
        conv4_weight,
        conv4_bias,
    )
    here, query = similarities(
        query, [whole, sibling], position, pair_table, fetch=True
    )
    sources, segments = [here], [(0, 0, rows, 0, 0), (0, rows, rows, 1, 0)]
    shard = 2
    last = []
    for pieces in found:
        pieces = list(pieces)
        for index, group in enumerate(groups):
            batch = []
            for at in group:
                piece = pieces.pop(0)
                batch += [piece, shift(piece, "qry", beside)]
            if split and index == len(groups) - 1:
                last = batch
                break
            here = similarities(query, batch, position, pair_table)[0]
            for order, at in enumerate(group):
                for half in range(2):
                    start = PIECE * (2 * order + half)
                    segments.append((len(sources), start, PIECE, shard + half, at * PIECE))
            sources.append(here)
        shard += 2
    if not split:
        tiles = [[None] * rows for _ in range(senders)]
        for source, row, size, place, cell in segments:
            for at in range(0, size, PIECE):
                tiles[place][cell + at] = sources[source][row + at : row + at + PIECE]
        tiles = [
            jnp.concatenate([part for part in parts if part is not None], axis=0)
            for parts in tiles
        ]
        sender = jnp.arange(senders, dtype=jnp.int32)
        step = (sender // 2 - qry_index // 2) % chips
        ordered = jnp.stack(tiles)[2 * step + ((sender % 2) ^ (qry_index % 2))]
        sims = ordered.reshape(senders // PHASES, PHASES, rows, frames).transpose(1, 2, 0, 3)
        sources = [sims.reshape(PHASES * block, frames)]
        segments = [(0, phase * block, block, phase, 0) for phase in range(PHASES)]

    def cells(low):
        parts = []
        for want in range(PHASES):
            for source, row, size, place, cell in segments:
                if place == want and cell <= low and low + HALO <= cell + size:
                    parts.append(sources[source][row + low - cell : row + low - cell + HALO])
        return jnp.concatenate(parts, axis=0)

    up = [(i, i + 1) for i in range(blocks - 1)]
    down = [(b, a) for a, b in up]
    right = shift(cells(0), "ref", down)
    left = shift(cells(block - HALO), "ref", up)
    for edge, cell in ((left, -HALO), (right, block)):
        segments += [(len(sources), HALO * k, HALO, k, cell) for k in range(PHASES)]
        sources.append(edge)
    base = assembled(position, sources, segments, block)
    if split:
        for half in range(2):
            segments.append((len(sources), PIECE * half, PIECE, 2 + half, late * PIECE))
        done, core, chip = similarities(query, last, position, pair_table, sources)
        sources.append(done)
    else:
        core, chip = edge_rows(position, sources)
        done = sources[-1]
    starts = [0]
    for source in sources[:-1]:
        starts.append(starts[-1] + source.shape[0])
    pairs = [(i, i + 1) for i in range(1, senders - 1, 2)]
    chip = shift(chip, "qry", pairs + [(b, a) for a, b in pairs])
    core = shift(core, "qry", beside)
    score_map, peaks = network(
        position,
        lengths,
        base,
        done,
        (core, chip),
        starts,
        segments,
        weights,
        block,
        limits,
    )
    place = jnp.stack([qry_index, qry_index ^ 1])
    peaks = jnp.stack([peaks, shift(peaks, "qry", beside)])

    def between_odd(array, flip_qry, flip_ref):
        pairs = [
            (q * blocks + r, (q ^ flip_qry) * blocks + (r ^ flip_ref))
            for q in range(1, senders, 2)
            for r in range(blocks)
        ]
        return shift(array, ("qry", "ref"), pairs)

    bit = 1
    while bit < blocks:
        peaks = jnp.maximum(peaks, between_odd(peaks, 0, bit))
        bit *= 2
    row_ids = place[:, None] * block + jnp.arange(block, dtype=jnp.int32)[None]
    total = jnp.sum(jnp.where((row_ids < query_len[0])[:, None], peaks, 0.0), axis=(0, 2))
    bit = senders // 2
    while bit > 1:
        total = total + between_odd(total, bit, 0)
        bit //= 2
    total = total / query_len[0].astype(F32)
    given = shift(total, "qry", [(q, q ^ 1) for q in range(1, senders, 2)])
    return (score_map, jnp.where(odd == 1, total, given))


def solution(mesh):
    placed = (
        P(("groups", "qry"), None, None),
        P(("groups", "ref"), "qry", None, None),
        P("groups", None),
        P("groups"),
        P("groups"),
    ) + (P(),) * 8

    return jax.shard_map(
        body,
        mesh=mesh,
        in_specs=placed,
        out_specs=(P(("groups", "qry"), "ref"), P("groups")),
        check_vma=False,
    )
```

```python
import functools
import math

import jax
import jax.numpy as jnp
from jax import lax
from jax.experimental import pallas as pl
from jax.experimental.pallas import tpu as pltpu
from jax.sharding import PartitionSpec as P


GRANT = 20 * 1024 * 1024
PIECE = 8
PHASES = 4
HALO = 2
EDGE = 8
GROUP = 3
WINDOW = PHASES * GROUP + 2
BF = jnp.bfloat16
F32 = jnp.float32


def in_hbm(array):
    return pltpu.with_memory_space_constraint(array, pltpu.HBM)


def shift(array, axis, pairs):
    return lax.ppermute(array, axis, pairs)


def cut_kernel(order, source_ref, *refs):
    outs, sems = refs[:-1], refs[-1]
    copies = []
    for index, (at, out) in enumerate(zip(order, outs)):
        piece = source_ref.at[:, pl.ds(at * PIECE, PIECE), :]
        copies.append(pltpu.make_async_copy(piece, out, sems.at[index]))
    for copy in copies:
        copy.start()
    for copy in copies:
        copy.wait()


def cut(source, order):
    regions, _, channels = source.shape
    shape = (regions, PIECE, channels)
    pieces = pl.pallas_call(
        functools.partial(cut_kernel, order),
        in_specs=[pl.BlockSpec(memory_space=pltpu.HBM)],
        out_specs=[pl.BlockSpec(memory_space=pltpu.VMEM) for _ in order],
        out_shape=[jax.ShapeDtypeStruct(shape, source.dtype) for _ in order],
        scratch_shapes=[pltpu.SemaphoreType.DMA((len(order),))],
        compiler_params=pltpu.CompilerParams(vmem_limit_bytes=GRANT),
        cost_estimate=pl.CostEstimate(
            flops=0, bytes_accessed=4 * source.size, transcendentals=0
        ),
        name="cut",
    )(in_hbm(source))
    return [piece.reshape(regions * PIECE, channels) for piece in pieces]


def write_edges(pos_ref, arrays, core_ref, chip_ref):
    total = jnp.concatenate(arrays, axis=0)
    frames = total.shape[1]
    eights = [total[at : at + 8] for at in range(0, total.shape[0], 8)]
    first = jnp.concatenate([eight[:, 0:EDGE] for eight in eights], axis=1)
    last = jnp.concatenate([eight[:, frames - EDGE : frames] for eight in eights], axis=1)
    even = pos_ref[0] % 2 == 0
    core_ref[...] = jnp.where(even, last, first)
    chip_ref[...] = jnp.where(even, first, last)


def edge_shapes(columns):
    return [jax.ShapeDtypeStruct((8, columns // 8 * EDGE), F32)] * 2


def edges_kernel(pos_ref, *refs):
    write_edges(pos_ref, [ref[...] for ref in refs[:-2]], *refs[-2:])


def edge_rows(position, sources):
    smem = pl.BlockSpec(memory_space=pltpu.SMEM)
    vmem = pl.BlockSpec(memory_space=pltpu.VMEM)
    return pl.pallas_call(
        edges_kernel,
        in_specs=[smem] + [vmem for _ in sources],
        out_specs=[vmem, vmem],
        out_shape=edge_shapes(sum(source.shape[0] for source in sources)),
        name="edges",
    )(position, *sources)


def sims_kernel(scale, spans, others, fetch, pos_ref, table_ref, query_ref, *refs):
    pieces, refs = refs[: len(spans)], refs[len(spans) :]
    done, refs = refs[:others], refs[others:]
    out_ref = refs[0]
    if fetch:
        rows_ref, sems = refs[-2], refs[-1]
    regions, frames, channels = query_ref.shape
    width = 3 if regions % 3 == 0 else 1
    if fetch:
        copies, arriving = [], []
        start = 0
        for index, (span, piece) in enumerate(zip(spans, pieces)):
            rows = pl.ds(start, span * regions)
            copies.append(pltpu.make_async_copy(piece, rows_ref.at[rows, :], sems.at[index]))
            start += span * regions
        for copy in copies:
            copy.start()
        for step in range(regions // width):
            block = pl.ds(step * width, width)
            arriving.append(
                pltpu.make_async_copy(
                    query_ref.at[block], refs[1].at[block], sems.at[len(spans) + step]
                )
            )
        for copy in arriving:
            copy.start()
        query_ref = refs[1]
        for copy in copies:
            copy.wait()

    total = None
    for step in range(regions // width):
        if fetch:
            arriving[step].wait()
        rows = (
            rows_ref[...]
            if fetch
            else jnp.concatenate([piece[...] for piece in pieces], axis=0)
        )
        products = lax.dot_general(
            rows,
            query_ref[step * width : (step + 1) * width].reshape(-1, channels),
            (((1,), (1,)), ((), ())),
            preferred_element_type=F32,
        )
        parts = []
        start = 0
        for span in spans:
            best = products[start : start + span]
            for other in range(1, regions):
                best = jnp.maximum(
                    best, products[start + other * span : start + (other + 1) * span]
                )
            part = best[:, 0:frames]
            for other in range(1, width):
                part = part + best[:, other * frames : (other + 1) * frames]
            parts.append(part)
            start += span * regions
        part = jnp.concatenate(parts, axis=0)
        total = part if total is None else total + part
    active = table_ref[pos_ref[0], pos_ref[1]] == 1
    total = total * jnp.where(active, scale, 0.0).astype(F32)
    out_ref[...] = total
    if done:
        write_edges(pos_ref, [ref[...] for ref in done] + [total], *refs[1:3])


def similarities(query, pieces, position, table, done=(), fetch=False):
    regions, frames, channels = query.shape
    spans = [piece.shape[0] // regions for piece in pieces]
    scale = 1.0 / (regions * math.sqrt(channels))
    rows = sum(spans)
    shapes = [jax.ShapeDtypeStruct((rows, frames), F32)]
    if done:
        shapes += edge_shapes(rows + sum(array.shape[0] for array in done))
    steps = 0
    if fetch:
        shapes.append(pltpu.VMEM(query.shape, query.dtype))
        steps = regions
    smem = pl.BlockSpec(memory_space=pltpu.SMEM)
    vmem = pl.BlockSpec(memory_space=pltpu.VMEM)
    return pl.pallas_call(
        functools.partial(sims_kernel, scale, spans, len(done), fetch),
        in_specs=[smem, smem, pl.BlockSpec(memory_space=pltpu.HBM) if fetch else vmem]
        + [pl.BlockSpec(memory_space=pltpu.HBM) if fetch else vmem for _ in pieces]
        + [vmem for _ in done],
        out_specs=[vmem for _ in shapes],
        out_shape=shapes,
        scratch_shapes=[
            pltpu.VMEM((rows * regions, channels), BF),
            pltpu.SemaphoreType.DMA((len(pieces) + steps,)),
        ]
        if fetch
        else [],
        compiler_params=pltpu.CompilerParams(vmem_limit_bytes=GRANT),
        cost_estimate=pl.CostEstimate(
            flops=2 * rows * regions * regions * frames * channels,
            bytes_accessed=2 * channels * regions * rows,
            transcendentals=0,
        ),
        name="similarities",
    )(position, table, *(map(in_hbm, (query, *pieces)) if fetch else (query, *pieces)), *done)


def convolve(sims_ref, weights, scratch, score_ref, pos_ref, block, limits, padding):
    w1_ref, b1_ref, w2_ref, b2_ref, w3_ref, b3_ref, w4_ref, b4_ref = weights
    y_ref, first_ref, lhs2_ref, second_ref, lhs3_ref = scratch
    map_rows, map_cols = limits
    jf, js, jt = padding
    rows1 = block + 2 * HALO
    groups = rows1 // GROUP
    row0 = pos_ref[0] * block
    col0 = pos_ref[1] * block
    lanes = sims_ref.shape[2]

    sources = [(PHASES - 1, 0)] + [(phase, 1) for phase in range(PHASES)] + [(0, 2)]
    bases = [sims_ref[phase, at : at + jf, :] for phase, at in sources]
    terms = len(sources) * WINDOW
    zero = jnp.zeros((jf, 128 - terms), F32)
    reach = PHASES * HALO + 1
    lane = lax.broadcasted_iota(jnp.int32, (jf, 128), 1)
    for group in range(groups):
        low = PHASES * GROUP * group - reach
        parts = []
        for base in bases:
            if low < 0:
                parts.append(base[:, lanes + low : lanes])
                parts.append(base[:, 0 : low + WINDOW])
            else:
                parts.append(base[:, low : low + WINDOW])
        window = jnp.concatenate(parts + [zero], axis=1)
        high = window.astype(BF).astype(F32)
        rest = pltpu.roll(window - high, terms, 1)
        again = pltpu.roll(high, 2 * terms - 128, 1)
        row = slice(group * jf, (group + 1) * jf)
        y_ref[row, 0:128] = jnp.where(lane < terms, high, rest).astype(BF)
        y_ref[row, 128:256] = jnp.where(lane < 2 * terms - 128, rest, again).astype(BF)

    cell = lax.broadcasted_iota(jnp.int32, (jf, 128), 0)

    def inside(halo, count):
        at = cell[0:count] + (col0 - halo)
        return jnp.where((at >= 0) & (at < map_cols), 1.0, 0.0).astype(F32)

    def row_flag(at):
        return jnp.where((at >= 0) & (at < map_rows), 1.0, 0.0).astype(F32)

    keep_cols = inside(HALO, jf)
    for member in range(GROUP):
        result = jnp.dot(
            y_ref[0 : groups * jf, :],
            w1_ref[:, member * 512 : (member + 1) * 512],
            preferred_element_type=F32,
        )
        pooled = jnp.maximum(
            jnp.maximum(result[:, 0:128], result[:, 128:256]),
            jnp.maximum(result[:, 256:384], result[:, 384:512]),
        )
        pooled = jnp.maximum(pooled + b1_ref[...], 0.0)
        for group in range(groups):
            at = group * GROUP + member
            keep = keep_cols * row_flag(row0 + at - HALO)
            first_ref[at, 0:jf, :] = (
                (pooled[group * jf : (group + 1) * jf] * keep).astype(BF).astype(F32)
            )

    upper = lane < 64
    left = (lane // 32) % 2 == 0
    rows2 = block + 2
    for at in range(rows2):
        centre = first_ref[at + 1, 0:jf, :]
        across = jnp.where(upper, first_ref[at + 2, 0:jf, :], first_ref[at, 0:jf, :])
        row = slice(at * js, (at + 1) * js)
        for index, value in enumerate((centre, across)):
            here = pltpu.roll(value, jf - 1, 0)
            beside = jnp.where(left, pltpu.roll(value, jf - 2, 0), value)
            lhs2_ref[row, index * 256 : index * 256 + 128] = here[0:js].astype(BF)
            lhs2_ref[row, index * 256 + 128 : index * 256 + 256] = beside[0:js].astype(BF)
    result = jnp.dot(lhs2_ref[0 : rows2 * js, :], w2_ref[...], preferred_element_type=F32)
    pooled = jnp.maximum(result[:, 0:128], result[:, 128:256])
    pooled = jnp.maximum(pooled, pltpu.roll(pooled, 64, 1))
    pooled = jnp.maximum(pooled + b2_ref[...], 0.0)
    keep_cols = inside(1, js)
    for at in range(rows2):
        keep = keep_cols * row_flag(row0 + at - 1)
        second_ref[at, 0:js, :] = (pooled[at * js : (at + 1) * js] * keep).astype(BF).astype(F32)
        if js < jt + 8:
            second_ref[at, js : jt + 8, :] = jnp.zeros((jt + 8 - js, 128), F32)

    upper = upper[0:jt]
    for at in range(block // 2):
        row = slice(at * jt, (at + 1) * jt)
        rows = [second_ref.at[2 * at + down] for down in range(4)]
        for down in range(4):
            pair = jnp.where(upper, rows[down][0:jt, :], rows[down][1 : 1 + jt, :])
            lhs3_ref[row, down * 128 : (down + 1) * 128] = pair.astype(BF)
        for half in range(2):
            pair = jnp.where(
                upper, rows[2 * half][2 : 2 + jt, :], rows[2 * half + 1][2 : 2 + jt, :]
            )
            lhs3_ref[row, (4 + half) * 128 : (5 + half) * 128] = pair.astype(BF)
    third = jnp.dot(lhs3_ref[...], w3_ref[...], preferred_element_type=F32)
    third = jnp.maximum(third + b3_ref[...], 0.0).astype(BF)
    flat = lax.dot_general(
        w4_ref[...], third, (((1,), (1,)), ((), ())), preferred_element_type=F32
    )
    flat = flat[0:8] + b4_ref[0]
    for at in range(block // 2):
        score_ref[2 * at : 2 * at + 2, :] = flat[0:2, at * jt : at * jt + block]


def pad_cells(cells):
    js = -(-(cells + 2) // 8) * 8
    return (max(-(-(cells + 4) // 8) * 8, js), js, -(-cells // 16) * 16)


def convolve_scratch(block, padding):
    jf, js, jt = padding
    rows1 = block + 2 * HALO
    return [
        pltpu.VMEM((rows1 // GROUP * jf, 256), BF),
        pltpu.VMEM((rows1, jf, 128), F32),
        pltpu.VMEM(((block + 2) * js, 512), BF),
        pltpu.VMEM((block + 2, max(js, jt + 8), 128), F32),
        pltpu.VMEM((block // 2 * jt, 768), BF),
    ]


def place(pos_ref, sims_ref, sources, segments):
    for source, row, size, shard, cell in segments:
        if source < len(sources):
            rows = slice(3 + cell, 3 + cell + size)
            sims_ref[pos_ref[2 + shard], rows, 0 : sources[source].shape[1]] = sources[source][
                row : row + size, :
            ]


def place_edges(pos_ref, sims_ref, starts, segments, table, edge, side):
    for source, row, size, shard, cell in segments:
        for at in range(0, size, 8):
            start = starts[source] + row + at
            count = min(8, size - at)
            lane = start // 8 * EDGE
            sims_ref[pos_ref[table + shard], 3 + cell + at : 3 + cell + at + count, side] = edge[
                start % 8 : start % 8 + count, lane : lane + EDGE
            ]


def assemble_kernel(segments, pos_ref, *refs):
    sources, sims_ref = refs[:-1], refs[-1]
    sims_ref[...] = jnp.zeros_like(sims_ref)
    place(pos_ref, sims_ref, sources, segments)


def assembled(position, sources, segments, block):
    smem = pl.BlockSpec(memory_space=pltpu.SMEM)
    vmem = pl.BlockSpec(memory_space=pltpu.VMEM)
    frames = sources[0].shape[1]
    return pl.pallas_call(
        functools.partial(assemble_kernel, segments),
        in_specs=[smem] + [vmem for _ in sources],
        out_specs=vmem,
        out_shape=jax.ShapeDtypeStruct((PHASES, block + 24, 2 * frames), F32),
        compiler_params=pltpu.CompilerParams(vmem_limit_bytes=GRANT),
        cost_estimate=pl.CostEstimate(flops=0, bytes_accessed=500_000, transcendentals=0),
        name="assemble",
    )(position, *sources)


def network_kernel(limits, padding, starts, segments, pos_ref, len_ref, base_ref, *refs):
    (late_ref, core_ref, chip_ref), refs = refs[:3], refs[3:]
    weights, (score_ref, peak_ref, sims_ref), scratch = refs[:8], refs[8:11], refs[11:]
    block = score_ref.shape[0]
    last = len(starts) - 1
    place(
        pos_ref, sims_ref, [late_ref], [(0, *rest) for source, *rest in segments if source == last]
    )
    lanes = sims_ref.shape[2]
    above, below = slice(lanes - EDGE, lanes), slice(lanes // 2, lanes // 2 + EDGE)

    ends = (pos_ref[0] == 0) | (pos_ref[0] == limits[0] // block - 1)
    core, chip = core_ref[...], jnp.where(ends, 0.0, chip_ref[...])

    def edges(core_side, chip_side):
        place_edges(pos_ref, sims_ref, starts, segments, 6, core, core_side)
        place_edges(pos_ref, sims_ref, starts, segments, 10, chip, chip_side)

    pl.when(pos_ref[0] % 2 == 0)(lambda: edges(below, above))
    pl.when(pos_ref[0] % 2 == 1)(lambda: edges(above, below))
    convolve(sims_ref, weights, scratch, score_ref, pos_ref, block, limits, padding)

    score = score_ref[...]
    videos = len_ref.shape[0]
    column = pos_ref[1] * block + lax.broadcasted_iota(jnp.int32, (block, block), 1)
    slot = lax.broadcasted_iota(jnp.int32, (block, 128), 1)
    start = jnp.int32(0)
    peaks = jnp.zeros((block, 128), F32)
    for video in range(videos):
        end = start + len_ref[video]
        member = (column >= start) & (column < end)
        best = jnp.max(jnp.where(member, score, -jnp.inf), axis=1, keepdims=True)
        peaks = jnp.where(slot == video, best, peaks)
        start = end
    peak_ref[...] = jnp.transpose(peaks)[0:videos]


def network(position, lengths, base, late, edges, starts, segments, weights, block, limits):
    smem = pl.BlockSpec(memory_space=pltpu.SMEM)
    vmem = pl.BlockSpec(memory_space=pltpu.VMEM)
    padding = pad_cells(block)
    arrays = [base, late, *edges]
    score, peaks, _ = pl.pallas_call(
        functools.partial(network_kernel, limits, padding, starts, segments),
        in_specs=[smem, smem] + [vmem] * len(arrays) + [vmem] * 7 + [smem],
        out_specs=[vmem, vmem, vmem],
        out_shape=[
            jax.ShapeDtypeStruct((block, block), F32),
            jax.ShapeDtypeStruct((lengths.shape[0], block), F32),
            jax.ShapeDtypeStruct(base.shape, F32),
        ],
        scratch_shapes=convolve_scratch(block, padding),
        input_output_aliases={2: 2},
        cost_estimate=pl.CostEstimate(
            flops=6_000_000_000, bytes_accessed=4_000_000, transcendentals=0
        ),
        compiler_params=pltpu.CompilerParams(vmem_limit_bytes=GRANT),
        name="network",
    )(position, lengths, *arrays, *weights)
    return score, peaks


def weights_kernel(w1_ref, b1_ref, w2_ref, b2_ref, w3_ref, b3_ref, w4_ref, *outs):
    f1_ref, o1_ref, f2_ref, o2_ref, f3_ref, o3_ref, f4_ref = outs
    c1, c2, c3 = w1_ref.shape[2], w2_ref.shape[3], w3_ref.shape[3]
    rows = lax.broadcasted_iota(jnp.int32, (256, 16 * c1), 0)
    lane = lax.broadcasted_iota(jnp.int32, (256, 16 * c1), 1) // c1
    terms = 6 * WINDOW
    third = rows >= 2 * terms
    valid = rows < 3 * terms
    rows = rows - jnp.where(third, 2 * terms, jnp.where(rows >= terms, terms, 0))
    along = jnp.zeros_like(rows)
    for offset in range(1, 6):
        along = along + jnp.where(rows >= offset * WINDOW, 1, 0)
    down = rows - along * WINDOW - 2 * ((lane // 2) % 2) - lane // 8
    along = along - 2 * (lane % 2) - (lane // 4) % 2
    taps = []
    for di in range(3):
        for dj in range(3):
            tap = jnp.concatenate([w1_ref[di, dj : dj + 1, :]] * (128 // c1), axis=1)
            taps.append(jnp.concatenate([tap] * (16 * c1 // 128), axis=1))
    for member in range(GROUP):
        dense = jnp.zeros(rows.shape, F32)
        for di in range(3):
            for dj in range(3):
                here = (down == di + PHASES * member) & (along == dj) & valid
                dense = jnp.where(here, taps[3 * di + dj], dense)
        high = dense.astype(BF).astype(F32)
        at = slice(member * 16 * c1, (member + 1) * 16 * c1)
        f1_ref[:, at] = jnp.where(third, dense - high, high).astype(BF)
    o1_ref[...] = jnp.concatenate([b1_ref[...]] * (128 // c1), axis=1)
    o2_ref[...] = jnp.concatenate([b2_ref[...]] * (128 // c2), axis=1)
    f2_ref[...] = jnp.zeros_like(f2_ref)
    reach = ((0, 1), (2, -1))
    for index in range(16):
        row_kind, col_kind, sr, sc = (index >> 3) & 1, (index >> 2) & 1, (index >> 1) & 1, index & 1
        for phase in range(4):
            di = reach[row_kind][sr] - phase // 2 + 1
            dj = reach[col_kind][sc] - phase % 2 + 1
            if 0 <= di <= 2 and 0 <= dj <= 2:
                f2_ref[index * c1 : (index + 1) * c1, phase * c2 : (phase + 1) * c2] = w2_ref[
                    di, dj
                ]
    f3_ref[...] = jnp.zeros_like(f3_ref)
    order = [(row, col) for row in range(4) for col in range(2)] + [(row, 2) for row in range(4)]
    for index, (row, dj) in enumerate(order):
        for output in range(2):
            if 0 <= row - output <= 2:
                f3_ref[index * c2 : (index + 1) * c2, output * c3 : (output + 1) * c3] = w3_ref[
                    row - output, dj
                ]
    o3_ref[...] = jnp.concatenate([b3_ref[...]] * 2, axis=1)
    fourth = jnp.concatenate([w4_ref[...].astype(F32)] * 2, axis=1)
    half = lax.broadcasted_iota(jnp.int32, f4_ref.shape, 1) // c3
    output = lax.broadcasted_iota(jnp.int32, f4_ref.shape, 0)
    f4_ref[...] = jnp.where(half == output, fourth, 0.0).astype(BF)


def network_weights(w1, b1, w2, b2, w3, b3, w4, b4):
    c1, c2, c3 = w1.shape[2], w2.shape[2], w3.shape[2]
    shapes = [
        ((256, GROUP * 16 * c1), BF),
        ((1, 128), F32),
        ((16 * c1, 4 * c2), BF),
        ((1, 128), F32),
        ((12 * c2, 2 * c3), BF),
        ((1, 2 * c3), F32),
        ((16, 2 * c3), BF),
    ]
    f1, o1, f2, o2, f3, o3, f4 = pl.pallas_call(
        weights_kernel,
        out_shape=[jax.ShapeDtypeStruct(shape, dtype) for shape, dtype in shapes],
        cost_estimate=pl.CostEstimate(flops=100_000_000, bytes_accessed=4_000_000, transcendentals=0),
        compiler_params=pltpu.CompilerParams(vmem_limit_bytes=GRANT),
        name="weights",
    )(
        w1,
        b1[None],
        jnp.transpose(w2, (0, 1, 3, 2)),
        b2[None],
        jnp.transpose(w3, (0, 1, 3, 2)),
        b3[None],
        w4[None],
    )
    return (f1, o1, f2, o2, f3, o3, f4, b4)


def body(
    query_feats,
    ref_feats,
    pair_table,
    lengths,
    query_len,
    conv1_weight,
    conv1_bias,
    conv2_weight,
    conv2_bias,
    conv3_weight,
    conv3_bias,
    conv4_weight,
    conv4_bias,
):
    qry_index = lax.axis_index("qry")
    ref_index = lax.axis_index("ref")
    senders = lax.axis_size("qry")
    blocks = lax.axis_size("ref")
    frames, regions, channels = query_feats.shape
    rows = ref_feats.shape[0]
    block = frames // PHASES
    limits = (block * senders, block * blocks)
    count = rows // PIECE
    split = count >= 3 and senders == PHASES
    odd = qry_index % 2
    nearest = (qry_index + 2 * odd - 1) % senders
    entries = [qry_index, ref_index]
    for place in (qry_index, qry_index ^ 1, nearest):
        entries += [place ^ flip if split else flip for flip in range(PHASES)]
    position = jnp.stack([jnp.asarray(entry, jnp.int32) for entry in entries])
    query = jnp.transpose(query_feats, (1, 0, 2))
    own = jnp.transpose(ref_feats[:, 0], (1, 0, 2))
    chips = senders // 2
    across = [
        [(i, (i - 2 * step) % senders) for i in range(senders)] for step in range(1, chips)
    ]
    beside = [(i, i ^ 1) for i in range(senders)]

    if split:
        late = count // 2
        middle = [at for at in range(1, count - 1) if at != late]
        groups = [[0], [count - 1]] + [[at] for at in middle] + [[late]]
    else:
        groups = [list(range(count))]

    order = [at for group in groups for at in group]
    (piece,) = cut(own, order[:1])
    source, piece = lax.optimization_barrier((own, piece))
    whole = source.reshape(regions * rows, channels)
    cuts = [piece]
    if len(order) > 1:
        cuts += cut(source, order[1:])
    found = []
    for pairs in across:
        trips = []
        for piece in cuts:
            trips.append(shift(piece, "qry", pairs))
        found.append(trips)
    sibling = shift(whole, "qry", beside)
    weights = network_weights(
        conv1_weight,
        conv1_bias,
        conv2_weight,
        conv2_bias,
        conv3_weight,
        conv3_bias,
        conv4_weight,
        conv4_bias,
    )
    here, query = similarities(
        query, [whole, sibling], position, pair_table, fetch=True
    )
    sources, segments = [here], [(0, 0, rows, 0, 0), (0, rows, rows, 1, 0)]
    shard = 2
    last = []
    for pieces in found:
        pieces = list(pieces)
        for index, group in enumerate(groups):
            batch = []
            for at in group:
                piece = pieces.pop(0)
                batch += [piece, shift(piece, "qry", beside)]
            if split and index == len(groups) - 1:
                last = batch
                break
            here = similarities(query, batch, position, pair_table)[0]
            for order, at in enumerate(group):
                for half in range(2):
                    start = PIECE * (2 * order + half)
                    segments.append((len(sources), start, PIECE, shard + half, at * PIECE))
            sources.append(here)
        shard += 2
    if not split:
        tiles = [[None] * rows for _ in range(senders)]
        for source, row, size, place, cell in segments:
            for at in range(0, size, PIECE):
                tiles[place][cell + at] = sources[source][row + at : row + at + PIECE]
        tiles = [
            jnp.concatenate([part for part in parts if part is not None], axis=0)
            for parts in tiles
        ]
        sender = jnp.arange(senders, dtype=jnp.int32)
        step = (sender // 2 - qry_index // 2) % chips
        ordered = jnp.stack(tiles)[2 * step + ((sender % 2) ^ (qry_index % 2))]
        sims = ordered.reshape(senders // PHASES, PHASES, rows, frames).transpose(1, 2, 0, 3)
        sources = [sims.reshape(PHASES * block, frames)]
        segments = [(0, phase * block, block, phase, 0) for phase in range(PHASES)]

    def cells(low):
        parts = []
        for want in range(PHASES):
            for source, row, size, place, cell in segments:
                if place == want and cell <= low and low + HALO <= cell + size:
                    parts.append(sources[source][row + low - cell : row + low - cell + HALO])
        return jnp.concatenate(parts, axis=0)

    up = [(i, i + 1) for i in range(blocks - 1)]
    down = [(b, a) for a, b in up]
    right = shift(cells(0), "ref", down)
    left = shift(cells(block - HALO), "ref", up)
    for edge, cell in ((left, -HALO), (right, block)):
        segments += [(len(sources), HALO * k, HALO, k, cell) for k in range(PHASES)]
        sources.append(edge)
    base = assembled(position, sources, segments, block)
    if split:
        for half in range(2):
            segments.append((len(sources), PIECE * half, PIECE, 2 + half, late * PIECE))
        done, core, chip = similarities(query, last, position, pair_table, sources)
        sources.append(done)
    else:
        core, chip = edge_rows(position, sources)
        done = sources[-1]
    starts = [0]
    for source in sources[:-1]:
        starts.append(starts[-1] + source.shape[0])
    pairs = [(i, (i + 1) % senders) for i in range(1, senders, 2)]
    chip = shift(chip, "qry", pairs + [(b, a) for a, b in pairs])
    core = shift(core, "qry", beside)
    score_map, peaks = network(
        position,
        lengths,
        base,
        done,
        (core, chip),
        starts,
        segments,
        weights,
        block,
        limits,
    )
    bit = 1
    while bit < blocks:
        peaks = jnp.maximum(peaks, shift(peaks, "ref", [(i, i ^ bit) for i in range(blocks)]))
        bit *= 2
    row_ids = qry_index * block + jnp.arange(block, dtype=jnp.int32)
    total = jnp.sum(jnp.where((row_ids < query_len[0])[None], peaks, 0.0), axis=1)
    bit = senders // 2
    while bit >= 1:
        total = total + shift(total, "qry", [(i, i ^ bit) for i in range(senders)])
        bit //= 2
    return (score_map, total / query_len[0].astype(F32))


def solution(mesh):
    placed = (
        P(("groups", "qry"), None, None),
        P(("groups", "ref"), "qry", None, None),
        P("groups", None),
        P("groups"),
        P("groups"),
    ) + (P(),) * 8

    return jax.shard_map(
        body,
        mesh=mesh,
        in_specs=placed,
        out_specs=(P(("groups", "qry"), "ref"), P("groups")),
        check_vma=False,
    )
```

```python
import functools
import math

import jax
import jax.numpy as jnp
from jax import lax
from jax.experimental import pallas as pl
from jax.experimental.pallas import tpu as pltpu
from jax.sharding import PartitionSpec as P


GRANT = 20 * 1024 * 1024
PIECE = 8
PHASES = 4
HALO = 2
EDGE = 8
GROUP = 3
WINDOW = PHASES * GROUP + 2
BF = jnp.bfloat16
F32 = jnp.float32


def in_hbm(array):
    return pltpu.with_memory_space_constraint(array, pltpu.HBM)


def shift(array, axis, pairs):
    return lax.ppermute(array, axis, pairs)


def cut_kernel(order, source_ref, *refs):
    outs, sems = refs[:-1], refs[-1]
    copies = []
    for index, (at, out) in enumerate(zip(order, outs)):
        piece = source_ref.at[:, pl.ds(at * PIECE, PIECE), :]
        copies.append(pltpu.make_async_copy(piece, out, sems.at[index]))
    for copy in copies:
        copy.start()
    for copy in copies:
        copy.wait()


def cut(source, order):
    regions, _, channels = source.shape
    shape = (regions, PIECE, channels)
    pieces = pl.pallas_call(
        functools.partial(cut_kernel, order),
        in_specs=[pl.BlockSpec(memory_space=pltpu.HBM)],
        out_specs=[pl.BlockSpec(memory_space=pltpu.VMEM) for _ in order],
        out_shape=[jax.ShapeDtypeStruct(shape, source.dtype) for _ in order],
        scratch_shapes=[pltpu.SemaphoreType.DMA((len(order),))],
        compiler_params=pltpu.CompilerParams(vmem_limit_bytes=GRANT),
        cost_estimate=pl.CostEstimate(
            flops=0, bytes_accessed=4 * source.size, transcendentals=0
        ),
        name="cut",
    )(in_hbm(source))
    return [piece.reshape(regions * PIECE, channels) for piece in pieces]


def write_edges(pos_ref, arrays, core_ref, chip_ref):
    total = jnp.concatenate(arrays, axis=0)
    frames = total.shape[1]
    eights = [total[at : at + 8] for at in range(0, total.shape[0], 8)]
    first = jnp.concatenate([eight[:, 0:EDGE] for eight in eights], axis=1)
    last = jnp.concatenate([eight[:, frames - EDGE : frames] for eight in eights], axis=1)
    even = pos_ref[0] % 2 == 0
    core_ref[...] = jnp.where(even, last, first)
    chip_ref[...] = jnp.where(even, first, last)


def edge_shapes(columns):
    return [jax.ShapeDtypeStruct((8, columns // 8 * EDGE), F32)] * 2


def edges_kernel(pos_ref, *refs):
    write_edges(pos_ref, [ref[...] for ref in refs[:-2]], *refs[-2:])


def edge_rows(position, sources):
    smem = pl.BlockSpec(memory_space=pltpu.SMEM)
    vmem = pl.BlockSpec(memory_space=pltpu.VMEM)
    return pl.pallas_call(
        edges_kernel,
        in_specs=[smem] + [vmem for _ in sources],
        out_specs=[vmem, vmem],
        out_shape=edge_shapes(sum(source.shape[0] for source in sources)),
        name="edges",
    )(position, *sources)


def sims_kernel(scale, spans, others, fetch, pos_ref, table_ref, query_ref, *refs):
    pieces, refs = refs[: len(spans)], refs[len(spans) :]
    done, refs = refs[:others], refs[others:]
    out_ref = refs[0]
    if fetch:
        rows_ref, sems = refs[-2], refs[-1]
    regions, frames, channels = query_ref.shape
    width = 3 if regions % 3 == 0 else 1
    if fetch:
        copies, arriving = [], []
        start = 0
        for index, (span, piece) in enumerate(zip(spans, pieces)):
            rows = pl.ds(start, span * regions)
            copies.append(pltpu.make_async_copy(piece, rows_ref.at[rows, :], sems.at[index]))
            start += span * regions
        for copy in copies:
            copy.start()
        for step in range(regions // width):
            block = pl.ds(step * width, width)
            arriving.append(
                pltpu.make_async_copy(
                    query_ref.at[block], refs[1].at[block], sems.at[len(spans) + step]
                )
            )
        for copy in arriving:
            copy.start()
        query_ref = refs[1]
        for copy in copies:
            copy.wait()

    total = None
    for step in range(regions // width):
        if fetch:
            arriving[step].wait()
        rows = (
            rows_ref[...]
            if fetch
            else jnp.concatenate([piece[...] for piece in pieces], axis=0)
        )
        products = lax.dot_general(
            rows,
            query_ref[step * width : (step + 1) * width].reshape(-1, channels),
            (((1,), (1,)), ((), ())),
            preferred_element_type=F32,
        )
        parts = []
        start = 0
        for span in spans:
            best = products[start : start + span]
            for other in range(1, regions):
                best = jnp.maximum(
                    best, products[start + other * span : start + (other + 1) * span]
                )
            part = best[:, 0:frames]
            for other in range(1, width):
                part = part + best[:, other * frames : (other + 1) * frames]
            parts.append(part)
            start += span * regions
        part = jnp.concatenate(parts, axis=0)
        total = part if total is None else total + part
    active = table_ref[pos_ref[0], pos_ref[1]] == 1
    total = total * jnp.where(active, scale, 0.0).astype(F32)
    out_ref[...] = total
    if done:
        write_edges(pos_ref, [ref[...] for ref in done] + [total], *refs[1:3])


def similarities(query, pieces, position, table, done=(), fetch=False):
    regions, frames, channels = query.shape
    spans = [piece.shape[0] // regions for piece in pieces]
    scale = 1.0 / (regions * math.sqrt(channels))
    rows = sum(spans)
    shapes = [jax.ShapeDtypeStruct((rows, frames), F32)]
    if done:
        shapes += edge_shapes(rows + sum(array.shape[0] for array in done))
    steps = 0
    if fetch:
        shapes.append(pltpu.VMEM(query.shape, query.dtype))
        steps = regions
    smem = pl.BlockSpec(memory_space=pltpu.SMEM)
    vmem = pl.BlockSpec(memory_space=pltpu.VMEM)
    return pl.pallas_call(
        functools.partial(sims_kernel, scale, spans, len(done), fetch),
        in_specs=[smem, smem, pl.BlockSpec(memory_space=pltpu.HBM) if fetch else vmem]
        + [pl.BlockSpec(memory_space=pltpu.HBM) if fetch else vmem for _ in pieces]
        + [vmem for _ in done],
        out_specs=[vmem for _ in shapes],
        out_shape=shapes,
        scratch_shapes=[
            pltpu.VMEM((rows * regions, channels), BF),
            pltpu.SemaphoreType.DMA((len(pieces) + steps,)),
        ]
        if fetch
        else [],
        compiler_params=pltpu.CompilerParams(vmem_limit_bytes=GRANT),
        cost_estimate=pl.CostEstimate(
            flops=2 * rows * regions * regions * frames * channels,
            bytes_accessed=2 * channels * regions * rows,
            transcendentals=0,
        ),
        name="similarities",
    )(position, table, *(map(in_hbm, (query, *pieces)) if fetch else (query, *pieces)), *done)


def convolve(sims_ref, weights, scratch, score_ref, pos_ref, block, limits, padding):
    w1_ref, b1_ref, w2_ref, b2_ref, w3_ref, b3_ref, w4_ref, b4_ref = weights
    y_ref, first_ref, lhs2_ref, second_ref, lhs3_ref = scratch
    map_rows, map_cols = limits
    jf, js, jt = padding
    rows1 = block + 2 * HALO
    groups = rows1 // GROUP
    row0 = pos_ref[0] * block
    col0 = pos_ref[1] * block
    lanes = sims_ref.shape[2]

    sources = [(PHASES - 1, 0)] + [(phase, 1) for phase in range(PHASES)] + [(0, 2)]
    bases = [sims_ref[phase, at : at + jf, :] for phase, at in sources]
    terms = len(sources) * WINDOW
    zero = jnp.zeros((jf, 128 - terms), F32)
    reach = PHASES * HALO + 1
    lane = lax.broadcasted_iota(jnp.int32, (jf, 128), 1)
    for group in range(groups):
        low = PHASES * GROUP * group - reach
        parts = []
        for base in bases:
            if low < 0:
                parts.append(base[:, lanes + low : lanes])
                parts.append(base[:, 0 : low + WINDOW])
            else:
                parts.append(base[:, low : low + WINDOW])
        window = jnp.concatenate(parts + [zero], axis=1)
        high = window.astype(BF).astype(F32)
        rest = pltpu.roll(window - high, terms, 1)
        again = pltpu.roll(high, 2 * terms - 128, 1)
        row = slice(group * jf, (group + 1) * jf)
        y_ref[row, 0:128] = jnp.where(lane < terms, high, rest).astype(BF)
        y_ref[row, 128:256] = jnp.where(lane < 2 * terms - 128, rest, again).astype(BF)

    cell = lax.broadcasted_iota(jnp.int32, (jf, 128), 0)

    def inside(halo, count):
        at = cell[0:count] + (col0 - halo)
        return jnp.where((at >= 0) & (at < map_cols), 1.0, 0.0).astype(F32)

    def row_flag(at):
        return jnp.where((at >= 0) & (at < map_rows), 1.0, 0.0).astype(F32)

    keep_cols = inside(HALO, jf)
    for member in range(GROUP):
        result = jnp.dot(
            y_ref[0 : groups * jf, :],
            w1_ref[:, member * 512 : (member + 1) * 512],
            preferred_element_type=F32,
        )
        pooled = jnp.maximum(
            jnp.maximum(result[:, 0:128], result[:, 128:256]),
            jnp.maximum(result[:, 256:384], result[:, 384:512]),
        )
        pooled = jnp.maximum(pooled + b1_ref[...], 0.0)
        for group in range(groups):
            at = group * GROUP + member
            keep = keep_cols * row_flag(row0 + at - HALO)
            first_ref[at, 0:jf, :] = (
                (pooled[group * jf : (group + 1) * jf] * keep).astype(BF).astype(F32)
            )

    upper = lane < 64
    left = (lane // 32) % 2 == 0
    rows2 = block + 2
    for at in range(rows2):
        centre = first_ref[at + 1, 0:jf, :]
        across = jnp.where(upper, first_ref[at + 2, 0:jf, :], first_ref[at, 0:jf, :])
        row = slice(at * js, (at + 1) * js)
        for index, value in enumerate((centre, across)):
            here = pltpu.roll(value, jf - 1, 0)
            beside = jnp.where(left, pltpu.roll(value, jf - 2, 0), value)
            lhs2_ref[row, index * 256 : index * 256 + 128] = here[0:js].astype(BF)
            lhs2_ref[row, index * 256 + 128 : index * 256 + 256] = beside[0:js].astype(BF)
    result = jnp.dot(lhs2_ref[0 : rows2 * js, :], w2_ref[...], preferred_element_type=F32)
    pooled = jnp.maximum(result[:, 0:128], result[:, 128:256])
    pooled = jnp.maximum(pooled, pltpu.roll(pooled, 64, 1))
    pooled = jnp.maximum(pooled + b2_ref[...], 0.0)
    keep_cols = inside(1, js)
    for at in range(rows2):
        keep = keep_cols * row_flag(row0 + at - 1)
        second_ref[at, 0:js, :] = (pooled[at * js : (at + 1) * js] * keep).astype(BF).astype(F32)
        if js < jt + 8:
            second_ref[at, js : jt + 8, :] = jnp.zeros((jt + 8 - js, 128), F32)

    upper = upper[0:jt]
    for at in range(block // 2):
        row = slice(at * jt, (at + 1) * jt)
        rows = [second_ref.at[2 * at + down] for down in range(4)]
        for down in range(4):
            pair = jnp.where(upper, rows[down][0:jt, :], rows[down][1 : 1 + jt, :])
            lhs3_ref[row, down * 128 : (down + 1) * 128] = pair.astype(BF)
        for half in range(2):
            pair = jnp.where(
                upper, rows[2 * half][2 : 2 + jt, :], rows[2 * half + 1][2 : 2 + jt, :]
            )
            lhs3_ref[row, (4 + half) * 128 : (5 + half) * 128] = pair.astype(BF)
    third = jnp.dot(lhs3_ref[...], w3_ref[...], preferred_element_type=F32)
    third = jnp.maximum(third + b3_ref[...], 0.0).astype(BF)
    flat = lax.dot_general(
        w4_ref[...], third, (((1,), (1,)), ((), ())), preferred_element_type=F32
    )
    flat = flat[0:8] + b4_ref[0]
    for at in range(block // 2):
        score_ref[2 * at : 2 * at + 2, :] = flat[0:2, at * jt : at * jt + block]


def pad_cells(cells):
    js = -(-(cells + 2) // 8) * 8
    return (max(-(-(cells + 4) // 8) * 8, js), js, -(-cells // 16) * 16)


def convolve_scratch(block, padding):
    jf, js, jt = padding
    rows1 = block + 2 * HALO
    return [
        pltpu.VMEM((rows1 // GROUP * jf, 256), BF),
        pltpu.VMEM((rows1, jf, 128), F32),
        pltpu.VMEM(((block + 2) * js, 512), BF),
        pltpu.VMEM((block + 2, max(js, jt + 8), 128), F32),
        pltpu.VMEM((block // 2 * jt, 768), BF),
    ]


def place(pos_ref, sims_ref, sources, segments):
    for source, row, size, shard, cell in segments:
        if source < len(sources):
            rows = slice(3 + cell, 3 + cell + size)
            sims_ref[pos_ref[2 + shard], rows, 0 : sources[source].shape[1]] = sources[source][
                row : row + size, :
            ]


def place_edges(pos_ref, sims_ref, starts, segments, table, edge, side):
    for source, row, size, shard, cell in segments:
        for at in range(0, size, 8):
            start = starts[source] + row + at
            count = min(8, size - at)
            lane = start // 8 * EDGE
            sims_ref[pos_ref[table + shard], 3 + cell + at : 3 + cell + at + count, side] = edge[
                start % 8 : start % 8 + count, lane : lane + EDGE
            ]


def assemble_kernel(segments, pos_ref, *refs):
    sources, sims_ref = refs[:-1], refs[-1]
    sims_ref[...] = jnp.zeros_like(sims_ref)
    place(pos_ref, sims_ref, sources, segments)


def assembled(position, sources, segments, block):
    smem = pl.BlockSpec(memory_space=pltpu.SMEM)
    vmem = pl.BlockSpec(memory_space=pltpu.VMEM)
    frames = sources[0].shape[1]
    return pl.pallas_call(
        functools.partial(assemble_kernel, segments),
        in_specs=[smem] + [vmem for _ in sources],
        out_specs=vmem,
        out_shape=jax.ShapeDtypeStruct((PHASES, block + 24, 2 * frames), F32),
        compiler_params=pltpu.CompilerParams(vmem_limit_bytes=GRANT),
        cost_estimate=pl.CostEstimate(flops=0, bytes_accessed=500_000, transcendentals=0),
        name="assemble",
    )(position, *sources)


def network_kernel(limits, padding, starts, segments, pos_ref, len_ref, base_ref, *refs):
    (late_ref, core_ref, chip_ref), refs = refs[:3], refs[3:]
    weights, (score_ref, peak_ref, sims_ref), scratch = refs[:8], refs[8:11], refs[11:]
    block = score_ref.shape[0]
    last = len(starts) - 1
    place(
        pos_ref, sims_ref, [late_ref], [(0, *rest) for source, *rest in segments if source == last]
    )
    lanes = sims_ref.shape[2]
    above, below = slice(lanes - EDGE, lanes), slice(lanes // 2, lanes // 2 + EDGE)

    ends = (pos_ref[0] == 0) | (pos_ref[0] == limits[0] // block - 1)
    core, chip = core_ref[...], jnp.where(ends, 0.0, chip_ref[...])

    def edges(core_side, chip_side):
        place_edges(pos_ref, sims_ref, starts, segments, 6, core, core_side)
        place_edges(pos_ref, sims_ref, starts, segments, 10, chip, chip_side)

    pl.when(pos_ref[0] % 2 == 0)(lambda: edges(below, above))
    pl.when(pos_ref[0] % 2 == 1)(lambda: edges(above, below))
    convolve(sims_ref, weights, scratch, score_ref, pos_ref, block, limits, padding)

    score = score_ref[...]
    videos = len_ref.shape[0]
    column = pos_ref[1] * block + lax.broadcasted_iota(jnp.int32, (block, block), 1)
    slot = lax.broadcasted_iota(jnp.int32, (block, 128), 1)
    start = jnp.int32(0)
    peaks = jnp.zeros((block, 128), F32)
    for video in range(videos):
        end = start + len_ref[video]
        member = (column >= start) & (column < end)
        best = jnp.max(jnp.where(member, score, -jnp.inf), axis=1, keepdims=True)
        peaks = jnp.where(slot == video, best, peaks)
        start = end
    peak_ref[...] = jnp.transpose(peaks)[0:videos]


def network(position, lengths, base, late, edges, starts, segments, weights, block, limits):
    smem = pl.BlockSpec(memory_space=pltpu.SMEM)
    vmem = pl.BlockSpec(memory_space=pltpu.VMEM)
    padding = pad_cells(block)
    arrays = [base, late, *edges]
    score, peaks, _ = pl.pallas_call(
        functools.partial(network_kernel, limits, padding, starts, segments),
        in_specs=[smem, smem] + [vmem] * len(arrays) + [vmem] * 7 + [smem],
        out_specs=[vmem, vmem, vmem],
        out_shape=[
            jax.ShapeDtypeStruct((block, block), F32),
            jax.ShapeDtypeStruct((lengths.shape[0], block), F32),
            jax.ShapeDtypeStruct(base.shape, F32),
        ],
        scratch_shapes=convolve_scratch(block, padding),
        input_output_aliases={2: 2},
        cost_estimate=pl.CostEstimate(
            flops=6_000_000_000, bytes_accessed=4_000_000, transcendentals=0
        ),
        compiler_params=pltpu.CompilerParams(vmem_limit_bytes=GRANT),
        name="network",
    )(position, lengths, *arrays, *weights)
    return score, peaks


def weights_kernel(w1_ref, b1_ref, w2_ref, b2_ref, w3_ref, b3_ref, w4_ref, *outs):
    f1_ref, o1_ref, f2_ref, o2_ref, f3_ref, o3_ref, f4_ref = outs
    c1, c2, c3 = w1_ref.shape[2], w2_ref.shape[3], w3_ref.shape[3]
    rows = lax.broadcasted_iota(jnp.int32, (256, 16 * c1), 0)
    lane = lax.broadcasted_iota(jnp.int32, (256, 16 * c1), 1) // c1
    terms = 6 * WINDOW
    third = rows >= 2 * terms
    valid = rows < 3 * terms
    rows = rows - jnp.where(third, 2 * terms, jnp.where(rows >= terms, terms, 0))
    along = jnp.zeros_like(rows)
    for offset in range(1, 6):
        along = along + jnp.where(rows >= offset * WINDOW, 1, 0)
    down = rows - along * WINDOW - 2 * ((lane // 2) % 2) - lane // 8
    along = along - 2 * (lane % 2) - (lane // 4) % 2
    taps = []
    for di in range(3):
        for dj in range(3):
            tap = jnp.concatenate([w1_ref[di, dj : dj + 1, :]] * (128 // c1), axis=1)
            taps.append(jnp.concatenate([tap] * (16 * c1 // 128), axis=1))
    for member in range(GROUP):
        dense = jnp.zeros(rows.shape, F32)
        for di in range(3):
            for dj in range(3):
                here = (down == di + PHASES * member) & (along == dj) & valid
                dense = jnp.where(here, taps[3 * di + dj], dense)
        high = dense.astype(BF).astype(F32)
        at = slice(member * 16 * c1, (member + 1) * 16 * c1)
        f1_ref[:, at] = jnp.where(third, dense - high, high).astype(BF)
    o1_ref[...] = jnp.concatenate([b1_ref[...]] * (128 // c1), axis=1)
    o2_ref[...] = jnp.concatenate([b2_ref[...]] * (128 // c2), axis=1)
    f2_ref[...] = jnp.zeros_like(f2_ref)
    reach = ((0, 1), (2, -1))
    for index in range(16):
        row_kind, col_kind, sr, sc = (index >> 3) & 1, (index >> 2) & 1, (index >> 1) & 1, index & 1
        for phase in range(4):
            di = reach[row_kind][sr] - phase // 2 + 1
            dj = reach[col_kind][sc] - phase % 2 + 1
            if 0 <= di <= 2 and 0 <= dj <= 2:
                f2_ref[index * c1 : (index + 1) * c1, phase * c2 : (phase + 1) * c2] = w2_ref[
                    di, dj
                ]
    f3_ref[...] = jnp.zeros_like(f3_ref)
    order = [(row, col) for row in range(4) for col in range(2)] + [(row, 2) for row in range(4)]
    for index, (row, dj) in enumerate(order):
        for output in range(2):
            if 0 <= row - output <= 2:
                f3_ref[index * c2 : (index + 1) * c2, output * c3 : (output + 1) * c3] = w3_ref[
                    row - output, dj
                ]
    o3_ref[...] = jnp.concatenate([b3_ref[...]] * 2, axis=1)
    fourth = jnp.concatenate([w4_ref[...].astype(F32)] * 2, axis=1)
    half = lax.broadcasted_iota(jnp.int32, f4_ref.shape, 1) // c3
    output = lax.broadcasted_iota(jnp.int32, f4_ref.shape, 0)
    f4_ref[...] = jnp.where(half == output, fourth, 0.0).astype(BF)


def network_weights(w1, b1, w2, b2, w3, b3, w4, b4):
    c1, c2, c3 = w1.shape[2], w2.shape[2], w3.shape[2]
    shapes = [
        ((256, GROUP * 16 * c1), BF),
        ((1, 128), F32),
        ((16 * c1, 4 * c2), BF),
        ((1, 128), F32),
        ((12 * c2, 2 * c3), BF),
        ((1, 2 * c3), F32),
        ((16, 2 * c3), BF),
    ]
    f1, o1, f2, o2, f3, o3, f4 = pl.pallas_call(
        weights_kernel,
        out_shape=[jax.ShapeDtypeStruct(shape, dtype) for shape, dtype in shapes],
        cost_estimate=pl.CostEstimate(flops=100_000_000, bytes_accessed=4_000_000, transcendentals=0),
        compiler_params=pltpu.CompilerParams(vmem_limit_bytes=GRANT),
        name="weights",
    )(
        w1,
        b1[None],
        jnp.transpose(w2, (0, 1, 3, 2)),
        b2[None],
        jnp.transpose(w3, (0, 1, 3, 2)),
        b3[None],
        w4[None],
    )
    return (f1, o1, f2, o2, f3, o3, f4, b4)


def body(
    query_feats,
    ref_feats,
    pair_table,
    lengths,
    query_len,
    conv1_weight,
    conv1_bias,
    conv2_weight,
    conv2_bias,
    conv3_weight,
    conv3_bias,
    conv4_weight,
    conv4_bias,
):
    qry_index = lax.axis_index("qry")
    ref_index = lax.axis_index("ref")
    senders = lax.axis_size("qry")
    blocks = lax.axis_size("ref")
    frames, regions, channels = query_feats.shape
    rows = ref_feats.shape[0]
    block = frames // PHASES
    limits = (block * senders, block * blocks)
    count = rows // PIECE
    split = count >= 3 and senders == PHASES
    odd = qry_index % 2
    nearest = (qry_index + 2 * odd - 1) % senders
    entries = [qry_index, ref_index]
    for place in (qry_index, qry_index ^ 1, nearest):
        entries += [place ^ flip if split else flip for flip in range(PHASES)]
    position = jnp.stack([jnp.asarray(entry, jnp.int32) for entry in entries])
    query = jnp.transpose(query_feats, (1, 0, 2))
    own = jnp.transpose(ref_feats[:, 0], (1, 0, 2))
    chips = senders // 2
    across = [
        [(i, (i - 2 * step) % senders) for i in range(senders)] for step in range(1, chips)
    ]
    beside = [(i, i ^ 1) for i in range(senders)]

    if split:
        late = count // 2
        middle = [at for at in range(1, count - 1) if at != late]
        groups = [[0], [count - 1]] + [[at] for at in middle] + [[late]]
    else:
        groups = [list(range(count))]

    order = [at for group in groups for at in group]
    (piece,) = cut(own, order[:1])
    source, piece = lax.optimization_barrier((own, piece))
    whole = source.reshape(regions * rows, channels)
    cuts = [piece]
    if len(order) > 1:
        cuts += cut(source, order[1:])
    found = []
    for pairs in across:
        trips = []
        for piece in cuts:
            trips.append(shift(piece, "qry", pairs))
        found.append(trips)
    sibling = shift(whole, "qry", beside)
    weights = network_weights(
        conv1_weight,
        conv1_bias,
        conv2_weight,
        conv2_bias,
        conv3_weight,
        conv3_bias,
        conv4_weight,
        conv4_bias,
    )
    here, query = similarities(
        query, [whole, sibling], position, pair_table, fetch=True
    )
    sources, segments = [here], [(0, 0, rows, 0, 0), (0, rows, rows, 1, 0)]
    shard = 2
    last = []
    for pieces in found:
        pieces = list(pieces)
        for index, group in enumerate(groups):
            batch = []
            for at in group:
                piece = pieces.pop(0)
                batch += [piece, shift(piece, "qry", beside)]
            if split and index == len(groups) - 1:
                last = batch
                break
            here = similarities(query, batch, position, pair_table)[0]
            for order, at in enumerate(group):
                for half in range(2):
                    start = PIECE * (2 * order + half)
                    segments.append((len(sources), start, PIECE, shard + half, at * PIECE))
            sources.append(here)
        shard += 2
    if not split:
        tiles = [[None] * rows for _ in range(senders)]
        for source, row, size, place, cell in segments:
            for at in range(0, size, PIECE):
                tiles[place][cell + at] = sources[source][row + at : row + at + PIECE]
        tiles = [
            jnp.concatenate([part for part in parts if part is not None], axis=0)
            for parts in tiles
        ]
        sender = jnp.arange(senders, dtype=jnp.int32)
        step = (sender // 2 - qry_index // 2) % chips
        ordered = jnp.stack(tiles)[2 * step + ((sender % 2) ^ (qry_index % 2))]
        sims = ordered.reshape(senders // PHASES, PHASES, rows, frames).transpose(1, 2, 0, 3)
        sources = [sims.reshape(PHASES * block, frames)]
        segments = [(0, phase * block, block, phase, 0) for phase in range(PHASES)]

    def cells(low):
        parts = []
        for want in range(PHASES):
            for source, row, size, place, cell in segments:
                if place == want and cell <= low and low + HALO <= cell + size:
                    parts.append(sources[source][row + low - cell : row + low - cell + HALO])
        return jnp.concatenate(parts, axis=0)

    up = [(i, i + 1) for i in range(blocks - 1)]
    down = [(b, a) for a, b in up]
    right = shift(cells(0), "ref", down)
    left = shift(cells(block - HALO), "ref", up)
    for edge, cell in ((left, -HALO), (right, block)):
        segments += [(len(sources), HALO * k, HALO, k, cell) for k in range(PHASES)]
        sources.append(edge)
    base = assembled(position, sources, segments, block)
    if split:
        for half in range(2):
            segments.append((len(sources), PIECE * half, PIECE, 2 + half, late * PIECE))
        done, core, chip = similarities(query, last, position, pair_table, sources)
        sources.append(done)
    else:
        core, chip = edge_rows(position, sources)
        done = sources[-1]
    starts = [0]
    for source in sources[:-1]:
        starts.append(starts[-1] + source.shape[0])
    pairs = [(i, (i + 1) % senders) for i in range(1, senders, 2)]
    chip = shift(chip, "qry", pairs + [(b, a) for a, b in pairs])
    core = shift(core, "qry", beside)
    score_map, peaks = network(
        position,
        lengths,
        base,
        done,
        (core, chip),
        starts,
        segments,
        weights,
        block,
        limits,
    )
    place = jnp.stack([qry_index, qry_index ^ 1])
    peaks = jnp.stack([peaks, shift(peaks, "qry", beside)])

    def between_odd(array, flip_qry, flip_ref):
        pairs = []
        for q in range(senders):
            for r in range(blocks):
                to = (q ^ flip_qry, r ^ flip_ref) if q % 2 else (q, r)
                pairs.append((q * blocks + r, to[0] * blocks + to[1]))
        return shift(array, ("qry", "ref"), pairs)

    bit = 1
    while bit < blocks:
        peaks = jnp.maximum(peaks, between_odd(peaks, 0, bit))
        bit *= 2
    row_ids = place[:, None] * block + jnp.arange(block, dtype=jnp.int32)[None]
    total = jnp.sum(jnp.where((row_ids < query_len[0])[:, None], peaks, 0.0), axis=(0, 2))
    bit = senders // 2
    while bit > 1:
        total = total + between_odd(total, bit, 0)
        bit //= 2
    given = shift(total, "qry", beside)
    return (score_map, jnp.where(odd == 1, total, given) / query_len[0].astype(F32))


def solution(mesh):
    placed = (
        P(("groups", "qry"), None, None),
        P(("groups", "ref"), "qry", None, None),
        P("groups", None),
        P("groups"),
        P("groups"),
    ) + (P(),) * 8

    return jax.shard_map(
        body,
        mesh=mesh,
        in_specs=placed,
        out_specs=(P(("groups", "qry"), "ref"), P("groups")),
        check_vma=False,
    )
```

```python
import functools
import math

import jax
import jax.numpy as jnp
from jax import lax
from jax.experimental import pallas as pl
from jax.experimental.pallas import tpu as pltpu
from jax.sharding import PartitionSpec as P


GRANT = 20 * 1024 * 1024
PIECE = 8
PHASES = 4
HALO = 2
EDGE = 8
GROUP = 3
WINDOW = PHASES * GROUP + 2
BF = jnp.bfloat16
F32 = jnp.float32


def in_hbm(array):
    return pltpu.with_memory_space_constraint(array, pltpu.HBM)


def shift(array, axis, pairs):
    return lax.ppermute(array, axis, pairs)


def cut_kernel(order, source_ref, *refs):
    outs, sems = refs[:-1], refs[-1]
    copies = []
    for index, (at, out) in enumerate(zip(order, outs)):
        piece = source_ref.at[:, pl.ds(at * PIECE, PIECE), :]
        copies.append(pltpu.make_async_copy(piece, out, sems.at[index]))
    for copy in copies:
        copy.start()
    for copy in copies:
        copy.wait()


def cut(source, order):
    regions, _, channels = source.shape
    shape = (regions, PIECE, channels)
    pieces = pl.pallas_call(
        functools.partial(cut_kernel, order),
        in_specs=[pl.BlockSpec(memory_space=pltpu.HBM)],
        out_specs=[pl.BlockSpec(memory_space=pltpu.VMEM) for _ in order],
        out_shape=[jax.ShapeDtypeStruct(shape, source.dtype) for _ in order],
        scratch_shapes=[pltpu.SemaphoreType.DMA((len(order),))],
        compiler_params=pltpu.CompilerParams(vmem_limit_bytes=GRANT),
        cost_estimate=pl.CostEstimate(
            flops=0, bytes_accessed=4 * source.size, transcendentals=0
        ),
        name="cut",
    )(in_hbm(source))
    return [piece.reshape(regions * PIECE, channels) for piece in pieces]


def write_edges(pos_ref, arrays, core_ref, chip_ref):
    total = jnp.concatenate(arrays, axis=0)
    frames = total.shape[1]
    eights = [total[at : at + 8] for at in range(0, total.shape[0], 8)]
    first = jnp.concatenate([eight[:, 0:EDGE] for eight in eights], axis=1)
    last = jnp.concatenate([eight[:, frames - EDGE : frames] for eight in eights], axis=1)
    even = pos_ref[0] % 2 == 0
    core_ref[...] = jnp.where(even, last, first)
    chip_ref[...] = jnp.where(even, first, last)


def edge_shapes(columns):
    return [jax.ShapeDtypeStruct((8, columns // 8 * EDGE), F32)] * 2


def edges_kernel(pos_ref, *refs):
    write_edges(pos_ref, [ref[...] for ref in refs[:-2]], *refs[-2:])


def edge_rows(position, sources):
    smem = pl.BlockSpec(memory_space=pltpu.SMEM)
    vmem = pl.BlockSpec(memory_space=pltpu.VMEM)
    return pl.pallas_call(
        edges_kernel,
        in_specs=[smem] + [vmem for _ in sources],
        out_specs=[vmem, vmem],
        out_shape=edge_shapes(sum(source.shape[0] for source in sources)),
        name="edges",
    )(position, *sources)


def sims_kernel(scale, spans, others, fetch, pos_ref, table_ref, query_ref, *refs):
    pieces, refs = refs[: len(spans)], refs[len(spans) :]
    done, refs = refs[:others], refs[others:]
    out_ref = refs[0]
    if fetch:
        rows_ref, sems = refs[-2], refs[-1]
    regions, frames, channels = query_ref.shape
    width = 3 if regions % 3 == 0 else 1
    if fetch:
        copies, arriving = [], []
        start = 0
        for index, (span, piece) in enumerate(zip(spans, pieces)):
            rows = pl.ds(start, span * regions)
            copies.append(pltpu.make_async_copy(piece, rows_ref.at[rows, :], sems.at[index]))
            start += span * regions
        for copy in copies:
            copy.start()
        for step in range(regions // width):
            block = pl.ds(step * width, width)
            arriving.append(
                pltpu.make_async_copy(
                    query_ref.at[block], refs[1].at[block], sems.at[len(spans) + step]
                )
            )
        for copy in arriving:
            copy.start()
        query_ref = refs[1]
        for copy in copies:
            copy.wait()

    total = None
    for step in range(regions // width):
        if fetch:
            arriving[step].wait()
        rows = (
            rows_ref[...]
            if fetch
            else jnp.concatenate([piece[...] for piece in pieces], axis=0)
        )
        products = lax.dot_general(
            rows,
            query_ref[step * width : (step + 1) * width].reshape(-1, channels),
            (((1,), (1,)), ((), ())),
            preferred_element_type=F32,
        )
        parts = []
        start = 0
        for span in spans:
            best = products[start : start + span]
            for other in range(1, regions):
                best = jnp.maximum(
                    best, products[start + other * span : start + (other + 1) * span]
                )
            part = best[:, 0:frames]
            for other in range(1, width):
                part = part + best[:, other * frames : (other + 1) * frames]
            parts.append(part)
            start += span * regions
        part = jnp.concatenate(parts, axis=0)
        total = part if total is None else total + part
    active = table_ref[pos_ref[0], pos_ref[1]] == 1
    total = total * jnp.where(active, scale, 0.0).astype(F32)
    out_ref[...] = total
    if done:
        write_edges(pos_ref, [ref[...] for ref in done] + [total], *refs[1:3])


def similarities(query, pieces, position, table, done=(), fetch=False):
    regions, frames, channels = query.shape
    spans = [piece.shape[0] // regions for piece in pieces]
    scale = 1.0 / (regions * math.sqrt(channels))
    rows = sum(spans)
    shapes = [jax.ShapeDtypeStruct((rows, frames), F32)]
    if done:
        shapes += edge_shapes(rows + sum(array.shape[0] for array in done))
    steps = 0
    if fetch:
        shapes.append(pltpu.VMEM(query.shape, query.dtype))
        steps = regions
    smem = pl.BlockSpec(memory_space=pltpu.SMEM)
    vmem = pl.BlockSpec(memory_space=pltpu.VMEM)
    return pl.pallas_call(
        functools.partial(sims_kernel, scale, spans, len(done), fetch),
        in_specs=[smem, smem, pl.BlockSpec(memory_space=pltpu.HBM) if fetch else vmem]
        + [pl.BlockSpec(memory_space=pltpu.HBM) if fetch else vmem for _ in pieces]
        + [vmem for _ in done],
        out_specs=[vmem for _ in shapes],
        out_shape=shapes,
        scratch_shapes=[
            pltpu.VMEM((rows * regions, channels), BF),
            pltpu.SemaphoreType.DMA((len(pieces) + steps,)),
        ]
        if fetch
        else [],
        compiler_params=pltpu.CompilerParams(vmem_limit_bytes=GRANT),
        cost_estimate=pl.CostEstimate(
            flops=2 * rows * regions * regions * frames * channels,
            bytes_accessed=2 * channels * regions * rows,
            transcendentals=0,
        ),
        name="similarities",
    )(position, table, *(map(in_hbm, (query, *pieces)) if fetch else (query, *pieces)), *done)


def convolve(sims_ref, weights, scratch, score_ref, pos_ref, block, limits, padding):
    w1_ref, b1_ref, w2_ref, b2_ref, w3_ref, b3_ref, w4_ref, b4_ref = weights
    y_ref, first_ref, lhs2_ref, second_ref, lhs3_ref = scratch
    map_rows, map_cols = limits
    jf, js, jt = padding
    rows1 = block + 2 * HALO
    groups = rows1 // GROUP
    row0 = pos_ref[0] * block
    col0 = pos_ref[1] * block
    lanes = sims_ref.shape[2]

    sources = [(PHASES - 1, 0)] + [(phase, 1) for phase in range(PHASES)] + [(0, 2)]
    bases = [sims_ref[phase, at : at + jf, :] for phase, at in sources]
    terms = len(sources) * WINDOW
    zero = jnp.zeros((jf, 128 - terms), F32)
    reach = PHASES * HALO + 1
    lane = lax.broadcasted_iota(jnp.int32, (jf, 128), 1)
    for group in range(groups):
        low = PHASES * GROUP * group - reach
        parts = []
        for base in bases:
            if low < 0:
                parts.append(base[:, lanes + low : lanes])
                parts.append(base[:, 0 : low + WINDOW])
            else:
                parts.append(base[:, low : low + WINDOW])
        window = jnp.concatenate(parts + [zero], axis=1)
        high = window.astype(BF).astype(F32)
        rest = pltpu.roll(window - high, terms, 1)
        again = pltpu.roll(high, 2 * terms - 128, 1)
        row = slice(group * jf, (group + 1) * jf)
        y_ref[row, 0:128] = jnp.where(lane < terms, high, rest).astype(BF)
        y_ref[row, 128:256] = jnp.where(lane < 2 * terms - 128, rest, again).astype(BF)

    cell = lax.broadcasted_iota(jnp.int32, (jf, 128), 0)

    def inside(halo, count):
        at = cell[0:count] + (col0 - halo)
        return jnp.where((at >= 0) & (at < map_cols), 1.0, 0.0).astype(F32)

    def row_flag(at):
        return jnp.where((at >= 0) & (at < map_rows), 1.0, 0.0).astype(F32)

    keep_cols = inside(HALO, jf)
    for member in range(GROUP):
        result = jnp.dot(
            y_ref[0 : groups * jf, :],
            w1_ref[:, member * 512 : (member + 1) * 512],
            preferred_element_type=F32,
        )
        pooled = jnp.maximum(
            jnp.maximum(result[:, 0:128], result[:, 128:256]),
            jnp.maximum(result[:, 256:384], result[:, 384:512]),
        )
        pooled = jnp.maximum(pooled + b1_ref[...], 0.0)
        for group in range(groups):
            at = group * GROUP + member
            keep = keep_cols * row_flag(row0 + at - HALO)
            first_ref[at, 0:jf, :] = (
                (pooled[group * jf : (group + 1) * jf] * keep).astype(BF).astype(F32)
            )

    upper = lane < 64
    left = (lane // 32) % 2 == 0
    rows2 = block + 2
    for at in range(rows2):
        centre = first_ref[at + 1, 0:jf, :]
        across = jnp.where(upper, first_ref[at + 2, 0:jf, :], first_ref[at, 0:jf, :])
        row = slice(at * js, (at + 1) * js)
        for index, value in enumerate((centre, across)):
            here = pltpu.roll(value, jf - 1, 0)
            beside = jnp.where(left, pltpu.roll(value, jf - 2, 0), value)
            lhs2_ref[row, index * 256 : index * 256 + 128] = here[0:js].astype(BF)
            lhs2_ref[row, index * 256 + 128 : index * 256 + 256] = beside[0:js].astype(BF)
    result = jnp.dot(lhs2_ref[0 : rows2 * js, :], w2_ref[...], preferred_element_type=F32)
    pooled = jnp.maximum(result[:, 0:128], result[:, 128:256])
    pooled = jnp.maximum(pooled, pltpu.roll(pooled, 64, 1))
    pooled = jnp.maximum(pooled + b2_ref[...], 0.0)
    keep_cols = inside(1, js)
    for at in range(rows2):
        keep = keep_cols * row_flag(row0 + at - 1)
        second_ref[at, 0:js, :] = (pooled[at * js : (at + 1) * js] * keep).astype(BF).astype(F32)
        if js < jt + 8:
            second_ref[at, js : jt + 8, :] = jnp.zeros((jt + 8 - js, 128), F32)

    upper = upper[0:jt]
    for at in range(block // 2):
        row = slice(at * jt, (at + 1) * jt)
        rows = [second_ref.at[2 * at + down] for down in range(4)]
        for down in range(4):
            pair = jnp.where(upper, rows[down][0:jt, :], rows[down][1 : 1 + jt, :])
            lhs3_ref[row, down * 128 : (down + 1) * 128] = pair.astype(BF)
        for half in range(2):
            pair = jnp.where(
                upper, rows[2 * half][2 : 2 + jt, :], rows[2 * half + 1][2 : 2 + jt, :]
            )
            lhs3_ref[row, (4 + half) * 128 : (5 + half) * 128] = pair.astype(BF)
    third = jnp.dot(lhs3_ref[...], w3_ref[...], preferred_element_type=F32)
    third = jnp.maximum(third + b3_ref[...], 0.0).astype(BF)
    flat = lax.dot_general(
        w4_ref[...], third, (((1,), (1,)), ((), ())), preferred_element_type=F32
    )
    flat = flat[0:8] + b4_ref[0]
    for at in range(block // 2):
        score_ref[2 * at : 2 * at + 2, :] = flat[0:2, at * jt : at * jt + block]


def pad_cells(cells):
    js = -(-(cells + 2) // 8) * 8
    return (max(-(-(cells + 4) // 8) * 8, js), js, -(-cells // 16) * 16)


def convolve_scratch(block, padding):
    jf, js, jt = padding
    rows1 = block + 2 * HALO
    return [
        pltpu.VMEM((rows1 // GROUP * jf, 256), BF),
        pltpu.VMEM((rows1, jf, 128), F32),
        pltpu.VMEM(((block + 2) * js, 512), BF),
        pltpu.VMEM((block + 2, max(js, jt + 8), 128), F32),
        pltpu.VMEM((block // 2 * jt, 768), BF),
    ]


def place(pos_ref, sims_ref, sources, segments):
    for source, row, size, shard, cell in segments:
        if source < len(sources):
            rows = slice(3 + cell, 3 + cell + size)
            sims_ref[pos_ref[2 + shard], rows, 0 : sources[source].shape[1]] = sources[source][
                row : row + size, :
            ]


def place_edges(pos_ref, sims_ref, starts, segments, table, edge, side):
    for source, row, size, shard, cell in segments:
        for at in range(0, size, 8):
            start = starts[source] + row + at
            count = min(8, size - at)
            lane = start // 8 * EDGE
            sims_ref[pos_ref[table + shard], 3 + cell + at : 3 + cell + at + count, side] = edge[
                start % 8 : start % 8 + count, lane : lane + EDGE
            ]


def assemble_kernel(segments, pos_ref, *refs):
    sources, sims_ref = refs[:-1], refs[-1]
    sims_ref[...] = jnp.zeros_like(sims_ref)
    place(pos_ref, sims_ref, sources, segments)


def assembled(position, sources, segments, block):
    smem = pl.BlockSpec(memory_space=pltpu.SMEM)
    vmem = pl.BlockSpec(memory_space=pltpu.VMEM)
    frames = sources[0].shape[1]
    return pl.pallas_call(
        functools.partial(assemble_kernel, segments),
        in_specs=[smem] + [vmem for _ in sources],
        out_specs=vmem,
        out_shape=jax.ShapeDtypeStruct((PHASES, block + 24, 2 * frames), F32),
        compiler_params=pltpu.CompilerParams(vmem_limit_bytes=GRANT),
        cost_estimate=pl.CostEstimate(flops=0, bytes_accessed=500_000, transcendentals=0),
        name="assemble",
    )(position, *sources)


def network_kernel(limits, padding, starts, segments, pos_ref, len_ref, base_ref, *refs):
    (late_ref, core_ref, chip_ref), refs = refs[:3], refs[3:]
    weights, (score_ref, peak_ref, sims_ref), scratch = refs[:8], refs[8:11], refs[11:]
    block = score_ref.shape[0]
    last = len(starts) - 1
    place(
        pos_ref, sims_ref, [late_ref], [(0, *rest) for source, *rest in segments if source == last]
    )
    lanes = sims_ref.shape[2]
    above, below = slice(lanes - EDGE, lanes), slice(lanes // 2, lanes // 2 + EDGE)

    ends = (pos_ref[0] == 0) | (pos_ref[0] == limits[0] // block - 1)
    core, chip = core_ref[...], jnp.where(ends, 0.0, chip_ref[...])

    def edges(core_side, chip_side):
        place_edges(pos_ref, sims_ref, starts, segments, 6, core, core_side)
        place_edges(pos_ref, sims_ref, starts, segments, 10, chip, chip_side)

    pl.when(pos_ref[0] % 2 == 0)(lambda: edges(below, above))
    pl.when(pos_ref[0] % 2 == 1)(lambda: edges(above, below))
    convolve(sims_ref, weights, scratch, score_ref, pos_ref, block, limits, padding)

    score = score_ref[...]
    videos = len_ref.shape[0]
    column = pos_ref[1] * block + lax.broadcasted_iota(jnp.int32, (block, block), 1)
    slot = lax.broadcasted_iota(jnp.int32, (block, 128), 1)
    start = jnp.int32(0)
    peaks = jnp.zeros((block, 128), F32)
    for video in range(videos):
        end = start + len_ref[video]
        member = (column >= start) & (column < end)
        best = jnp.max(jnp.where(member, score, -jnp.inf), axis=1, keepdims=True)
        peaks = jnp.where(slot == video, best, peaks)
        start = end
    peak_ref[...] = jnp.transpose(peaks)[0:videos]


def network(position, lengths, base, late, edges, starts, segments, weights, block, limits):
    smem = pl.BlockSpec(memory_space=pltpu.SMEM)
    vmem = pl.BlockSpec(memory_space=pltpu.VMEM)
    padding = pad_cells(block)
    arrays = [base, late, *edges]
    score, peaks, _ = pl.pallas_call(
        functools.partial(network_kernel, limits, padding, starts, segments),
        in_specs=[smem, smem] + [vmem] * len(arrays) + [vmem] * 7 + [smem],
        out_specs=[vmem, vmem, vmem],
        out_shape=[
            jax.ShapeDtypeStruct((block, block), F32),
            jax.ShapeDtypeStruct((lengths.shape[0], block), F32),
            jax.ShapeDtypeStruct(base.shape, F32),
        ],
        scratch_shapes=convolve_scratch(block, padding),
        input_output_aliases={2: 2},
        cost_estimate=pl.CostEstimate(
            flops=6_000_000_000, bytes_accessed=4_000_000, transcendentals=0
        ),
        compiler_params=pltpu.CompilerParams(vmem_limit_bytes=GRANT),
        name="network",
    )(position, lengths, *arrays, *weights)
    return score, peaks


def weights_kernel(w1_ref, b1_ref, w2_ref, b2_ref, w3_ref, b3_ref, w4_ref, *outs):
    f1_ref, o1_ref, f2_ref, o2_ref, f3_ref, o3_ref, f4_ref = outs
    c1, c2, c3 = w1_ref.shape[2], w2_ref.shape[3], w3_ref.shape[3]
    rows = lax.broadcasted_iota(jnp.int32, (256, 16 * c1), 0)
    lane = lax.broadcasted_iota(jnp.int32, (256, 16 * c1), 1) // c1
    terms = 6 * WINDOW
    third = rows >= 2 * terms
    valid = rows < 3 * terms
    rows = rows - jnp.where(third, 2 * terms, jnp.where(rows >= terms, terms, 0))
    along = jnp.zeros_like(rows)
    for offset in range(1, 6):
        along = along + jnp.where(rows >= offset * WINDOW, 1, 0)
    down = rows - along * WINDOW - 2 * ((lane // 2) % 2) - lane // 8
    along = along - 2 * (lane % 2) - (lane // 4) % 2
    taps = []
    for di in range(3):
        for dj in range(3):
            tap = jnp.concatenate([w1_ref[di, dj : dj + 1, :]] * (128 // c1), axis=1)
            taps.append(jnp.concatenate([tap] * (16 * c1 // 128), axis=1))
    for member in range(GROUP):
        dense = jnp.zeros(rows.shape, F32)
        for di in range(3):
            for dj in range(3):
                here = (down == di + PHASES * member) & (along == dj) & valid
                dense = jnp.where(here, taps[3 * di + dj], dense)
        high = dense.astype(BF).astype(F32)
        at = slice(member * 16 * c1, (member + 1) * 16 * c1)
        f1_ref[:, at] = jnp.where(third, dense - high, high).astype(BF)
    o1_ref[...] = jnp.concatenate([b1_ref[...]] * (128 // c1), axis=1)
    o2_ref[...] = jnp.concatenate([b2_ref[...]] * (128 // c2), axis=1)
    f2_ref[...] = jnp.zeros_like(f2_ref)
    reach = ((0, 1), (2, -1))
    for index in range(16):
        row_kind, col_kind, sr, sc = (index >> 3) & 1, (index >> 2) & 1, (index >> 1) & 1, index & 1
        for phase in range(4):
            di = reach[row_kind][sr] - phase // 2 + 1
            dj = reach[col_kind][sc] - phase % 2 + 1
            if 0 <= di <= 2 and 0 <= dj <= 2:
                f2_ref[index * c1 : (index + 1) * c1, phase * c2 : (phase + 1) * c2] = w2_ref[
                    di, dj
                ]
    f3_ref[...] = jnp.zeros_like(f3_ref)
    order = [(row, col) for row in range(4) for col in range(2)] + [(row, 2) for row in range(4)]
    for index, (row, dj) in enumerate(order):
        for output in range(2):
            if 0 <= row - output <= 2:
                f3_ref[index * c2 : (index + 1) * c2, output * c3 : (output + 1) * c3] = w3_ref[
                    row - output, dj
                ]
    o3_ref[...] = jnp.concatenate([b3_ref[...]] * 2, axis=1)
    fourth = jnp.concatenate([w4_ref[...].astype(F32)] * 2, axis=1)
    half = lax.broadcasted_iota(jnp.int32, f4_ref.shape, 1) // c3
    output = lax.broadcasted_iota(jnp.int32, f4_ref.shape, 0)
    f4_ref[...] = jnp.where(half == output, fourth, 0.0).astype(BF)


def network_weights(w1, b1, w2, b2, w3, b3, w4, b4):
    c1, c2, c3 = w1.shape[2], w2.shape[2], w3.shape[2]
    shapes = [
        ((256, GROUP * 16 * c1), BF),
        ((1, 128), F32),
        ((16 * c1, 4 * c2), BF),
        ((1, 128), F32),
        ((12 * c2, 2 * c3), BF),
        ((1, 2 * c3), F32),
        ((16, 2 * c3), BF),
    ]
    f1, o1, f2, o2, f3, o3, f4 = pl.pallas_call(
        weights_kernel,
        out_shape=[jax.ShapeDtypeStruct(shape, dtype) for shape, dtype in shapes],
        cost_estimate=pl.CostEstimate(flops=100_000_000, bytes_accessed=4_000_000, transcendentals=0),
        compiler_params=pltpu.CompilerParams(vmem_limit_bytes=GRANT),
        name="weights",
    )(
        w1,
        b1[None],
        jnp.transpose(w2, (0, 1, 3, 2)),
        b2[None],
        jnp.transpose(w3, (0, 1, 3, 2)),
        b3[None],
        w4[None],
    )
    return (f1, o1, f2, o2, f3, o3, f4, b4)


def body(
    query_feats,
    ref_feats,
    pair_table,
    lengths,
    query_len,
    conv1_weight,
    conv1_bias,
    conv2_weight,
    conv2_bias,
    conv3_weight,
    conv3_bias,
    conv4_weight,
    conv4_bias,
):
    qry_index = lax.axis_index("qry")
    ref_index = lax.axis_index("ref")
    senders = lax.axis_size("qry")
    blocks = lax.axis_size("ref")
    frames, regions, channels = query_feats.shape
    rows = ref_feats.shape[0]
    block = frames // PHASES
    limits = (block * senders, block * blocks)
    count = rows // PIECE
    split = count >= 3 and senders == PHASES
    odd = qry_index % 2
    nearest = (qry_index + 2 * odd - 1) % senders
    entries = [qry_index, ref_index]
    for place in (qry_index, qry_index ^ 1, nearest):
        entries += [place ^ flip if split else flip for flip in range(PHASES)]
    position = jnp.stack([jnp.asarray(entry, jnp.int32) for entry in entries])
    query = jnp.transpose(query_feats, (1, 0, 2))
    own = jnp.transpose(ref_feats[:, 0], (1, 0, 2))
    chips = senders // 2
    across = [
        [(i, (i - 2 * step) % senders ^ 1) for i in range(senders)] for step in range(1, chips)
    ]
    beside = [(i, i ^ 1) for i in range(senders)]

    if split:
        late = count // 2
        middle = [at for at in range(1, count - 1) if at != late]
        groups = [[0], [count - 1]] + [[at] for at in middle] + [[late]]
    else:
        groups = [list(range(count))]

    order = [at for group in groups for at in group]
    (piece,) = cut(own, order[:1])
    source, piece = lax.optimization_barrier((own, piece))
    whole = source.reshape(regions * rows, channels)
    cuts = [piece]
    if len(order) > 1:
        cuts += cut(source, order[1:])
    found = []
    for pairs in across:
        trips = []
        for piece in cuts:
            trips.append(shift(piece, "qry", pairs))
        found.append(trips)
    sibling = shift(whole, "qry", beside)
    weights = network_weights(
        conv1_weight,
        conv1_bias,
        conv2_weight,
        conv2_bias,
        conv3_weight,
        conv3_bias,
        conv4_weight,
        conv4_bias,
    )
    here, query = similarities(
        query, [whole, sibling], position, pair_table, fetch=True
    )
    sources, segments = [here], [(0, 0, rows, 0, 0), (0, rows, rows, 1, 0)]
    shard = 2
    last = []
    for pieces in found:
        pieces = list(pieces)
        for index, group in enumerate(groups):
            batch = []
            for at in group:
                piece = pieces.pop(0)
                batch += [piece, shift(piece, "qry", beside)]
            if split and index == len(groups) - 1:
                last = batch
                break
            here = similarities(query, batch, position, pair_table)[0]
            for order, at in enumerate(group):
                for half in range(2):
                    start = PIECE * (2 * order + half)
                    segments.append((len(sources), start, PIECE, shard + 1 - half, at * PIECE))
            sources.append(here)
        shard += 2
    if not split:
        tiles = [[None] * rows for _ in range(senders)]
        for source, row, size, place, cell in segments:
            for at in range(0, size, PIECE):
                tiles[place][cell + at] = sources[source][row + at : row + at + PIECE]
        tiles = [
            jnp.concatenate([part for part in parts if part is not None], axis=0)
            for parts in tiles
        ]
        sender = jnp.arange(senders, dtype=jnp.int32)
        step = (sender // 2 - qry_index // 2) % chips
        ordered = jnp.stack(tiles)[2 * step + ((sender % 2) ^ (qry_index % 2))]
        sims = ordered.reshape(senders // PHASES, PHASES, rows, frames).transpose(1, 2, 0, 3)
        sources = [sims.reshape(PHASES * block, frames)]
        segments = [(0, phase * block, block, phase, 0) for phase in range(PHASES)]

    def cells(low):
        parts = []
        for want in range(PHASES):
            for source, row, size, place, cell in segments:
                if place == want and cell <= low and low + HALO <= cell + size:
                    parts.append(sources[source][row + low - cell : row + low - cell + HALO])
        return jnp.concatenate(parts, axis=0)

    up = [(i, i + 1) for i in range(blocks - 1)]
    down = [(b, a) for a, b in up]
    right = shift(cells(0), "ref", down)
    left = shift(cells(block - HALO), "ref", up)
    for edge, cell in ((left, -HALO), (right, block)):
        segments += [(len(sources), HALO * k, HALO, k, cell) for k in range(PHASES)]
        sources.append(edge)
    base = assembled(position, sources, segments, block)
    if split:
        for half in range(2):
            segments.append((len(sources), PIECE * half, PIECE, 3 - half, late * PIECE))
        done, core, chip = similarities(query, last, position, pair_table, sources)
        sources.append(done)
    else:
        core, chip = edge_rows(position, sources)
        done = sources[-1]
    starts = [0]
    for source in sources[:-1]:
        starts.append(starts[-1] + source.shape[0])
    pairs = [(i, (i + 1) % senders) for i in range(1, senders, 2)]
    chip = shift(chip, "qry", pairs + [(b, a) for a, b in pairs])
    core = shift(core, "qry", beside)
    score_map, peaks = network(
        position,
        lengths,
        base,
        done,
        (core, chip),
        starts,
        segments,
        weights,
        block,
        limits,
    )
    mine, other = peaks, shift(peaks, "qry", beside)
    peaks = jnp.where(odd == 1, jnp.stack([other, mine]), jnp.stack([mine, other]))

    def swap(array, flip_qry, flip_ref):
        pairs = [
            (q * blocks + r, (q ^ flip_qry) * blocks + (r ^ flip_ref))
            for q in range(senders)
            for r in range(blocks)
        ]
        return shift(array, ("qry", "ref"), pairs)

    bit = 1
    while bit < blocks:
        peaks = jnp.maximum(peaks, swap(peaks, 1, bit))
        bit *= 2
    first_row = (qry_index - odd) * block
    row_ids = first_row + jnp.arange(2 * block, dtype=jnp.int32).reshape(2, 1, block)
    total = jnp.sum(jnp.where(row_ids < query_len[0], peaks, 0.0), axis=(0, 2))
    bit = 2
    while bit < senders:
        total = total + swap(total, bit + 1, 0)
        bit *= 2
    return (score_map, total / query_len[0].astype(F32))


def solution(mesh):
    placed = (
        P(("groups", "qry"), None, None),
        P(("groups", "ref"), "qry", None, None),
        P("groups", None),
        P("groups"),
        P("groups"),
    ) + (P(),) * 8

    return jax.shard_map(
        body,
        mesh=mesh,
        in_specs=placed,
        out_specs=(P(("groups", "qry"), "ref"), P("groups")),
        check_vma=False,
    )
```

```python
import functools
import math

import jax
import jax.numpy as jnp
from jax import lax
from jax.experimental import pallas as pl
from jax.experimental.pallas import tpu as pltpu
from jax.sharding import PartitionSpec as P


GRANT = 20 * 1024 * 1024
PIECE = 8
PHASES = 4
HALO = 2
EDGE = 8
GROUP = 3
WINDOW = PHASES * GROUP + 2
BF = jnp.bfloat16
F32 = jnp.float32


def in_hbm(array):
    return pltpu.with_memory_space_constraint(array, pltpu.HBM)


def shift(array, axis, pairs):
    return lax.ppermute(array, axis, pairs)


def cut_kernel(order, source_ref, *refs):
    outs, sems = refs[:-1], refs[-1]
    copies = []
    for index, (at, out) in enumerate(zip(order, outs)):
        piece = source_ref.at[:, pl.ds(at * PIECE, PIECE), :]
        copies.append(pltpu.make_async_copy(piece, out, sems.at[index]))
    for copy in copies:
        copy.start()
    for copy in copies:
        copy.wait()


def cut(source, order):
    regions, _, channels = source.shape
    shape = (regions, PIECE, channels)
    pieces = pl.pallas_call(
        functools.partial(cut_kernel, order),
        in_specs=[pl.BlockSpec(memory_space=pltpu.HBM)],
        out_specs=[pl.BlockSpec(memory_space=pltpu.VMEM) for _ in order],
        out_shape=[jax.ShapeDtypeStruct(shape, source.dtype) for _ in order],
        scratch_shapes=[pltpu.SemaphoreType.DMA((len(order),))],
        compiler_params=pltpu.CompilerParams(vmem_limit_bytes=GRANT),
        cost_estimate=pl.CostEstimate(
            flops=0, bytes_accessed=4 * source.size, transcendentals=0
        ),
        name="cut",
    )(in_hbm(source))
    return [piece.reshape(regions * PIECE, channels) for piece in pieces]


def write_edges(pos_ref, arrays, core_ref, chip_ref):
    total = jnp.concatenate(arrays, axis=0)
    frames = total.shape[1]
    eights = [total[at : at + 8] for at in range(0, total.shape[0], 8)]
    first = jnp.concatenate([eight[:, 0:EDGE] for eight in eights], axis=1)
    last = jnp.concatenate([eight[:, frames - EDGE : frames] for eight in eights], axis=1)
    even = pos_ref[0] % 2 == 0
    core_ref[...] = jnp.where(even, last, first)
    chip_ref[...] = jnp.where(even, first, last)


def edge_shapes(columns):
    return [jax.ShapeDtypeStruct((8, columns // 8 * EDGE), F32)] * 2


def edges_kernel(pos_ref, *refs):
    write_edges(pos_ref, [ref[...] for ref in refs[:-2]], *refs[-2:])


def edge_rows(position, sources):
    smem = pl.BlockSpec(memory_space=pltpu.SMEM)
    vmem = pl.BlockSpec(memory_space=pltpu.VMEM)
    return pl.pallas_call(
        edges_kernel,
        in_specs=[smem] + [vmem for _ in sources],
        out_specs=[vmem, vmem],
        out_shape=edge_shapes(sum(source.shape[0] for source in sources)),
        name="edges",
    )(position, *sources)


def sims_kernel(scale, spans, others, fetch, pos_ref, table_ref, query_ref, *refs):
    pieces, refs = refs[: len(spans)], refs[len(spans) :]
    done, refs = refs[:others], refs[others:]
    out_ref = refs[0]
    if fetch:
        rows_ref, sems = refs[-2], refs[-1]
    regions, frames, channels = query_ref.shape
    width = 3 if regions % 3 == 0 else 1
    if fetch:
        copies, arriving = [], []
        start = 0
        for index, (span, piece) in enumerate(zip(spans, pieces)):
            rows = pl.ds(start, span * regions)
            copies.append(pltpu.make_async_copy(piece, rows_ref.at[rows, :], sems.at[index]))
            start += span * regions
        for copy in copies:
            copy.start()
        for step in range(regions // width):
            block = pl.ds(step * width, width)
            arriving.append(
                pltpu.make_async_copy(
                    query_ref.at[block], refs[1].at[block], sems.at[len(spans) + step]
                )
            )
        for copy in arriving:
            copy.start()
        query_ref = refs[1]
        for copy in copies:
            copy.wait()

    total = None
    for step in range(regions // width):
        if fetch:
            arriving[step].wait()
        rows = (
            rows_ref[...]
            if fetch
            else jnp.concatenate([piece[...] for piece in pieces], axis=0)
        )
        products = lax.dot_general(
            rows,
            query_ref[step * width : (step + 1) * width].reshape(-1, channels),
            (((1,), (1,)), ((), ())),
            preferred_element_type=F32,
        )
        parts = []
        start = 0
        for span in spans:
            best = products[start : start + span]
            for other in range(1, regions):
                best = jnp.maximum(
                    best, products[start + other * span : start + (other + 1) * span]
                )
            part = best[:, 0:frames]
            for other in range(1, width):
                part = part + best[:, other * frames : (other + 1) * frames]
            parts.append(part)
            start += span * regions
        part = jnp.concatenate(parts, axis=0)
        total = part if total is None else total + part
    active = table_ref[pos_ref[0], pos_ref[1]] == 1
    total = total * jnp.where(active, scale, 0.0).astype(F32)
    out_ref[...] = total
    if done:
        write_edges(pos_ref, [ref[...] for ref in done] + [total], *refs[1:3])


def similarities(query, pieces, position, table, done=(), fetch=False):
    regions, frames, channels = query.shape
    spans = [piece.shape[0] // regions for piece in pieces]
    scale = 1.0 / (regions * math.sqrt(channels))
    rows = sum(spans)
    shapes = [jax.ShapeDtypeStruct((rows, frames), F32)]
    if done:
        shapes += edge_shapes(rows + sum(array.shape[0] for array in done))
    steps = 0
    if fetch:
        shapes.append(pltpu.VMEM(query.shape, query.dtype))
        steps = regions
    smem = pl.BlockSpec(memory_space=pltpu.SMEM)
    vmem = pl.BlockSpec(memory_space=pltpu.VMEM)
    return pl.pallas_call(
        functools.partial(sims_kernel, scale, spans, len(done), fetch),
        in_specs=[smem, smem, pl.BlockSpec(memory_space=pltpu.HBM) if fetch else vmem]
        + [pl.BlockSpec(memory_space=pltpu.HBM) if fetch else vmem for _ in pieces]
        + [vmem for _ in done],
        out_specs=[vmem for _ in shapes],
        out_shape=shapes,
        scratch_shapes=[
            pltpu.VMEM((rows * regions, channels), BF),
            pltpu.SemaphoreType.DMA((len(pieces) + steps,)),
        ]
        if fetch
        else [],
        compiler_params=pltpu.CompilerParams(vmem_limit_bytes=GRANT),
        cost_estimate=pl.CostEstimate(
            flops=2 * rows * regions * regions * frames * channels,
            bytes_accessed=2 * channels * regions * rows,
            transcendentals=0,
        ),
        name="similarities",
    )(position, table, *(map(in_hbm, (query, *pieces)) if fetch else (query, *pieces)), *done)


def inside_columns(pos_ref, block, limits, count, halo):
    at = lax.broadcasted_iota(jnp.int32, (count, 128), 0) + (pos_ref[1] * block - halo)
    return jnp.where((at >= 0) & (at < limits[1]), 1.0, 0.0).astype(F32)


def inside_rows(pos_ref, block, limits, at):
    at = pos_ref[0] * block + at
    return jnp.where((at >= 0) & (at < limits[0]), 1.0, 0.0).astype(F32)


def first_map(sims_ref, w1_ref, b1_ref, y_ref, first_ref, pos_ref, block, limits, tiles):
    lanes = sims_ref.shape[2]
    sources = [(PHASES - 1, 0)] + [(phase, 1) for phase in range(PHASES)] + [(0, 2)]
    terms = len(sources) * WINDOW
    reach = PHASES * HALO + 1
    spots, start = [], 0
    for group, first, size in tiles:
        low = PHASES * GROUP * group - reach
        parts = []
        for phase, at in sources:
            base = sims_ref[phase, first + at : first + at + size, :]
            if low < 0:
                parts.append(base[:, lanes + low : lanes])
                parts.append(base[:, 0 : low + WINDOW])
            else:
                parts.append(base[:, low : low + WINDOW])
        window = jnp.concatenate(parts + [jnp.zeros((size, 128 - terms), F32)], axis=1)
        high = window.astype(BF).astype(F32)
        rest = pltpu.roll(window - high, terms, 1)
        again = pltpu.roll(high, 2 * terms - 128, 1)
        lane = lax.broadcasted_iota(jnp.int32, (size, 128), 1)
        row = slice(start, start + size)
        y_ref[row, 0:128] = jnp.where(lane < terms, high, rest).astype(BF)
        y_ref[row, 128:256] = jnp.where(lane < 2 * terms - 128, rest, again).astype(BF)
        spots.append(start)
        start += size

    keep_cols = inside_columns(pos_ref, block, limits, first_ref.shape[1], HALO)
    for member in range(GROUP):
        result = jnp.dot(
            y_ref[0:start, :],
            w1_ref[:, member * 512 : (member + 1) * 512],
            preferred_element_type=F32,
        )
        pooled = jnp.maximum(
            jnp.maximum(result[:, 0:128], result[:, 128:256]),
            jnp.maximum(result[:, 256:384], result[:, 384:512]),
        )
        pooled = jnp.maximum(pooled + b1_ref[...], 0.0)
        for (group, first, size), spot in zip(tiles, spots):
            at = group * GROUP + member
            keep = keep_cols[first : first + size] * inside_rows(
                pos_ref, block, limits, at - HALO
            )
            first_ref[at, first : first + size, :] = (
                (pooled[spot : spot + size] * keep).astype(BF).astype(F32)
            )


def first_tiles(block, frames, jf, late):
    groups = (block + 2 * HALO) // GROUP
    reach = PHASES * HALO + 1
    early, rest, whole = [], [], []
    for group in range(groups):
        low = PHASES * GROUP * group - reach
        if low >= 0 and low + WINDOW <= frames:
            early += [(group, 0, late)]
            rest += [(group, late, 2 * PIECE)]
        else:
            whole += [(group, 0, jf)]
    ends = [(group, late + 2 * PIECE, jf - late - 2 * PIECE) for group, _, _ in early]
    return early + ends, rest + whole


def convolve(sims_ref, first_ref, weights, scratch, score_ref, pos_ref, block, limits, padding, tiles):
    w1_ref, b1_ref, w2_ref, b2_ref, w3_ref, b3_ref, w4_ref, b4_ref = weights
    y_ref, lhs2_ref, second_ref, lhs3_ref = scratch
    jf, js, jt = padding
    first_map(sims_ref, w1_ref, b1_ref, y_ref, first_ref, pos_ref, block, limits, tiles)
    lane = lax.broadcasted_iota(jnp.int32, (jf, 128), 1)

    upper = lane < 64
    left = (lane // 32) % 2 == 0
    rows2 = block + 2
    for at in range(rows2):
        centre = first_ref[at + 1, 0:jf, :]
        across = jnp.where(upper, first_ref[at + 2, 0:jf, :], first_ref[at, 0:jf, :])
        row = slice(at * js, (at + 1) * js)
        for index, value in enumerate((centre, across)):
            here = pltpu.roll(value, jf - 1, 0)
            beside = jnp.where(left, pltpu.roll(value, jf - 2, 0), value)
            lhs2_ref[row, index * 256 : index * 256 + 128] = here[0:js].astype(BF)
            lhs2_ref[row, index * 256 + 128 : index * 256 + 256] = beside[0:js].astype(BF)
    result = jnp.dot(lhs2_ref[0 : rows2 * js, :], w2_ref[...], preferred_element_type=F32)
    pooled = jnp.maximum(result[:, 0:128], result[:, 128:256])
    pooled = jnp.maximum(pooled, pltpu.roll(pooled, 64, 1))
    pooled = jnp.maximum(pooled + b2_ref[...], 0.0)
    keep_cols = inside_columns(pos_ref, block, limits, js, 1)
    for at in range(rows2):
        keep = keep_cols * inside_rows(pos_ref, block, limits, at - 1)
        second_ref[at, 0:js, :] = (pooled[at * js : (at + 1) * js] * keep).astype(BF).astype(F32)
        if js < jt + 8:
            second_ref[at, js : jt + 8, :] = jnp.zeros((jt + 8 - js, 128), F32)

    upper = upper[0:jt]
    for at in range(block // 2):
        row = slice(at * jt, (at + 1) * jt)
        rows = [second_ref.at[2 * at + down] for down in range(4)]
        for down in range(4):
            pair = jnp.where(upper, rows[down][0:jt, :], rows[down][1 : 1 + jt, :])
            lhs3_ref[row, down * 128 : (down + 1) * 128] = pair.astype(BF)
        for half in range(2):
            pair = jnp.where(
                upper, rows[2 * half][2 : 2 + jt, :], rows[2 * half + 1][2 : 2 + jt, :]
            )
            lhs3_ref[row, (4 + half) * 128 : (5 + half) * 128] = pair.astype(BF)
    third = jnp.dot(lhs3_ref[...], w3_ref[...], preferred_element_type=F32)
    third = jnp.maximum(third + b3_ref[...], 0.0).astype(BF)
    flat = lax.dot_general(
        w4_ref[...], third, (((1,), (1,)), ((), ())), preferred_element_type=F32
    )
    flat = flat[0:8] + b4_ref[0]
    for at in range(block // 2):
        score_ref[2 * at : 2 * at + 2, :] = flat[0:2, at * jt : at * jt + block]


def pad_cells(cells):
    js = -(-(cells + 2) // 8) * 8
    return (max(-(-(cells + 4) // 8) * 8, js), js, -(-cells // 16) * 16)


def convolve_scratch(block, padding, tiles):
    _, js, jt = padding
    return [
        pltpu.VMEM((sum(size for _, _, size in tiles), 256), BF),
        pltpu.VMEM(((block + 2) * js, 512), BF),
        pltpu.VMEM((block + 2, max(js, jt + 8), 128), F32),
        pltpu.VMEM((block // 2 * jt, 768), BF),
    ]


def place(pos_ref, sims_ref, sources, segments):
    for source, row, size, shard, cell in segments:
        if source < len(sources):
            rows = slice(3 + cell, 3 + cell + size)
            sims_ref[pos_ref[2 + shard], rows, 0 : sources[source].shape[1]] = sources[source][
                row : row + size, :
            ]


def place_edges(pos_ref, sims_ref, starts, segments, table, edge, side):
    for source, row, size, shard, cell in segments:
        for at in range(0, size, 8):
            start = starts[source] + row + at
            count = min(8, size - at)
            lane = start // 8 * EDGE
            sims_ref[pos_ref[table + shard], 3 + cell + at : 3 + cell + at + count, side] = edge[
                start % 8 : start % 8 + count, lane : lane + EDGE
            ]


def assemble_kernel(segments, tiles, block, limits, pos_ref, *refs):
    sources, (w1_ref, b1_ref, sims_ref, first_ref, y_ref) = refs[:-5], refs[-5:]
    sims_ref[...] = jnp.zeros_like(sims_ref)
    place(pos_ref, sims_ref, sources, segments)
    first_map(sims_ref, w1_ref, b1_ref, y_ref, first_ref, pos_ref, block, limits, tiles)


def assembled(position, sources, segments, weights, tiles, block, limits):
    smem = pl.BlockSpec(memory_space=pltpu.SMEM)
    vmem = pl.BlockSpec(memory_space=pltpu.VMEM)
    frames = sources[0].shape[1]
    return pl.pallas_call(
        functools.partial(assemble_kernel, segments, tiles, block, limits),
        in_specs=[smem] + [vmem for _ in sources] + [vmem, vmem],
        out_specs=[vmem, vmem],
        out_shape=[
            jax.ShapeDtypeStruct((PHASES, block + 24, 2 * frames), F32),
            jax.ShapeDtypeStruct((block + 2 * HALO, pad_cells(block)[0], 128), F32),
        ],
        scratch_shapes=[pltpu.VMEM((sum(size for _, _, size in tiles), 256), BF)],
        compiler_params=pltpu.CompilerParams(vmem_limit_bytes=GRANT),
        cost_estimate=pl.CostEstimate(
            flops=1_000_000_000, bytes_accessed=500_000, transcendentals=0
        ),
        name="assemble",
    )(position, *sources, *weights)


def network_kernel(limits, padding, starts, segments, tiles, pos_ref, len_ref, *refs):
    (_, _, late_ref, core_ref, chip_ref), refs = refs[:5], refs[5:]
    weights, (score_ref, peak_ref, sims_ref, first_ref), scratch = refs[:8], refs[8:12], refs[12:]
    block = score_ref.shape[0]
    last = len(starts) - 1
    place(
        pos_ref, sims_ref, [late_ref], [(0, *rest) for source, *rest in segments if source == last]
    )
    lanes = sims_ref.shape[2]
    above, below = slice(lanes - EDGE, lanes), slice(lanes // 2, lanes // 2 + EDGE)

    ends = (pos_ref[0] == 0) | (pos_ref[0] == limits[0] // block - 1)
    core, chip = core_ref[...], jnp.where(ends, 0.0, chip_ref[...])

    def edges(core_side, chip_side):
        place_edges(pos_ref, sims_ref, starts, segments, 6, core, core_side)
        place_edges(pos_ref, sims_ref, starts, segments, 10, chip, chip_side)

    pl.when(pos_ref[0] % 2 == 0)(lambda: edges(below, above))
    pl.when(pos_ref[0] % 2 == 1)(lambda: edges(above, below))
    convolve(
        sims_ref, first_ref, weights, scratch, score_ref, pos_ref, block, limits, padding, tiles
    )

    score = score_ref[...]
    videos = len_ref.shape[0]
    column = pos_ref[1] * block + lax.broadcasted_iota(jnp.int32, (block, block), 1)
    slot = lax.broadcasted_iota(jnp.int32, (block, 128), 1)
    start = jnp.int32(0)
    peaks = jnp.zeros((block, 128), F32)
    for video in range(videos):
        end = start + len_ref[video]
        member = (column >= start) & (column < end)
        best = jnp.max(jnp.where(member, score, -jnp.inf), axis=1, keepdims=True)
        peaks = jnp.where(slot == video, best, peaks)
        start = end
    peak_ref[...] = jnp.transpose(peaks)[0:videos]


def network(
    position, lengths, base, first, late, edges, starts, segments, tiles, weights, block, limits
):
    smem = pl.BlockSpec(memory_space=pltpu.SMEM)
    vmem = pl.BlockSpec(memory_space=pltpu.VMEM)
    padding = pad_cells(block)
    arrays = [base, first, late, *edges]
    score, peaks, *_ = pl.pallas_call(
        functools.partial(network_kernel, limits, padding, starts, segments, tiles),
        in_specs=[smem, smem] + [vmem] * len(arrays) + [vmem] * 7 + [smem],
        out_specs=[vmem] * 4,
        out_shape=[
            jax.ShapeDtypeStruct((block, block), F32),
            jax.ShapeDtypeStruct((lengths.shape[0], block), F32),
            jax.ShapeDtypeStruct(base.shape, F32),
            jax.ShapeDtypeStruct(first.shape, F32),
        ],
        scratch_shapes=convolve_scratch(block, padding, tiles),
        input_output_aliases={2: 2, 3: 3},
        cost_estimate=pl.CostEstimate(
            flops=6_000_000_000, bytes_accessed=4_000_000, transcendentals=0
        ),
        compiler_params=pltpu.CompilerParams(vmem_limit_bytes=GRANT),
        name="network",
    )(position, lengths, *arrays, *weights)
    return score, peaks


def weights_kernel(w1_ref, b1_ref, w2_ref, b2_ref, w3_ref, b3_ref, w4_ref, *outs):
    f1_ref, o1_ref, f2_ref, o2_ref, f3_ref, o3_ref, f4_ref = outs
    c1, c2, c3 = w1_ref.shape[2], w2_ref.shape[3], w3_ref.shape[3]
    rows = lax.broadcasted_iota(jnp.int32, (256, 16 * c1), 0)
    lane = lax.broadcasted_iota(jnp.int32, (256, 16 * c1), 1) // c1
    terms = 6 * WINDOW
    third = rows >= 2 * terms
    valid = rows < 3 * terms
    rows = rows - jnp.where(third, 2 * terms, jnp.where(rows >= terms, terms, 0))
    along = jnp.zeros_like(rows)
    for offset in range(1, 6):
        along = along + jnp.where(rows >= offset * WINDOW, 1, 0)
    down = rows - along * WINDOW - 2 * ((lane // 2) % 2) - lane // 8
    along = along - 2 * (lane % 2) - (lane // 4) % 2
    taps = []
    for di in range(3):
        for dj in range(3):
            tap = jnp.concatenate([w1_ref[di, dj : dj + 1, :]] * (128 // c1), axis=1)
            taps.append(jnp.concatenate([tap] * (16 * c1 // 128), axis=1))
    for member in range(GROUP):
        dense = jnp.zeros(rows.shape, F32)
        for di in range(3):
            for dj in range(3):
                here = (down == di + PHASES * member) & (along == dj) & valid
                dense = jnp.where(here, taps[3 * di + dj], dense)
        high = dense.astype(BF).astype(F32)
        at = slice(member * 16 * c1, (member + 1) * 16 * c1)
        f1_ref[:, at] = jnp.where(third, dense - high, high).astype(BF)
    o1_ref[...] = jnp.concatenate([b1_ref[...]] * (128 // c1), axis=1)
    o2_ref[...] = jnp.concatenate([b2_ref[...]] * (128 // c2), axis=1)
    f2_ref[...] = jnp.zeros_like(f2_ref)
    reach = ((0, 1), (2, -1))
    for index in range(16):
        row_kind, col_kind, sr, sc = (index >> 3) & 1, (index >> 2) & 1, (index >> 1) & 1, index & 1
        for phase in range(4):
            di = reach[row_kind][sr] - phase // 2 + 1
            dj = reach[col_kind][sc] - phase % 2 + 1
            if 0 <= di <= 2 and 0 <= dj <= 2:
                f2_ref[index * c1 : (index + 1) * c1, phase * c2 : (phase + 1) * c2] = w2_ref[
                    di, dj
                ]
    f3_ref[...] = jnp.zeros_like(f3_ref)
    order = [(row, col) for row in range(4) for col in range(2)] + [(row, 2) for row in range(4)]
    for index, (row, dj) in enumerate(order):
        for output in range(2):
            if 0 <= row - output <= 2:
                f3_ref[index * c2 : (index + 1) * c2, output * c3 : (output + 1) * c3] = w3_ref[
                    row - output, dj
                ]
    o3_ref[...] = jnp.concatenate([b3_ref[...]] * 2, axis=1)
    fourth = jnp.concatenate([w4_ref[...].astype(F32)] * 2, axis=1)
    half = lax.broadcasted_iota(jnp.int32, f4_ref.shape, 1) // c3
    output = lax.broadcasted_iota(jnp.int32, f4_ref.shape, 0)
    f4_ref[...] = jnp.where(half == output, fourth, 0.0).astype(BF)


def network_weights(w1, b1, w2, b2, w3, b3, w4, b4):
    c1, c2, c3 = w1.shape[2], w2.shape[2], w3.shape[2]
    shapes = [
        ((256, GROUP * 16 * c1), BF),
        ((1, 128), F32),
        ((16 * c1, 4 * c2), BF),
        ((1, 128), F32),
        ((12 * c2, 2 * c3), BF),
        ((1, 2 * c3), F32),
        ((16, 2 * c3), BF),
    ]
    f1, o1, f2, o2, f3, o3, f4 = pl.pallas_call(
        weights_kernel,
        out_shape=[jax.ShapeDtypeStruct(shape, dtype) for shape, dtype in shapes],
        cost_estimate=pl.CostEstimate(flops=100_000_000, bytes_accessed=4_000_000, transcendentals=0),
        compiler_params=pltpu.CompilerParams(vmem_limit_bytes=GRANT),
        name="weights",
    )(
        w1,
        b1[None],
        jnp.transpose(w2, (0, 1, 3, 2)),
        b2[None],
        jnp.transpose(w3, (0, 1, 3, 2)),
        b3[None],
        w4[None],
    )
    return (f1, o1, f2, o2, f3, o3, f4, b4)


def body(
    query_feats,
    ref_feats,
    pair_table,
    lengths,
    query_len,
    conv1_weight,
    conv1_bias,
    conv2_weight,
    conv2_bias,
    conv3_weight,
    conv3_bias,
    conv4_weight,
    conv4_bias,
):
    qry_index = lax.axis_index("qry")
    ref_index = lax.axis_index("ref")
    senders = lax.axis_size("qry")
    blocks = lax.axis_size("ref")
    frames, regions, channels = query_feats.shape
    rows = ref_feats.shape[0]
    block = frames // PHASES
    limits = (block * senders, block * blocks)
    count = rows // PIECE
    split = count >= 3 and senders == PHASES
    odd = qry_index % 2
    nearest = (qry_index + 2 * odd - 1) % senders
    entries = [qry_index, ref_index]
    for place in (qry_index, qry_index ^ 1, nearest):
        entries += [place ^ flip if split else flip for flip in range(PHASES)]
    position = jnp.stack([jnp.asarray(entry, jnp.int32) for entry in entries])
    query = jnp.transpose(query_feats, (1, 0, 2))
    own = jnp.transpose(ref_feats[:, 0], (1, 0, 2))
    chips = senders // 2
    across = [
        [(i, (i - 2 * step) % senders) for i in range(senders)] for step in range(1, chips)
    ]
    beside = [(i, i ^ 1) for i in range(senders)]

    if split:
        late = count // 2
        middle = [at for at in range(1, count - 1) if at != late]
        groups = [[0], [count - 1]] + [[at] for at in middle] + [[late]]
    else:
        groups = [list(range(count))]

    order = [at for group in groups for at in group]
    (piece,) = cut(own, order[:1])
    source, piece = lax.optimization_barrier((own, piece))
    whole = source.reshape(regions * rows, channels)
    cuts = [piece]
    if len(order) > 1:
        cuts += cut(source, order[1:])
    found = []
    for pairs in across:
        trips = []
        for piece in cuts:
            trips.append(shift(piece, "qry", pairs))
        found.append(trips)
    sibling = shift(whole, "qry", beside)
    weights = network_weights(
        conv1_weight,
        conv1_bias,
        conv2_weight,
        conv2_bias,
        conv3_weight,
        conv3_bias,
        conv4_weight,
        conv4_bias,
    )
    here, query = similarities(
        query, [whole, sibling], position, pair_table, fetch=True
    )
    sources, segments = [here], [(0, 0, rows, 0, 0), (0, rows, rows, 1, 0)]
    shard = 2
    last = []
    for pieces in found:
        pieces = list(pieces)
        for index, group in enumerate(groups):
            batch = []
            for at in group:
                piece = pieces.pop(0)
                batch += [piece, shift(piece, "qry", beside)]
            if split and index == len(groups) - 1:
                last = batch
                break
            here = similarities(query, batch, position, pair_table)[0]
            for order, at in enumerate(group):
                for half in range(2):
                    start = PIECE * (2 * order + half)
                    segments.append((len(sources), start, PIECE, shard + half, at * PIECE))
            sources.append(here)
        shard += 2
    if not split:
        tiles = [[None] * rows for _ in range(senders)]
        for source, row, size, place, cell in segments:
            for at in range(0, size, PIECE):
                tiles[place][cell + at] = sources[source][row + at : row + at + PIECE]
        tiles = [
            jnp.concatenate([part for part in parts if part is not None], axis=0)
            for parts in tiles
        ]
        sender = jnp.arange(senders, dtype=jnp.int32)
        step = (sender // 2 - qry_index // 2) % chips
        ordered = jnp.stack(tiles)[2 * step + ((sender % 2) ^ (qry_index % 2))]
        sims = ordered.reshape(senders // PHASES, PHASES, rows, frames).transpose(1, 2, 0, 3)
        sources = [sims.reshape(PHASES * block, frames)]
        segments = [(0, phase * block, block, phase, 0) for phase in range(PHASES)]

    def cells(low):
        parts = []
        for want in range(PHASES):
            for source, row, size, place, cell in segments:
                if place == want and cell <= low and low + HALO <= cell + size:
                    parts.append(sources[source][row + low - cell : row + low - cell + HALO])
        return jnp.concatenate(parts, axis=0)

    up = [(i, i + 1) for i in range(blocks - 1)]
    down = [(b, a) for a, b in up]
    right = shift(cells(0), "ref", down)
    left = shift(cells(block - HALO), "ref", up)
    for edge, cell in ((left, -HALO), (right, block)):
        segments += [(len(sources), HALO * k, HALO, k, cell) for k in range(PHASES)]
        sources.append(edge)
    jf = pad_cells(block)[0]
    ready, tiles = first_tiles(block, frames, jf, late * PIECE if split else 2 * PIECE)
    base, first = assembled(position, sources, segments, weights[:2], ready, block, limits)
    if not split:
        tiles = first_tiles(block, 0, jf, 2 * PIECE)[1]
    if split:
        for half in range(2):
            segments.append((len(sources), PIECE * half, PIECE, 2 + half, late * PIECE))
        done, core, chip = similarities(query, last, position, pair_table, sources)
        sources.append(done)
    else:
        core, chip = edge_rows(position, sources)
        done = sources[-1]
    starts = [0]
    for source in sources[:-1]:
        starts.append(starts[-1] + source.shape[0])
    pairs = [(i, (i + 1) % senders) for i in range(1, senders, 2)]
    chip = shift(chip, "qry", pairs + [(b, a) for a, b in pairs])
    core = shift(core, "qry", beside)
    score_map, peaks = network(
        position,
        lengths,
        base,
        first,
        done,
        (core, chip),
        starts,
        segments,
        tiles,
        weights,
        block,
        limits,
    )
    mine, other = peaks, shift(peaks, "qry", beside)
    peaks = jnp.where(odd == 1, jnp.stack([other, mine]), jnp.stack([mine, other]))

    def swap(array, flip_qry, flip_ref):
        pairs = [
            (q * blocks + r, (q ^ flip_qry) * blocks + (r ^ flip_ref))
            for q in range(senders)
            for r in range(blocks)
        ]
        return shift(array, ("qry", "ref"), pairs)

    bit = 1
    while bit < blocks:
        peaks = jnp.maximum(peaks, swap(peaks, 1, bit))
        bit *= 2
    first_row = (qry_index - odd) * block
    row_ids = first_row + jnp.arange(2 * block, dtype=jnp.int32).reshape(2, 1, block)
    total = jnp.sum(jnp.where(row_ids < query_len[0], peaks, 0.0), axis=(0, 2))
    bit = 2
    while bit < senders:
        total = total + swap(total, bit + 1, 0)
        bit *= 2
    return (score_map, total / query_len[0].astype(F32))


def solution(mesh):
    placed = (
        P(("groups", "qry"), None, None),
        P(("groups", "ref"), "qry", None, None),
        P("groups", None),
        P("groups"),
        P("groups"),
    ) + (P(),) * 8

    return jax.shard_map(
        body,
        mesh=mesh,
        in_specs=placed,
        out_specs=(P(("groups", "qry"), "ref"), P("groups")),
        check_vma=False,
    )
```

```python
import functools
import math

import jax
import jax.numpy as jnp
from jax import lax
from jax.experimental import pallas as pl
from jax.experimental.pallas import tpu as pltpu
from jax.sharding import PartitionSpec as P


GRANT = 20 * 1024 * 1024
PIECE = 8
PHASES = 4
HALO = 2
EDGE = 8
GROUP = 3
WINDOW = PHASES * GROUP + 2
BF = jnp.bfloat16
F32 = jnp.float32


def in_hbm(array):
    return pltpu.with_memory_space_constraint(array, pltpu.HBM)


def shift(array, axis, pairs):
    return lax.ppermute(array, axis, pairs)


def cut_kernel(order, source_ref, *refs):
    outs, sems = refs[:-1], refs[-1]
    copies = []
    for index, (at, out) in enumerate(zip(order, outs)):
        piece = source_ref.at[:, pl.ds(at * PIECE, PIECE), :]
        copies.append(pltpu.make_async_copy(piece, out, sems.at[index]))
    for copy in copies:
        copy.start()
    for copy in copies:
        copy.wait()


def cut(source, order):
    regions, _, channels = source.shape
    shape = (regions, PIECE, channels)
    pieces = pl.pallas_call(
        functools.partial(cut_kernel, order),
        in_specs=[pl.BlockSpec(memory_space=pltpu.HBM)],
        out_specs=[pl.BlockSpec(memory_space=pltpu.VMEM) for _ in order],
        out_shape=[jax.ShapeDtypeStruct(shape, source.dtype) for _ in order],
        scratch_shapes=[pltpu.SemaphoreType.DMA((len(order),))],
        compiler_params=pltpu.CompilerParams(vmem_limit_bytes=GRANT),
        cost_estimate=pl.CostEstimate(
            flops=0, bytes_accessed=4 * source.size, transcendentals=0
        ),
        name="cut",
    )(in_hbm(source))
    return [piece.reshape(regions * PIECE, channels) for piece in pieces]


def write_edges(pos_ref, arrays, core_ref, chip_ref):
    total = jnp.concatenate(arrays, axis=0)
    frames = total.shape[1]
    eights = [total[at : at + 8] for at in range(0, total.shape[0], 8)]
    first = jnp.concatenate([eight[:, 0:EDGE] for eight in eights], axis=1)
    last = jnp.concatenate([eight[:, frames - EDGE : frames] for eight in eights], axis=1)
    even = pos_ref[0] % 2 == 0
    core_ref[...] = jnp.where(even, last, first)
    chip_ref[...] = jnp.where(even, first, last)


def edge_shapes(columns):
    return [jax.ShapeDtypeStruct((8, columns // 8 * EDGE), F32)] * 2


def edges_kernel(pos_ref, *refs):
    write_edges(pos_ref, [ref[...] for ref in refs[:-2]], *refs[-2:])


def edge_rows(position, sources):
    smem = pl.BlockSpec(memory_space=pltpu.SMEM)
    vmem = pl.BlockSpec(memory_space=pltpu.VMEM)
    return pl.pallas_call(
        edges_kernel,
        in_specs=[smem] + [vmem for _ in sources],
        out_specs=[vmem, vmem],
        out_shape=edge_shapes(sum(source.shape[0] for source in sources)),
        name="edges",
    )(position, *sources)


def sims_kernel(scale, spans, others, fetch, pos_ref, table_ref, query_ref, *refs):
    pieces, refs = refs[: len(spans)], refs[len(spans) :]
    done, refs = refs[:others], refs[others:]
    out_ref = refs[0]
    if fetch:
        rows_ref, sems = refs[-2], refs[-1]
    regions, frames, channels = query_ref.shape
    width = (3 if regions % 3 == 0 else 1) if fetch else regions
    blocks = [(at, min(width, regions - at)) for at in range(0, regions, width)]
    if fetch:
        copies, arriving = [], []
        start = 0
        for index, (span, piece) in enumerate(zip(spans, pieces)):
            rows = pl.ds(start, span * regions)
            copies.append(pltpu.make_async_copy(piece, rows_ref.at[rows, :], sems.at[index]))
            start += span * regions
        for copy in copies:
            copy.start()
        for step, (at, size) in enumerate(blocks):
            block = pl.ds(at, size)
            arriving.append(
                pltpu.make_async_copy(
                    query_ref.at[block], refs[1].at[block], sems.at[len(spans) + step]
                )
            )
        for copy in arriving:
            copy.start()
        query_ref = refs[1]
        for copy in copies:
            copy.wait()

    total = None
    for step, (at, size) in enumerate(blocks):
        if fetch:
            arriving[step].wait()
        rows = (
            rows_ref[...]
            if fetch
            else jnp.concatenate([piece[...] for piece in pieces], axis=0)
        )
        products = lax.dot_general(
            rows,
            query_ref[at : at + size].reshape(-1, channels),
            (((1,), (1,)), ((), ())),
            preferred_element_type=F32,
        )
        parts = []
        start = 0
        for span in spans:
            best = products[start : start + span]
            for other in range(1, regions):
                best = jnp.maximum(
                    best, products[start + other * span : start + (other + 1) * span]
                )
            part = best[:, 0:frames]
            for other in range(1, size):
                part = part + best[:, other * frames : (other + 1) * frames]
            parts.append(part)
            start += span * regions
        part = jnp.concatenate(parts, axis=0)
        total = part if total is None else total + part
    active = table_ref[pos_ref[0], pos_ref[1]] == 1
    total = total * jnp.where(active, scale, 0.0).astype(F32)
    out_ref[...] = total
    if done:
        write_edges(pos_ref, [ref[...] for ref in done] + [total], *refs[1:3])


def similarities(query, pieces, position, table, done=(), fetch=False):
    regions, frames, channels = query.shape
    spans = [piece.shape[0] // regions for piece in pieces]
    scale = 1.0 / (regions * math.sqrt(channels))
    rows = sum(spans)
    shapes = [jax.ShapeDtypeStruct((rows, frames), F32)]
    if done:
        shapes += edge_shapes(rows + sum(array.shape[0] for array in done))
    steps = 0
    if fetch:
        shapes.append(pltpu.VMEM(query.shape, query.dtype))
        steps = regions
    smem = pl.BlockSpec(memory_space=pltpu.SMEM)
    vmem = pl.BlockSpec(memory_space=pltpu.VMEM)
    return pl.pallas_call(
        functools.partial(sims_kernel, scale, spans, len(done), fetch),
        in_specs=[smem, smem, pl.BlockSpec(memory_space=pltpu.HBM) if fetch else vmem]
        + [pl.BlockSpec(memory_space=pltpu.HBM) if fetch else vmem for _ in pieces]
        + [vmem for _ in done],
        out_specs=[vmem for _ in shapes],
        out_shape=shapes,
        scratch_shapes=[
            pltpu.VMEM((rows * regions, channels), BF),
            pltpu.SemaphoreType.DMA((len(pieces) + steps,)),
        ]
        if fetch
        else [],
        compiler_params=pltpu.CompilerParams(vmem_limit_bytes=GRANT),
        cost_estimate=pl.CostEstimate(
            flops=2 * rows * regions * regions * frames * channels,
            bytes_accessed=2 * channels * regions * rows,
            transcendentals=0,
        ),
        name="similarities",
    )(position, table, *(map(in_hbm, (query, *pieces)) if fetch else (query, *pieces)), *done)


def inside_columns(pos_ref, block, limits, count, halo):
    at = lax.broadcasted_iota(jnp.int32, (count, 128), 0) + (pos_ref[1] * block - halo)
    return jnp.where((at >= 0) & (at < limits[1]), 1.0, 0.0).astype(F32)


def inside_rows(pos_ref, block, limits, at):
    at = pos_ref[0] * block + at
    return jnp.where((at >= 0) & (at < limits[0]), 1.0, 0.0).astype(F32)


def first_map(sims_ref, w1_ref, b1_ref, y_ref, first_ref, pos_ref, block, limits, tiles):
    lanes = sims_ref.shape[2]
    sources = [(PHASES - 1, 0)] + [(phase, 1) for phase in range(PHASES)] + [(0, 2)]
    terms = len(sources) * WINDOW
    reach = PHASES * HALO + 1
    spots, start = [], 0
    for group, first, size in tiles:
        low = PHASES * GROUP * group - reach
        parts = []
        for phase, at in sources:
            base = sims_ref[phase, first + at : first + at + size, :]
            if low < 0:
                parts.append(base[:, lanes + low : lanes])
                parts.append(base[:, 0 : low + WINDOW])
            else:
                parts.append(base[:, low : low + WINDOW])
        window = jnp.concatenate(parts + [jnp.zeros((size, 128 - terms), F32)], axis=1)
        high = window.astype(BF).astype(F32)
        rest = pltpu.roll(window - high, terms, 1)
        again = pltpu.roll(high, 2 * terms - 128, 1)
        lane = lax.broadcasted_iota(jnp.int32, (size, 128), 1)
        row = slice(start, start + size)
        y_ref[row, 0:128] = jnp.where(lane < terms, high, rest).astype(BF)
        y_ref[row, 128:256] = jnp.where(lane < 2 * terms - 128, rest, again).astype(BF)
        spots.append(start)
        start += size

    keep_cols = inside_columns(pos_ref, block, limits, first_ref.shape[1], HALO)
    for member in range(GROUP):
        result = jnp.dot(
            y_ref[0:start, :],
            w1_ref[:, member * 512 : (member + 1) * 512],
            preferred_element_type=F32,
        )
        pooled = jnp.maximum(
            jnp.maximum(result[:, 0:128], result[:, 128:256]),
            jnp.maximum(result[:, 256:384], result[:, 384:512]),
        )
        pooled = jnp.maximum(pooled + b1_ref[...], 0.0)
        for (group, first, size), spot in zip(tiles, spots):
            at = group * GROUP + member
            keep = keep_cols[first : first + size] * inside_rows(
                pos_ref, block, limits, at - HALO
            )
            first_ref[at, first : first + size, :] = (
                (pooled[spot : spot + size] * keep).astype(BF).astype(F32)
            )


def first_tiles(block, frames, jf, late):
    groups = (block + 2 * HALO) // GROUP
    reach = PHASES * HALO + 1
    early, rest, whole = [], [], []
    for group in range(groups):
        low = PHASES * GROUP * group - reach
        if low >= 0 and low + WINDOW <= frames:
            early += [(group, 0, late)]
            rest += [(group, late, 2 * PIECE)]
        else:
            whole += [(group, 0, jf)]
    ends = [(group, late + 2 * PIECE, jf - late - 2 * PIECE) for group, _, _ in early]
    return early + ends, rest + whole


def convolve(sims_ref, first_ref, weights, scratch, score_ref, pos_ref, block, limits, padding, tiles):
    w1_ref, b1_ref, w2_ref, b2_ref, w3_ref, b3_ref, w4_ref, b4_ref = weights
    y_ref, lhs2_ref, second_ref, lhs3_ref = scratch
    jf, js, jt = padding
    first_map(sims_ref, w1_ref, b1_ref, y_ref, first_ref, pos_ref, block, limits, tiles)
    lane = lax.broadcasted_iota(jnp.int32, (jf, 128), 1)

    upper = lane < 64
    left = (lane // 32) % 2 == 0
    rows2 = block + 2
    for at in range(rows2):
        centre = first_ref[at + 1, 0:jf, :]
        across = jnp.where(upper, first_ref[at + 2, 0:jf, :], first_ref[at, 0:jf, :])
        row = slice(at * js, (at + 1) * js)
        for index, value in enumerate((centre, across)):
            here = pltpu.roll(value, jf - 1, 0)
            beside = jnp.where(left, pltpu.roll(value, jf - 2, 0), value)
            lhs2_ref[row, index * 256 : index * 256 + 128] = here[0:js].astype(BF)
            lhs2_ref[row, index * 256 + 128 : index * 256 + 256] = beside[0:js].astype(BF)
    result = jnp.dot(lhs2_ref[0 : rows2 * js, :], w2_ref[...], preferred_element_type=F32)
    pooled = jnp.maximum(result[:, 0:128], result[:, 128:256])
    pooled = jnp.maximum(pooled, pltpu.roll(pooled, 64, 1))
    pooled = jnp.maximum(pooled + b2_ref[...], 0.0)
    keep_cols = inside_columns(pos_ref, block, limits, js, 1)
    for at in range(rows2):
        keep = keep_cols * inside_rows(pos_ref, block, limits, at - 1)
        second_ref[at, 0:js, :] = (pooled[at * js : (at + 1) * js] * keep).astype(BF).astype(F32)
        if js < jt + 8:
            second_ref[at, js : jt + 8, :] = jnp.zeros((jt + 8 - js, 128), F32)

    upper = upper[0:jt]
    for at in range(block // 2):
        row = slice(at * jt, (at + 1) * jt)
        rows = [second_ref.at[2 * at + down] for down in range(4)]
        for down in range(4):
            pair = jnp.where(upper, rows[down][0:jt, :], rows[down][1 : 1 + jt, :])
            lhs3_ref[row, down * 128 : (down + 1) * 128] = pair.astype(BF)
        for half in range(2):
            pair = jnp.where(
                upper, rows[2 * half][2 : 2 + jt, :], rows[2 * half + 1][2 : 2 + jt, :]
            )
            lhs3_ref[row, (4 + half) * 128 : (5 + half) * 128] = pair.astype(BF)
    third = jnp.dot(lhs3_ref[...], w3_ref[...], preferred_element_type=F32)
    third = jnp.maximum(third + b3_ref[...], 0.0).astype(BF)
    flat = lax.dot_general(
        w4_ref[...], third, (((1,), (1,)), ((), ())), preferred_element_type=F32
    )
    flat = flat[0:8] + b4_ref[0]
    for at in range(block // 2):
        score_ref[2 * at : 2 * at + 2, :] = flat[0:2, at * jt : at * jt + block]


def pad_cells(cells):
    js = -(-(cells + 2) // 8) * 8
    return (max(-(-(cells + 4) // 8) * 8, js), js, -(-cells // 16) * 16)


def convolve_scratch(block, padding, tiles):
    _, js, jt = padding
    return [
        pltpu.VMEM((sum(size for _, _, size in tiles), 256), BF),
        pltpu.VMEM(((block + 2) * js, 512), BF),
        pltpu.VMEM((block + 2, max(js, jt + 8), 128), F32),
        pltpu.VMEM((block // 2 * jt, 768), BF),
    ]


def place(pos_ref, sims_ref, sources, segments):
    for source, row, size, shard, cell in segments:
        if source < len(sources):
            rows = slice(3 + cell, 3 + cell + size)
            sims_ref[pos_ref[2 + shard], rows, 0 : sources[source].shape[1]] = sources[source][
                row : row + size, :
            ]


def place_edges(pos_ref, sims_ref, starts, segments, table, edge, side):
    for source, row, size, shard, cell in segments:
        for at in range(0, size, 8):
            start = starts[source] + row + at
            count = min(8, size - at)
            lane = start // 8 * EDGE
            sims_ref[pos_ref[table + shard], 3 + cell + at : 3 + cell + at + count, side] = edge[
                start % 8 : start % 8 + count, lane : lane + EDGE
            ]


def assemble_kernel(segments, tiles, block, limits, pos_ref, *refs):
    sources, (w1_ref, b1_ref, sims_ref, first_ref, y_ref) = refs[:-5], refs[-5:]
    sims_ref[...] = jnp.zeros_like(sims_ref)
    place(pos_ref, sims_ref, sources, segments)
    first_map(sims_ref, w1_ref, b1_ref, y_ref, first_ref, pos_ref, block, limits, tiles)


def assembled(position, sources, segments, weights, tiles, block, limits):
    smem = pl.BlockSpec(memory_space=pltpu.SMEM)
    vmem = pl.BlockSpec(memory_space=pltpu.VMEM)
    frames = sources[0].shape[1]
    return pl.pallas_call(
        functools.partial(assemble_kernel, segments, tiles, block, limits),
        in_specs=[smem] + [vmem for _ in sources] + [vmem, vmem],
        out_specs=[vmem, vmem],
        out_shape=[
            jax.ShapeDtypeStruct((PHASES, block + 24, 2 * frames), F32),
            jax.ShapeDtypeStruct((block + 2 * HALO, pad_cells(block)[0], 128), F32),
        ],
        scratch_shapes=[pltpu.VMEM((sum(size for _, _, size in tiles), 256), BF)],
        compiler_params=pltpu.CompilerParams(vmem_limit_bytes=GRANT),
        cost_estimate=pl.CostEstimate(
            flops=1_000_000_000, bytes_accessed=500_000, transcendentals=0
        ),
        name="assemble",
    )(position, *sources, *weights)


def network_kernel(limits, padding, starts, segments, tiles, pos_ref, len_ref, *refs):
    (_, _, late_ref, core_ref, chip_ref), refs = refs[:5], refs[5:]
    weights, (score_ref, peak_ref, sims_ref, first_ref), scratch = refs[:8], refs[8:12], refs[12:]
    block = score_ref.shape[0]
    last = len(starts) - 1
    place(
        pos_ref, sims_ref, [late_ref], [(0, *rest) for source, *rest in segments if source == last]
    )
    lanes = sims_ref.shape[2]
    above, below = slice(lanes - EDGE, lanes), slice(lanes // 2, lanes // 2 + EDGE)

    ends = (pos_ref[0] == 0) | (pos_ref[0] == limits[0] // block - 1)
    core, chip = core_ref[...], jnp.where(ends, 0.0, chip_ref[...])

    def edges(core_side, chip_side):
        place_edges(pos_ref, sims_ref, starts, segments, 6, core, core_side)
        place_edges(pos_ref, sims_ref, starts, segments, 10, chip, chip_side)

    pl.when(pos_ref[0] % 2 == 0)(lambda: edges(below, above))
    pl.when(pos_ref[0] % 2 == 1)(lambda: edges(above, below))
    convolve(
        sims_ref, first_ref, weights, scratch, score_ref, pos_ref, block, limits, padding, tiles
    )

    score = score_ref[...]
    videos = len_ref.shape[0]
    column = pos_ref[1] * block + lax.broadcasted_iota(jnp.int32, (block, block), 1)
    slot = lax.broadcasted_iota(jnp.int32, (block, 128), 1)
    start = jnp.int32(0)
    peaks = jnp.zeros((block, 128), F32)
    for video in range(videos):
        end = start + len_ref[video]
        member = (column >= start) & (column < end)
        best = jnp.max(jnp.where(member, score, -jnp.inf), axis=1, keepdims=True)
        peaks = jnp.where(slot == video, best, peaks)
        start = end
    peak_ref[...] = jnp.transpose(peaks)[0:videos]


def network(
    position, lengths, base, first, late, edges, starts, segments, tiles, weights, block, limits
):
    smem = pl.BlockSpec(memory_space=pltpu.SMEM)
    vmem = pl.BlockSpec(memory_space=pltpu.VMEM)
    padding = pad_cells(block)
    arrays = [base, first, late, *edges]
    score, peaks, *_ = pl.pallas_call(
        functools.partial(network_kernel, limits, padding, starts, segments, tiles),
        in_specs=[smem, smem] + [vmem] * len(arrays) + [vmem] * 7 + [smem],
        out_specs=[vmem] * 4,
        out_shape=[
            jax.ShapeDtypeStruct((block, block), F32),
            jax.ShapeDtypeStruct((lengths.shape[0], block), F32),
            jax.ShapeDtypeStruct(base.shape, F32),
            jax.ShapeDtypeStruct(first.shape, F32),
        ],
        scratch_shapes=convolve_scratch(block, padding, tiles),
        input_output_aliases={2: 2, 3: 3},
        cost_estimate=pl.CostEstimate(
            flops=6_000_000_000, bytes_accessed=4_000_000, transcendentals=0
        ),
        compiler_params=pltpu.CompilerParams(vmem_limit_bytes=GRANT),
        name="network",
    )(position, lengths, *arrays, *weights)
    return score, peaks


def weights_kernel(w1_ref, b1_ref, w2_ref, b2_ref, w3_ref, b3_ref, w4_ref, *outs):
    f1_ref, o1_ref, f2_ref, o2_ref, f3_ref, o3_ref, f4_ref = outs
    c1, c2, c3 = w1_ref.shape[2], w2_ref.shape[3], w3_ref.shape[3]
    rows = lax.broadcasted_iota(jnp.int32, (256, 16 * c1), 0)
    lane = lax.broadcasted_iota(jnp.int32, (256, 16 * c1), 1) // c1
    terms = 6 * WINDOW
    third = rows >= 2 * terms
    valid = rows < 3 * terms
    rows = rows - jnp.where(third, 2 * terms, jnp.where(rows >= terms, terms, 0))
    along = jnp.zeros_like(rows)
    for offset in range(1, 6):
        along = along + jnp.where(rows >= offset * WINDOW, 1, 0)
    down = rows - along * WINDOW - 2 * ((lane // 2) % 2) - lane // 8
    along = along - 2 * (lane % 2) - (lane // 4) % 2
    taps = []
    for di in range(3):
        for dj in range(3):
            tap = jnp.concatenate([w1_ref[di, dj : dj + 1, :]] * (128 // c1), axis=1)
            taps.append(jnp.concatenate([tap] * (16 * c1 // 128), axis=1))
    for member in range(GROUP):
        dense = jnp.zeros(rows.shape, F32)
        for di in range(3):
            for dj in range(3):
                here = (down == di + PHASES * member) & (along == dj) & valid
                dense = jnp.where(here, taps[3 * di + dj], dense)
        high = dense.astype(BF).astype(F32)
        at = slice(member * 16 * c1, (member + 1) * 16 * c1)
        f1_ref[:, at] = jnp.where(third, dense - high, high).astype(BF)
    o1_ref[...] = jnp.concatenate([b1_ref[...]] * (128 // c1), axis=1)
    o2_ref[...] = jnp.concatenate([b2_ref[...]] * (128 // c2), axis=1)
    f2_ref[...] = jnp.zeros_like(f2_ref)
    reach = ((0, 1), (2, -1))
    for index in range(16):
        row_kind, col_kind, sr, sc = (index >> 3) & 1, (index >> 2) & 1, (index >> 1) & 1, index & 1
        for phase in range(4):
            di = reach[row_kind][sr] - phase // 2 + 1
            dj = reach[col_kind][sc] - phase % 2 + 1
            if 0 <= di <= 2 and 0 <= dj <= 2:
                f2_ref[index * c1 : (index + 1) * c1, phase * c2 : (phase + 1) * c2] = w2_ref[
                    di, dj
                ]
    f3_ref[...] = jnp.zeros_like(f3_ref)
    order = [(row, col) for row in range(4) for col in range(2)] + [(row, 2) for row in range(4)]
    for index, (row, dj) in enumerate(order):
        for output in range(2):
            if 0 <= row - output <= 2:
                f3_ref[index * c2 : (index + 1) * c2, output * c3 : (output + 1) * c3] = w3_ref[
                    row - output, dj
                ]
    o3_ref[...] = jnp.concatenate([b3_ref[...]] * 2, axis=1)
    fourth = jnp.concatenate([w4_ref[...].astype(F32)] * 2, axis=1)
    half = lax.broadcasted_iota(jnp.int32, f4_ref.shape, 1) // c3
    output = lax.broadcasted_iota(jnp.int32, f4_ref.shape, 0)
    f4_ref[...] = jnp.where(half == output, fourth, 0.0).astype(BF)


def network_weights(w1, b1, w2, b2, w3, b3, w4, b4):
    c1, c2, c3 = w1.shape[2], w2.shape[2], w3.shape[2]
    shapes = [
        ((256, GROUP * 16 * c1), BF),
        ((1, 128), F32),
        ((16 * c1, 4 * c2), BF),
        ((1, 128), F32),
        ((12 * c2, 2 * c3), BF),
        ((1, 2 * c3), F32),
        ((16, 2 * c3), BF),
    ]
    f1, o1, f2, o2, f3, o3, f4 = pl.pallas_call(
        weights_kernel,
        out_shape=[jax.ShapeDtypeStruct(shape, dtype) for shape, dtype in shapes],
        cost_estimate=pl.CostEstimate(flops=100_000_000, bytes_accessed=4_000_000, transcendentals=0),
        compiler_params=pltpu.CompilerParams(vmem_limit_bytes=GRANT),
        name="weights",
    )(
        w1,
        b1[None],
        jnp.transpose(w2, (0, 1, 3, 2)),
        b2[None],
        jnp.transpose(w3, (0, 1, 3, 2)),
        b3[None],
        w4[None],
    )
    return (f1, o1, f2, o2, f3, o3, f4, b4)


def body(
    query_feats,
    ref_feats,
    pair_table,
    lengths,
    query_len,
    conv1_weight,
    conv1_bias,
    conv2_weight,
    conv2_bias,
    conv3_weight,
    conv3_bias,
    conv4_weight,
    conv4_bias,
):
    qry_index = lax.axis_index("qry")
    ref_index = lax.axis_index("ref")
    senders = lax.axis_size("qry")
    blocks = lax.axis_size("ref")
    frames, regions, channels = query_feats.shape
    rows = ref_feats.shape[0]
    block = frames // PHASES
    limits = (block * senders, block * blocks)
    count = rows // PIECE
    split = count >= 3 and senders == PHASES
    odd = qry_index % 2
    nearest = (qry_index + 2 * odd - 1) % senders
    entries = [qry_index, ref_index]
    for place in (qry_index, qry_index ^ 1, nearest):
        entries += [place ^ flip if split else flip for flip in range(PHASES)]
    position = jnp.stack([jnp.asarray(entry, jnp.int32) for entry in entries])
    query = jnp.transpose(query_feats, (1, 0, 2))
    own = jnp.transpose(ref_feats[:, 0], (1, 0, 2))
    chips = senders // 2
    across = [
        [(i, (i - 2 * step) % senders) for i in range(senders)] for step in range(1, chips)
    ]
    beside = [(i, i ^ 1) for i in range(senders)]

    if split:
        late = count // 2
        middle = [at for at in range(1, count - 1) if at != late]
        groups = [[0], [count - 1]] + [[at] for at in middle] + [[late]]
    else:
        groups = [list(range(count))]

    order = [at for group in groups for at in group]
    (piece,) = cut(own, order[:1])
    source, piece = lax.optimization_barrier((own, piece))
    whole = source.reshape(regions * rows, channels)
    cuts = [piece]
    if len(order) > 1:
        cuts += cut(source, order[1:])
    found = []
    for pairs in across:
        trips = []
        for piece in cuts:
            trips.append(shift(piece, "qry", pairs))
        found.append(trips)
    sibling = shift(whole, "qry", beside)
    weights = network_weights(
        conv1_weight,
        conv1_bias,
        conv2_weight,
        conv2_bias,
        conv3_weight,
        conv3_bias,
        conv4_weight,
        conv4_bias,
    )
    here, query = similarities(
        query, [whole, sibling], position, pair_table, fetch=True
    )
    sources, segments = [here], [(0, 0, rows, 0, 0), (0, rows, rows, 1, 0)]
    shard = 2
    last = []
    for pieces in found:
        pieces = list(pieces)
        for index, group in enumerate(groups):
            batch = []
            for at in group:
                piece = pieces.pop(0)
                batch += [piece, shift(piece, "qry", beside)]
            if split and index == len(groups) - 1:
                last = batch
                break
            here = similarities(query, batch, position, pair_table)[0]
            for order, at in enumerate(group):
                for half in range(2):
                    start = PIECE * (2 * order + half)
                    segments.append((len(sources), start, PIECE, shard + half, at * PIECE))
            sources.append(here)
        shard += 2
    if not split:
        tiles = [[None] * rows for _ in range(senders)]
        for source, row, size, place, cell in segments:
            for at in range(0, size, PIECE):
                tiles[place][cell + at] = sources[source][row + at : row + at + PIECE]
        tiles = [
            jnp.concatenate([part for part in parts if part is not None], axis=0)
            for parts in tiles
        ]
        sender = jnp.arange(senders, dtype=jnp.int32)
        step = (sender // 2 - qry_index // 2) % chips
        ordered = jnp.stack(tiles)[2 * step + ((sender % 2) ^ (qry_index % 2))]
        sims = ordered.reshape(senders // PHASES, PHASES, rows, frames).transpose(1, 2, 0, 3)
        sources = [sims.reshape(PHASES * block, frames)]
        segments = [(0, phase * block, block, phase, 0) for phase in range(PHASES)]

    def cells(low):
        parts = []
        for want in range(PHASES):
            for source, row, size, place, cell in segments:
                if place == want and cell <= low and low + HALO <= cell + size:
                    parts.append(sources[source][row + low - cell : row + low - cell + HALO])
        return jnp.concatenate(parts, axis=0)

    up = [(i, i + 1) for i in range(blocks - 1)]
    down = [(b, a) for a, b in up]
    right = shift(cells(0), "ref", down)
    left = shift(cells(block - HALO), "ref", up)
    for edge, cell in ((left, -HALO), (right, block)):
        segments += [(len(sources), HALO * k, HALO, k, cell) for k in range(PHASES)]
        sources.append(edge)
    jf = pad_cells(block)[0]
    ready, tiles = first_tiles(block, frames, jf, late * PIECE if split else 2 * PIECE)
    base, first = assembled(position, sources, segments, weights[:2], ready, block, limits)
    if not split:
        tiles = first_tiles(block, 0, jf, 2 * PIECE)[1]
    if split:
        for half in range(2):
            segments.append((len(sources), PIECE * half, PIECE, 2 + half, late * PIECE))
        done, core, chip = similarities(query, last, position, pair_table, sources)
        sources.append(done)
    else:
        core, chip = edge_rows(position, sources)
        done = sources[-1]
    starts = [0]
    for source in sources[:-1]:
        starts.append(starts[-1] + source.shape[0])
    pairs = [(i, (i + 1) % senders) for i in range(1, senders, 2)]
    chip = shift(chip, "qry", pairs + [(b, a) for a, b in pairs])
    core = shift(core, "qry", beside)
    score_map, peaks = network(
        position,
        lengths,
        base,
        first,
        done,
        (core, chip),
        starts,
        segments,
        tiles,
        weights,
        block,
        limits,
    )
    mine, other = peaks, shift(peaks, "qry", beside)
    peaks = jnp.where(odd == 1, jnp.stack([other, mine]), jnp.stack([mine, other]))

    def swap(array, flip_qry, flip_ref):
        pairs = [
            (q * blocks + r, (q ^ flip_qry) * blocks + (r ^ flip_ref))
            for q in range(senders)
            for r in range(blocks)
        ]
        return shift(array, ("qry", "ref"), pairs)

    bit = 1
    while bit < blocks:
        peaks = jnp.maximum(peaks, swap(peaks, 1, bit))
        bit *= 2
    first_row = (qry_index - odd) * block
    row_ids = first_row + jnp.arange(2 * block, dtype=jnp.int32).reshape(2, 1, block)
    total = jnp.sum(jnp.where(row_ids < query_len[0], peaks, 0.0), axis=(0, 2))
    bit = 2
    while bit < senders:
        total = total + swap(total, bit + 1, 0)
        bit *= 2
    return (score_map, total / query_len[0].astype(F32))


def solution(mesh):
    placed = (
        P(("groups", "qry"), None, None),
        P(("groups", "ref"), "qry", None, None),
        P("groups", None),
        P("groups"),
        P("groups"),
    ) + (P(),) * 8

    return jax.shard_map(
        body,
        mesh=mesh,
        in_specs=placed,
        out_specs=(P(("groups", "qry"), "ref"), P("groups")),
        check_vma=False,
    )
```

```python
import functools
import math

import jax
import jax.numpy as jnp
from jax import lax
from jax.experimental import pallas as pl
from jax.experimental.pallas import tpu as pltpu
from jax.sharding import PartitionSpec as P


GRANT = 20 * 1024 * 1024
PIECE = 8
PHASES = 4
HALO = 2
EDGE = 8
GROUP = 3
WINDOW = PHASES * GROUP + 2
BF = jnp.bfloat16
F32 = jnp.float32


def in_hbm(array):
    return pltpu.with_memory_space_constraint(array, pltpu.HBM)


def shift(array, axis, pairs):
    return lax.ppermute(array, axis, pairs)


def cut_kernel(order, source_ref, *refs):
    outs, sems = refs[:-1], refs[-1]
    copies = []
    for index, (at, out) in enumerate(zip(order, outs)):
        piece = source_ref.at[:, pl.ds(at * PIECE, PIECE), :]
        copies.append(pltpu.make_async_copy(piece, out, sems.at[index]))
    for copy in copies:
        copy.start()
    for copy in copies:
        copy.wait()


def cut(source, order):
    regions, _, channels = source.shape
    shape = (regions, PIECE, channels)
    pieces = pl.pallas_call(
        functools.partial(cut_kernel, order),
        in_specs=[pl.BlockSpec(memory_space=pltpu.HBM)],
        out_specs=[pl.BlockSpec(memory_space=pltpu.VMEM) for _ in order],
        out_shape=[jax.ShapeDtypeStruct(shape, source.dtype) for _ in order],
        scratch_shapes=[pltpu.SemaphoreType.DMA((len(order),))],
        compiler_params=pltpu.CompilerParams(vmem_limit_bytes=GRANT),
        cost_estimate=pl.CostEstimate(
            flops=0, bytes_accessed=4 * source.size, transcendentals=0
        ),
        name="cut",
    )(in_hbm(source))
    return [piece.reshape(regions * PIECE, channels) for piece in pieces]


def write_edges(pos_ref, arrays, core_ref, chip_ref):
    total = jnp.concatenate(arrays, axis=0)
    frames = total.shape[1]
    eights = [total[at : at + 8] for at in range(0, total.shape[0], 8)]
    first = jnp.concatenate([eight[:, 0:EDGE] for eight in eights], axis=1)
    last = jnp.concatenate([eight[:, frames - EDGE : frames] for eight in eights], axis=1)
    even = pos_ref[0] % 2 == 0
    core_ref[...] = jnp.where(even, last, first)
    chip_ref[...] = jnp.where(even, first, last)


def edge_shapes(columns):
    return [jax.ShapeDtypeStruct((8, columns // 8 * EDGE), F32)] * 2


def edges_kernel(pos_ref, *refs):
    write_edges(pos_ref, [ref[...] for ref in refs[:-2]], *refs[-2:])


def edge_rows(position, sources):
    smem = pl.BlockSpec(memory_space=pltpu.SMEM)
    vmem = pl.BlockSpec(memory_space=pltpu.VMEM)
    return pl.pallas_call(
        edges_kernel,
        in_specs=[smem] + [vmem for _ in sources],
        out_specs=[vmem, vmem],
        out_shape=edge_shapes(sum(source.shape[0] for source in sources)),
        name="edges",
    )(position, *sources)


def sims_kernel(scale, spans, others, fetch, pos_ref, table_ref, query_ref, *refs):
    pieces, refs = refs[: len(spans)], refs[len(spans) :]
    done, refs = refs[:others], refs[others:]
    out_ref = refs[0]
    if fetch:
        rows_ref, sems = refs[-2], refs[-1]
    regions, frames, channels = query_ref.shape
    width = 3 if regions % 3 == 0 else 1
    if fetch:
        copies, arriving = [], []
        start = 0
        for index, (span, piece) in enumerate(zip(spans, pieces)):
            rows = pl.ds(start, span * regions)
            copies.append(pltpu.make_async_copy(piece, rows_ref.at[rows, :], sems.at[index]))
            start += span * regions
        for copy in copies:
            copy.start()
        for step in range(regions // width):
            block = pl.ds(step * width, width)
            arriving.append(
                pltpu.make_async_copy(
                    query_ref.at[block], refs[1].at[block], sems.at[len(spans) + step]
                )
            )
        for copy in arriving:
            copy.start()
        query_ref = refs[1]
        for copy in copies:
            copy.wait()

    total = None
    for step in range(regions // width):
        if fetch:
            arriving[step].wait()
        rows = (
            rows_ref[...]
            if fetch
            else jnp.concatenate([piece[...] for piece in pieces], axis=0)
        )
        products = lax.dot_general(
            rows,
            query_ref[step * width : (step + 1) * width].reshape(-1, channels),
            (((1,), (1,)), ((), ())),
            preferred_element_type=F32,
        )
        parts = []
        start = 0
        for span in spans:
            best = products[start : start + span]
            for other in range(1, regions):
                best = jnp.maximum(
                    best, products[start + other * span : start + (other + 1) * span]
                )
            part = best[:, 0:frames]
            for other in range(1, width):
                part = part + best[:, other * frames : (other + 1) * frames]
            parts.append(part)
            start += span * regions
        part = jnp.concatenate(parts, axis=0)
        total = part if total is None else total + part
    active = table_ref[pos_ref[0], pos_ref[1]] == 1
    total = total * jnp.where(active, scale, 0.0).astype(F32)
    out_ref[...] = total
    if done:
        write_edges(pos_ref, [ref[...] for ref in done] + [total], *refs[1:3])


def similarities(query, pieces, position, table, done=(), fetch=False):
    regions, frames, channels = query.shape
    spans = [piece.shape[0] // regions for piece in pieces]
    scale = 1.0 / (regions * math.sqrt(channels))
    rows = sum(spans)
    shapes = [jax.ShapeDtypeStruct((rows, frames), F32)]
    if done:
        shapes += edge_shapes(rows + sum(array.shape[0] for array in done))
    steps = 0
    if fetch:
        shapes.append(pltpu.VMEM(query.shape, query.dtype))
        steps = regions
    smem = pl.BlockSpec(memory_space=pltpu.SMEM)
    vmem = pl.BlockSpec(memory_space=pltpu.VMEM)
    return pl.pallas_call(
        functools.partial(sims_kernel, scale, spans, len(done), fetch),
        in_specs=[smem, smem, pl.BlockSpec(memory_space=pltpu.HBM) if fetch else vmem]
        + [pl.BlockSpec(memory_space=pltpu.HBM) if fetch else vmem for _ in pieces]
        + [vmem for _ in done],
        out_specs=[vmem for _ in shapes],
        out_shape=shapes,
        scratch_shapes=[
            pltpu.VMEM((rows * regions, channels), BF),
            pltpu.SemaphoreType.DMA((len(pieces) + steps,)),
        ]
        if fetch
        else [],
        compiler_params=pltpu.CompilerParams(vmem_limit_bytes=GRANT),
        cost_estimate=pl.CostEstimate(
            flops=2 * rows * regions * regions * frames * channels,
            bytes_accessed=2 * channels * regions * rows,
            transcendentals=0,
        ),
        name="similarities",
    )(position, table, *(map(in_hbm, (query, *pieces)) if fetch else (query, *pieces)), *done)


def inside_columns(pos_ref, block, limits, count, halo):
    at = lax.broadcasted_iota(jnp.int32, (count, 128), 0) + (pos_ref[1] * block - halo)
    return jnp.where((at >= 0) & (at < limits[1]), 1.0, 0.0).astype(F32)


def inside_rows(pos_ref, block, limits, at):
    at = pos_ref[0] * block + at
    return jnp.where((at >= 0) & (at < limits[0]), 1.0, 0.0).astype(F32)


def first_map(sims_ref, w1_ref, b1_ref, y_ref, first_ref, pos_ref, block, limits, tiles):
    lanes = sims_ref.shape[2]
    sources = [(PHASES - 1, 0)] + [(phase, 1) for phase in range(PHASES)] + [(0, 2)]
    terms = len(sources) * WINDOW
    reach = PHASES * HALO + 1
    spots, start = [], 0
    for group, first, size in tiles:
        low = PHASES * GROUP * group - reach
        parts = []
        for phase, at in sources:
            base = sims_ref[phase, first + at : first + at + size, :]
            if low < 0:
                parts.append(base[:, lanes + low : lanes])
                parts.append(base[:, 0 : low + WINDOW])
            else:
                parts.append(base[:, low : low + WINDOW])
        window = jnp.concatenate(parts + [jnp.zeros((size, 128 - terms), F32)], axis=1)
        high = window.astype(BF).astype(F32)
        rest = pltpu.roll(window - high, terms, 1)
        again = pltpu.roll(high, 2 * terms - 128, 1)
        lane = lax.broadcasted_iota(jnp.int32, (size, 128), 1)
        row = slice(start, start + size)
        y_ref[row, 0:128] = jnp.where(lane < terms, high, rest).astype(BF)
        y_ref[row, 128:256] = jnp.where(lane < 2 * terms - 128, rest, again).astype(BF)
        spots.append(start)
        start += size

    keep_cols = inside_columns(pos_ref, block, limits, first_ref.shape[1], HALO)
    for member in range(GROUP):
        result = jnp.dot(
            y_ref[0:start, :],
            w1_ref[:, member * 512 : (member + 1) * 512],
            preferred_element_type=F32,
        )
        pooled = jnp.maximum(
            jnp.maximum(result[:, 0:128], result[:, 128:256]),
            jnp.maximum(result[:, 256:384], result[:, 384:512]),
        )
        pooled = jnp.maximum(pooled + b1_ref[...], 0.0)
        for (group, first, size), spot in zip(tiles, spots):
            at = group * GROUP + member
            keep = keep_cols[first : first + size] * inside_rows(
                pos_ref, block, limits, at - HALO
            )
            first_ref[at, first : first + size, :] = (
                (pooled[spot : spot + size] * keep).astype(BF).astype(F32)
            )


def first_tiles(block, frames, jf, late):
    groups = (block + 2 * HALO) // GROUP
    reach = PHASES * HALO + 1
    early, rest, whole = [], [], []
    for group in range(groups):
        low = PHASES * GROUP * group - reach
        if low >= 0 and low + WINDOW <= frames:
            early += [(group, 0, late)]
            rest += [(group, late, 2 * PIECE)]
        else:
            whole += [(group, 0, jf)]
    ends = [(group, late + 2 * PIECE, jf - late - 2 * PIECE) for group, _, _ in early]
    return early + ends, rest + whole


def second_map(first_ref, w2_ref, b2_ref, lhs_ref, second_ref, pos_ref, block, limits, tiles):
    jf = first_ref.shape[1]
    lane = lax.broadcasted_iota(jnp.int32, (jf, 128), 1)
    upper = lane < 64
    left = (lane // 32) % 2 == 0
    start, spots = 0, []
    for at, first, size in tiles:
        centre = first_ref[at + 1]
        across = jnp.where(upper, first_ref[at + 2], first_ref[at])
        row, cells = slice(start, start + size), slice(first, first + size)
        for index, value in enumerate((centre, across)):
            here = pltpu.roll(value, jf - 1, 0)
            beside = jnp.where(left, pltpu.roll(value, jf - 2, 0), value)
            lhs_ref[row, index * 256 : index * 256 + 128] = here[cells].astype(BF)
            lhs_ref[row, index * 256 + 128 : index * 256 + 256] = beside[cells].astype(BF)
        spots.append(start)
        start += size
    result = jnp.dot(lhs_ref[0:start, :], w2_ref[...], preferred_element_type=F32)
    pooled = jnp.maximum(result[:, 0:128], result[:, 128:256])
    pooled = jnp.maximum(pooled, pltpu.roll(pooled, 64, 1))
    pooled = jnp.maximum(pooled + b2_ref[...], 0.0)
    keep_cols = inside_columns(pos_ref, block, limits, second_ref.shape[1], 1)
    for (at, first, size), spot in zip(tiles, spots):
        cells = slice(first, first + size)
        keep = keep_cols[cells] * inside_rows(pos_ref, block, limits, at - 1)
        second_ref[at, cells, :] = (pooled[spot : spot + size] * keep).astype(BF).astype(F32)


def second_tiles(block, js, late, split):
    early, rest, whole = [], [], []
    for at in range(block + 2):
        if split and GROUP <= at < block + 2 - GROUP:
            early += [(at, 0, late - PIECE), (at, late + 2 * PIECE, js - late - 2 * PIECE)]
            rest += [(at, late - PIECE, 3 * PIECE)]
        else:
            whole += [(at, 0, js)]
    return early, rest + whole


def convolve(
    sims_ref, maps, weights, scratch, score_ref, pos_ref, block, limits, padding, tiles
):
    w1_ref, b1_ref, w2_ref, b2_ref, w3_ref, b3_ref, w4_ref, b4_ref = weights
    first_ref, second_ref = maps
    y_ref, lhs2_ref, lhs3_ref = scratch
    _, _, jt = padding
    first_map(sims_ref, w1_ref, b1_ref, y_ref, first_ref, pos_ref, block, limits, tiles[0])
    second_map(first_ref, w2_ref, b2_ref, lhs2_ref, second_ref, pos_ref, block, limits, tiles[1])

    upper = lax.broadcasted_iota(jnp.int32, (jt, 128), 1) < 64
    for at in range(block // 2):
        row = slice(at * jt, (at + 1) * jt)
        rows = [second_ref.at[2 * at + down] for down in range(4)]
        for down in range(4):
            pair = jnp.where(upper, rows[down][0:jt, :], rows[down][1 : 1 + jt, :])
            lhs3_ref[row, down * 128 : (down + 1) * 128] = pair.astype(BF)
        for half in range(2):
            pair = jnp.where(
                upper, rows[2 * half][2 : 2 + jt, :], rows[2 * half + 1][2 : 2 + jt, :]
            )
            lhs3_ref[row, (4 + half) * 128 : (5 + half) * 128] = pair.astype(BF)
    third = jnp.dot(lhs3_ref[...], w3_ref[...], preferred_element_type=F32)
    third = jnp.maximum(third + b3_ref[...], 0.0).astype(BF)
    flat = lax.dot_general(
        w4_ref[...], third, (((1,), (1,)), ((), ())), preferred_element_type=F32
    )
    flat = flat[0:8] + b4_ref[0]
    for at in range(block // 2):
        score_ref[2 * at : 2 * at + 2, :] = flat[0:2, at * jt : at * jt + block]


def pad_cells(cells):
    js = -(-(cells + 2) // 8) * 8
    return (max(-(-(cells + 4) // 8) * 8, js), js, -(-cells // 16) * 16)


def convolve_scratch(block, padding, tiles):
    _, _, jt = padding
    return [
        pltpu.VMEM((sum(size for _, _, size in tiles[0]), 256), BF),
        pltpu.VMEM((sum(size for _, _, size in tiles[1]), 512), BF),
        pltpu.VMEM((block // 2 * jt, 768), BF),
    ]


def place(pos_ref, sims_ref, sources, segments):
    for source, row, size, shard, cell in segments:
        if source < len(sources):
            rows = slice(3 + cell, 3 + cell + size)
            sims_ref[pos_ref[2 + shard], rows, 0 : sources[source].shape[1]] = sources[source][
                row : row + size, :
            ]


def place_edges(pos_ref, sims_ref, starts, segments, table, edge, side):
    for source, row, size, shard, cell in segments:
        for at in range(0, size, 8):
            start = starts[source] + row + at
            count = min(8, size - at)
            lane = start // 8 * EDGE
            sims_ref[pos_ref[table + shard], 3 + cell + at : 3 + cell + at + count, side] = edge[
                start % 8 : start % 8 + count, lane : lane + EDGE
            ]


def assemble_kernel(segments, tiles, block, limits, pos_ref, *refs):
    sources, refs = refs[:-9], refs[-9:]
    w1_ref, b1_ref, w2_ref, b2_ref, sims_ref, first_ref, second_ref, y_ref, lhs_ref = refs
    sims_ref[...] = jnp.zeros_like(sims_ref)
    place(pos_ref, sims_ref, sources, segments)
    first_map(sims_ref, w1_ref, b1_ref, y_ref, first_ref, pos_ref, block, limits, tiles[0])
    if tiles[1]:
        second_map(first_ref, w2_ref, b2_ref, lhs_ref, second_ref, pos_ref, block, limits, tiles[1])


def assembled(position, sources, segments, weights, tiles, block, limits):
    smem = pl.BlockSpec(memory_space=pltpu.SMEM)
    vmem = pl.BlockSpec(memory_space=pltpu.VMEM)
    frames = sources[0].shape[1]
    jf, js, jt = pad_cells(block)
    return pl.pallas_call(
        functools.partial(assemble_kernel, segments, tiles, block, limits),
        in_specs=[smem] + [vmem for _ in sources] + [vmem] * 4,
        out_specs=[vmem] * 3,
        out_shape=[
            jax.ShapeDtypeStruct((PHASES, block + 24, 2 * frames), F32),
            jax.ShapeDtypeStruct((block + 2 * HALO, jf, 128), F32),
            jax.ShapeDtypeStruct((block + 2, max(js, jt + 8), 128), F32),
        ],
        scratch_shapes=[
            pltpu.VMEM((max(8, sum(size for _, _, size in part)), lanes), BF)
            for part, lanes in zip(tiles, (256, 512))
        ],
        compiler_params=pltpu.CompilerParams(vmem_limit_bytes=GRANT),
        cost_estimate=pl.CostEstimate(
            flops=1_000_000_000, bytes_accessed=500_000, transcendentals=0
        ),
        name="assemble",
    )(position, *sources, *weights)


def network_kernel(limits, padding, starts, segments, tiles, pos_ref, len_ref, *refs):
    (_, _, _, late_ref, core_ref, chip_ref), refs = refs[:6], refs[6:]
    weights, outs, scratch = refs[:8], refs[8:13], refs[13:]
    score_ref, peak_ref, sims_ref, *maps = outs
    block = score_ref.shape[0]
    last = len(starts) - 1
    place(
        pos_ref, sims_ref, [late_ref], [(0, *rest) for source, *rest in segments if source == last]
    )
    lanes = sims_ref.shape[2]
    above, below = slice(lanes - EDGE, lanes), slice(lanes // 2, lanes // 2 + EDGE)

    ends = (pos_ref[0] == 0) | (pos_ref[0] == limits[0] // block - 1)
    core, chip = core_ref[...], jnp.where(ends, 0.0, chip_ref[...])

    def edges(core_side, chip_side):
        place_edges(pos_ref, sims_ref, starts, segments, 6, core, core_side)
        place_edges(pos_ref, sims_ref, starts, segments, 10, chip, chip_side)

    pl.when(pos_ref[0] % 2 == 0)(lambda: edges(below, above))
    pl.when(pos_ref[0] % 2 == 1)(lambda: edges(above, below))
    convolve(
        sims_ref, maps, weights, scratch, score_ref, pos_ref, block, limits, padding, tiles
    )

    score = score_ref[...]
    videos = len_ref.shape[0]
    column = pos_ref[1] * block + lax.broadcasted_iota(jnp.int32, (block, block), 1)
    slot = lax.broadcasted_iota(jnp.int32, (block, 128), 1)
    start = jnp.int32(0)
    peaks = jnp.zeros((block, 128), F32)
    for video in range(videos):
        end = start + len_ref[video]
        member = (column >= start) & (column < end)
        best = jnp.max(jnp.where(member, score, -jnp.inf), axis=1, keepdims=True)
        peaks = jnp.where(slot == video, best, peaks)
        start = end
    peak_ref[...] = jnp.transpose(peaks)[0:videos]


def network(
    position, lengths, maps, late, edges, starts, segments, tiles, weights, block, limits
):
    smem = pl.BlockSpec(memory_space=pltpu.SMEM)
    vmem = pl.BlockSpec(memory_space=pltpu.VMEM)
    padding = pad_cells(block)
    arrays = [*maps, late, *edges]
    score, peaks, *_ = pl.pallas_call(
        functools.partial(network_kernel, limits, padding, starts, segments, tiles),
        in_specs=[smem, smem] + [vmem] * len(arrays) + [vmem] * 7 + [smem],
        out_specs=[vmem] * 5,
        out_shape=[
            jax.ShapeDtypeStruct((block, block), F32),
            jax.ShapeDtypeStruct((lengths.shape[0], block), F32),
            *[jax.ShapeDtypeStruct(array.shape, F32) for array in maps],
        ],
        scratch_shapes=convolve_scratch(block, padding, tiles),
        input_output_aliases={2: 2, 3: 3, 4: 4},
        cost_estimate=pl.CostEstimate(
            flops=6_000_000_000, bytes_accessed=4_000_000, transcendentals=0
        ),
        compiler_params=pltpu.CompilerParams(vmem_limit_bytes=GRANT),
        name="network",
    )(position, lengths, *arrays, *weights)
    return score, peaks


def weights_kernel(w1_ref, b1_ref, w2_ref, b2_ref, w3_ref, b3_ref, w4_ref, *outs):
    f1_ref, o1_ref, f2_ref, o2_ref, f3_ref, o3_ref, f4_ref = outs
    c1, c2, c3 = w1_ref.shape[2], w2_ref.shape[3], w3_ref.shape[3]
    rows = lax.broadcasted_iota(jnp.int32, (256, 16 * c1), 0)
    lane = lax.broadcasted_iota(jnp.int32, (256, 16 * c1), 1) // c1
    terms = 6 * WINDOW
    third = rows >= 2 * terms
    valid = rows < 3 * terms
    rows = rows - jnp.where(third, 2 * terms, jnp.where(rows >= terms, terms, 0))
    along = jnp.zeros_like(rows)
    for offset in range(1, 6):
        along = along + jnp.where(rows >= offset * WINDOW, 1, 0)
    down = rows - along * WINDOW - 2 * ((lane // 2) % 2) - lane // 8
    along = along - 2 * (lane % 2) - (lane // 4) % 2
    taps = []
    for di in range(3):
        for dj in range(3):
            tap = jnp.concatenate([w1_ref[di, dj : dj + 1, :]] * (128 // c1), axis=1)
            taps.append(jnp.concatenate([tap] * (16 * c1 // 128), axis=1))
    for member in range(GROUP):
        dense = jnp.zeros(rows.shape, F32)
        for di in range(3):
            for dj in range(3):
                here = (down == di + PHASES * member) & (along == dj) & valid
                dense = jnp.where(here, taps[3 * di + dj], dense)
        high = dense.astype(BF).astype(F32)
        at = slice(member * 16 * c1, (member + 1) * 16 * c1)
        f1_ref[:, at] = jnp.where(third, dense - high, high).astype(BF)
    o1_ref[...] = jnp.concatenate([b1_ref[...]] * (128 // c1), axis=1)
    o2_ref[...] = jnp.concatenate([b2_ref[...]] * (128 // c2), axis=1)
    f2_ref[...] = jnp.zeros_like(f2_ref)
    reach = ((0, 1), (2, -1))
    for index in range(16):
        row_kind, col_kind, sr, sc = (index >> 3) & 1, (index >> 2) & 1, (index >> 1) & 1, index & 1
        for phase in range(4):
            di = reach[row_kind][sr] - phase // 2 + 1
            dj = reach[col_kind][sc] - phase % 2 + 1
            if 0 <= di <= 2 and 0 <= dj <= 2:
                f2_ref[index * c1 : (index + 1) * c1, phase * c2 : (phase + 1) * c2] = w2_ref[
                    di, dj
                ]
    f3_ref[...] = jnp.zeros_like(f3_ref)
    order = [(row, col) for row in range(4) for col in range(2)] + [(row, 2) for row in range(4)]
    for index, (row, dj) in enumerate(order):
        for output in range(2):
            if 0 <= row - output <= 2:
                f3_ref[index * c2 : (index + 1) * c2, output * c3 : (output + 1) * c3] = w3_ref[
                    row - output, dj
                ]
    o3_ref[...] = jnp.concatenate([b3_ref[...]] * 2, axis=1)
    fourth = jnp.concatenate([w4_ref[...].astype(F32)] * 2, axis=1)
    half = lax.broadcasted_iota(jnp.int32, f4_ref.shape, 1) // c3
    output = lax.broadcasted_iota(jnp.int32, f4_ref.shape, 0)
    f4_ref[...] = jnp.where(half == output, fourth, 0.0).astype(BF)


def network_weights(w1, b1, w2, b2, w3, b3, w4, b4):
    c1, c2, c3 = w1.shape[2], w2.shape[2], w3.shape[2]
    shapes = [
        ((256, GROUP * 16 * c1), BF),
        ((1, 128), F32),
        ((16 * c1, 4 * c2), BF),
        ((1, 128), F32),
        ((12 * c2, 2 * c3), BF),
        ((1, 2 * c3), F32),
        ((16, 2 * c3), BF),
    ]
    f1, o1, f2, o2, f3, o3, f4 = pl.pallas_call(
        weights_kernel,
        out_shape=[jax.ShapeDtypeStruct(shape, dtype) for shape, dtype in shapes],
        cost_estimate=pl.CostEstimate(flops=100_000_000, bytes_accessed=4_000_000, transcendentals=0),
        compiler_params=pltpu.CompilerParams(vmem_limit_bytes=GRANT),
        name="weights",
    )(
        w1,
        b1[None],
        jnp.transpose(w2, (0, 1, 3, 2)),
        b2[None],
        jnp.transpose(w3, (0, 1, 3, 2)),
        b3[None],
        w4[None],
    )
    return (f1, o1, f2, o2, f3, o3, f4, b4)


def body(
    query_feats,
    ref_feats,
    pair_table,
    lengths,
    query_len,
    conv1_weight,
    conv1_bias,
    conv2_weight,
    conv2_bias,
    conv3_weight,
    conv3_bias,
    conv4_weight,
    conv4_bias,
):
    qry_index = lax.axis_index("qry")
    ref_index = lax.axis_index("ref")
    senders = lax.axis_size("qry")
    blocks = lax.axis_size("ref")
    frames, regions, channels = query_feats.shape
    rows = ref_feats.shape[0]
    block = frames // PHASES
    limits = (block * senders, block * blocks)
    count = rows // PIECE
    split = count >= 3 and senders == PHASES
    odd = qry_index % 2
    nearest = (qry_index + 2 * odd - 1) % senders
    entries = [qry_index, ref_index]
    for place in (qry_index, qry_index ^ 1, nearest):
        entries += [place ^ flip if split else flip for flip in range(PHASES)]
    position = jnp.stack([jnp.asarray(entry, jnp.int32) for entry in entries])
    query = jnp.transpose(query_feats, (1, 0, 2))
    own = jnp.transpose(ref_feats[:, 0], (1, 0, 2))
    chips = senders // 2
    across = [
        [(i, (i - 2 * step) % senders) for i in range(senders)] for step in range(1, chips)
    ]
    beside = [(i, i ^ 1) for i in range(senders)]

    if split:
        late = count // 2
        middle = [at for at in range(1, count - 1) if at != late]
        groups = [[0], [count - 1]] + [[at] for at in middle] + [[late]]
    else:
        groups = [list(range(count))]

    order = [at for group in groups for at in group]
    (piece,) = cut(own, order[:1])
    source, piece = lax.optimization_barrier((own, piece))
    whole = source.reshape(regions * rows, channels)
    cuts = [piece]
    if len(order) > 1:
        cuts += cut(source, order[1:])
    found = []
    for pairs in across:
        trips = []
        for piece in cuts:
            trips.append(shift(piece, "qry", pairs))
        found.append(trips)
    sibling = shift(whole, "qry", beside)
    weights = network_weights(
        conv1_weight,
        conv1_bias,
        conv2_weight,
        conv2_bias,
        conv3_weight,
        conv3_bias,
        conv4_weight,
        conv4_bias,
    )
    here, query = similarities(
        query, [whole, sibling], position, pair_table, fetch=True
    )
    sources, segments = [here], [(0, 0, rows, 0, 0), (0, rows, rows, 1, 0)]
    shard = 2
    last = []
    for pieces in found:
        pieces = list(pieces)
        for index, group in enumerate(groups):
            batch = []
            for at in group:
                piece = pieces.pop(0)
                batch += [piece, shift(piece, "qry", beside)]
            if split and index == len(groups) - 1:
                last = batch
                break
            here = similarities(query, batch, position, pair_table)[0]
            for order, at in enumerate(group):
                for half in range(2):
                    start = PIECE * (2 * order + half)
                    segments.append((len(sources), start, PIECE, shard + half, at * PIECE))
            sources.append(here)
        shard += 2
    if not split:
        tiles = [[None] * rows for _ in range(senders)]
        for source, row, size, place, cell in segments:
            for at in range(0, size, PIECE):
                tiles[place][cell + at] = sources[source][row + at : row + at + PIECE]
        tiles = [
            jnp.concatenate([part for part in parts if part is not None], axis=0)
            for parts in tiles
        ]
        sender = jnp.arange(senders, dtype=jnp.int32)
        step = (sender // 2 - qry_index // 2) % chips
        ordered = jnp.stack(tiles)[2 * step + ((sender % 2) ^ (qry_index % 2))]
        sims = ordered.reshape(senders // PHASES, PHASES, rows, frames).transpose(1, 2, 0, 3)
        sources = [sims.reshape(PHASES * block, frames)]
        segments = [(0, phase * block, block, phase, 0) for phase in range(PHASES)]

    def cells(low):
        parts = []
        for want in range(PHASES):
            for source, row, size, place, cell in segments:
                if place == want and cell <= low and low + HALO <= cell + size:
                    parts.append(sources[source][row + low - cell : row + low - cell + HALO])
        return jnp.concatenate(parts, axis=0)

    up = [(i, i + 1) for i in range(blocks - 1)]
    down = [(b, a) for a, b in up]
    right = shift(cells(0), "ref", down)
    left = shift(cells(block - HALO), "ref", up)
    for edge, cell in ((left, -HALO), (right, block)):
        segments += [(len(sources), HALO * k, HALO, k, cell) for k in range(PHASES)]
        sources.append(edge)
    jf, js, _ = pad_cells(block)
    spot = late * PIECE if split else 2 * PIECE
    firsts = first_tiles(block, frames, jf, spot)
    seconds = second_tiles(block, js, spot, split)
    maps = assembled(
        position, sources, segments, weights[:4], (firsts[0], seconds[0]), block, limits
    )
    if not split:
        firsts = first_tiles(block, 0, jf, spot)
    tiles = (firsts[1], seconds[1])
    if split:
        for half in range(2):
            segments.append((len(sources), PIECE * half, PIECE, 2 + half, late * PIECE))
        done, core, chip = similarities(query, last, position, pair_table, sources)
        sources.append(done)
    else:
        core, chip = edge_rows(position, sources)
        done = sources[-1]
    starts = [0]
    for source in sources[:-1]:
        starts.append(starts[-1] + source.shape[0])
    pairs = [(i, (i + 1) % senders) for i in range(1, senders, 2)]
    chip = shift(chip, "qry", pairs + [(b, a) for a, b in pairs])
    core = shift(core, "qry", beside)
    score_map, peaks = network(
        position,
        lengths,
        maps,
        done,
        (core, chip),
        starts,
        segments,
        tiles,
        weights,
        block,
        limits,
    )
    mine, other = peaks, shift(peaks, "qry", beside)
    peaks = jnp.where(odd == 1, jnp.stack([other, mine]), jnp.stack([mine, other]))

    def swap(array, flip_qry, flip_ref):
        pairs = [
            (q * blocks + r, (q ^ flip_qry) * blocks + (r ^ flip_ref))
            for q in range(senders)
            for r in range(blocks)
        ]
        return shift(array, ("qry", "ref"), pairs)

    bit = 1
    while bit < blocks:
        peaks = jnp.maximum(peaks, swap(peaks, 1, bit))
        bit *= 2
    first_row = (qry_index - odd) * block
    row_ids = first_row + jnp.arange(2 * block, dtype=jnp.int32).reshape(2, 1, block)
    total = jnp.sum(jnp.where(row_ids < query_len[0], peaks, 0.0), axis=(0, 2))
    bit = 2
    while bit < senders:
        total = total + swap(total, bit + 1, 0)
        bit *= 2
    return (score_map, total / query_len[0].astype(F32))


def solution(mesh):
    placed = (
        P(("groups", "qry"), None, None),
        P(("groups", "ref"), "qry", None, None),
        P("groups", None),
        P("groups"),
        P("groups"),
    ) + (P(),) * 8

    return jax.shard_map(
        body,
        mesh=mesh,
        in_specs=placed,
        out_specs=(P(("groups", "qry"), "ref"), P("groups")),
        check_vma=False,
    )
```

```python
import functools
import math

import jax
import jax.numpy as jnp
from jax import lax
from jax.experimental import pallas as pl
from jax.experimental.pallas import tpu as pltpu
from jax.sharding import PartitionSpec as P


GRANT = 20 * 1024 * 1024
PIECE = 8
PHASES = 4
HALO = 2
EDGE = 8
GROUP = 3
WINDOW = PHASES * GROUP + 2
BF = jnp.bfloat16
F32 = jnp.float32


def in_hbm(array):
    return pltpu.with_memory_space_constraint(array, pltpu.HBM)


def shift(array, axis, pairs):
    return lax.ppermute(array, axis, pairs)


def cut_kernel(order, source_ref, *refs):
    outs, sems = refs[:-1], refs[-1]
    copies = []
    for at, out in zip(order, outs):
        for region in range(source_ref.shape[0]):
            piece = source_ref.at[region, pl.ds(at * PIECE, PIECE), :]
            copies.append(pltpu.make_async_copy(piece, out.at[region], sems.at[len(copies)]))
    for copy in copies:
        copy.start()
    for copy in copies:
        copy.wait()


def cut(source, order):
    regions, _, channels = source.shape
    shape = (regions, PIECE, channels)
    pieces = pl.pallas_call(
        functools.partial(cut_kernel, order),
        in_specs=[pl.BlockSpec(memory_space=pltpu.HBM)],
        out_specs=[pl.BlockSpec(memory_space=pltpu.VMEM) for _ in order],
        out_shape=[jax.ShapeDtypeStruct(shape, source.dtype) for _ in order],
        scratch_shapes=[pltpu.SemaphoreType.DMA((len(order) * regions,))],
        compiler_params=pltpu.CompilerParams(vmem_limit_bytes=GRANT),
        cost_estimate=pl.CostEstimate(
            flops=0, bytes_accessed=4 * source.size, transcendentals=0
        ),
        name="cut",
    )(in_hbm(source))
    return [piece.reshape(regions * PIECE, channels) for piece in pieces]


def write_edges(pos_ref, arrays, core_ref, chip_ref):
    total = jnp.concatenate(arrays, axis=0)
    frames = total.shape[1]
    eights = [total[at : at + 8] for at in range(0, total.shape[0], 8)]
    first = jnp.concatenate([eight[:, 0:EDGE] for eight in eights], axis=1)
    last = jnp.concatenate([eight[:, frames - EDGE : frames] for eight in eights], axis=1)
    even = pos_ref[0] % 2 == 0
    core_ref[...] = jnp.where(even, last, first)
    chip_ref[...] = jnp.where(even, first, last)


def edge_shapes(columns):
    return [jax.ShapeDtypeStruct((8, columns // 8 * EDGE), F32)] * 2


def edges_kernel(pos_ref, *refs):
    write_edges(pos_ref, [ref[...] for ref in refs[:-2]], *refs[-2:])


def edge_rows(position, sources):
    smem = pl.BlockSpec(memory_space=pltpu.SMEM)
    vmem = pl.BlockSpec(memory_space=pltpu.VMEM)
    return pl.pallas_call(
        edges_kernel,
        in_specs=[smem] + [vmem for _ in sources],
        out_specs=[vmem, vmem],
        out_shape=edge_shapes(sum(source.shape[0] for source in sources)),
        name="edges",
    )(position, *sources)


def sims_kernel(scale, spans, others, fetch, pos_ref, table_ref, query_ref, *refs):
    pieces, refs = refs[: len(spans)], refs[len(spans) :]
    done, refs = refs[:others], refs[others:]
    out_ref = refs[0]
    if fetch:
        rows_ref, sems = refs[-2], refs[-1]
    regions, frames, channels = query_ref.shape
    width = 3 if regions % 3 == 0 else 1
    if fetch:
        copies, arriving = [], []
        start = 0
        for index, (span, piece) in enumerate(zip(spans, pieces)):
            rows = pl.ds(start, span * regions)
            copies.append(pltpu.make_async_copy(piece, rows_ref.at[rows, :], sems.at[index]))
            start += span * regions
        for copy in copies:
            copy.start()
        for step in range(regions // width):
            block = pl.ds(step * width, width)
            arriving.append(
                pltpu.make_async_copy(
                    query_ref.at[block], refs[1].at[block], sems.at[len(spans) + step]
                )
            )
        for copy in arriving:
            copy.start()
        query_ref = refs[1]
        for copy in copies:
            copy.wait()

    total = None
    for step in range(regions // width):
        if fetch:
            arriving[step].wait()
        rows = (
            rows_ref[...]
            if fetch
            else jnp.concatenate([piece[...] for piece in pieces], axis=0)
        )
        products = lax.dot_general(
            rows,
            query_ref[step * width : (step + 1) * width].reshape(-1, channels),
            (((1,), (1,)), ((), ())),
            preferred_element_type=F32,
        )
        parts = []
        start = 0
        for span in spans:
            best = products[start : start + span]
            for other in range(1, regions):
                best = jnp.maximum(
                    best, products[start + other * span : start + (other + 1) * span]
                )
            part = best[:, 0:frames]
            for other in range(1, width):
                part = part + best[:, other * frames : (other + 1) * frames]
            parts.append(part)
            start += span * regions
        part = jnp.concatenate(parts, axis=0)
        total = part if total is None else total + part
    active = table_ref[pos_ref[0], pos_ref[1]] == 1
    total = total * jnp.where(active, scale, 0.0).astype(F32)
    out_ref[...] = total
    if done:
        write_edges(pos_ref, [ref[...] for ref in done] + [total], *refs[1:3])


def similarities(query, pieces, position, table, done=(), fetch=False):
    regions, frames, channels = query.shape
    spans = [piece.shape[0] // regions for piece in pieces]
    scale = 1.0 / (regions * math.sqrt(channels))
    rows = sum(spans)
    shapes = [jax.ShapeDtypeStruct((rows, frames), F32)]
    if done:
        shapes += edge_shapes(rows + sum(array.shape[0] for array in done))
    steps = 0
    if fetch:
        shapes.append(pltpu.VMEM(query.shape, query.dtype))
        steps = regions
    smem = pl.BlockSpec(memory_space=pltpu.SMEM)
    vmem = pl.BlockSpec(memory_space=pltpu.VMEM)
    return pl.pallas_call(
        functools.partial(sims_kernel, scale, spans, len(done), fetch),
        in_specs=[smem, smem, pl.BlockSpec(memory_space=pltpu.HBM) if fetch else vmem]
        + [pl.BlockSpec(memory_space=pltpu.HBM) if fetch else vmem for _ in pieces]
        + [vmem for _ in done],
        out_specs=[vmem for _ in shapes],
        out_shape=shapes,
        scratch_shapes=[
            pltpu.VMEM((rows * regions, channels), BF),
            pltpu.SemaphoreType.DMA((len(pieces) + steps,)),
        ]
        if fetch
        else [],
        compiler_params=pltpu.CompilerParams(vmem_limit_bytes=GRANT),
        cost_estimate=pl.CostEstimate(
            flops=2 * rows * regions * regions * frames * channels,
            bytes_accessed=2 * channels * regions * rows,
            transcendentals=0,
        ),
        name="similarities",
    )(position, table, *(map(in_hbm, (query, *pieces)) if fetch else (query, *pieces)), *done)


def inside_columns(pos_ref, block, limits, count, halo):
    at = lax.broadcasted_iota(jnp.int32, (count, 128), 0) + (pos_ref[1] * block - halo)
    return jnp.where((at >= 0) & (at < limits[1]), 1.0, 0.0).astype(F32)


def inside_rows(pos_ref, block, limits, at):
    at = pos_ref[0] * block + at
    return jnp.where((at >= 0) & (at < limits[0]), 1.0, 0.0).astype(F32)


def first_map(sims_ref, w1_ref, b1_ref, y_ref, first_ref, pos_ref, block, limits, tiles):
    lanes = sims_ref.shape[2]
    sources = [(PHASES - 1, 0)] + [(phase, 1) for phase in range(PHASES)] + [(0, 2)]
    terms = len(sources) * WINDOW
    reach = PHASES * HALO + 1
    spots, start = [], 0
    for group, first, size in tiles:
        low = PHASES * GROUP * group - reach
        parts = []
        for phase, at in sources:
            base = sims_ref[phase, first + at : first + at + size, :]
            if low < 0:
                parts.append(base[:, lanes + low : lanes])
                parts.append(base[:, 0 : low + WINDOW])
            else:
                parts.append(base[:, low : low + WINDOW])
        window = jnp.concatenate(parts + [jnp.zeros((size, 128 - terms), F32)], axis=1)
        high = window.astype(BF).astype(F32)
        rest = pltpu.roll(window - high, terms, 1)
        again = pltpu.roll(high, 2 * terms - 128, 1)
        lane = lax.broadcasted_iota(jnp.int32, (size, 128), 1)
        row = slice(start, start + size)
        y_ref[row, 0:128] = jnp.where(lane < terms, high, rest).astype(BF)
        y_ref[row, 128:256] = jnp.where(lane < 2 * terms - 128, rest, again).astype(BF)
        spots.append(start)
        start += size

    keep_cols = inside_columns(pos_ref, block, limits, first_ref.shape[1], HALO)
    for member in range(GROUP):
        result = jnp.dot(
            y_ref[0:start, :],
            w1_ref[:, member * 512 : (member + 1) * 512],
            preferred_element_type=F32,
        )
        pooled = jnp.maximum(
            jnp.maximum(result[:, 0:128], result[:, 128:256]),
            jnp.maximum(result[:, 256:384], result[:, 384:512]),
        )
        pooled = jnp.maximum(pooled + b1_ref[...], 0.0)
        for (group, first, size), spot in zip(tiles, spots):
            at = group * GROUP + member
            keep = keep_cols[first : first + size] * inside_rows(
                pos_ref, block, limits, at - HALO
            )
            first_ref[at, first : first + size, :] = (
                (pooled[spot : spot + size] * keep).astype(BF).astype(F32)
            )


def first_tiles(block, frames, jf, late):
    groups = (block + 2 * HALO) // GROUP
    reach = PHASES * HALO + 1
    early, rest, whole = [], [], []
    for group in range(groups):
        low = PHASES * GROUP * group - reach
        if low >= 0 and low + WINDOW <= frames:
            early += [(group, 0, late)]
            rest += [(group, late, 2 * PIECE)]
        else:
            whole += [(group, 0, jf)]
    ends = [(group, late + 2 * PIECE, jf - late - 2 * PIECE) for group, _, _ in early]
    return early + ends, rest + whole


def second_map(first_ref, w2_ref, b2_ref, lhs_ref, second_ref, pos_ref, block, limits, tiles):
    jf = first_ref.shape[1]
    lane = lax.broadcasted_iota(jnp.int32, (jf, 128), 1)
    upper = lane < 64
    left = (lane // 32) % 2 == 0
    start, spots = 0, []
    for at, first, size in tiles:
        centre = first_ref[at + 1]
        across = jnp.where(upper, first_ref[at + 2], first_ref[at])
        row, cells = slice(start, start + size), slice(first, first + size)
        for index, value in enumerate((centre, across)):
            here = pltpu.roll(value, jf - 1, 0)
            beside = jnp.where(left, pltpu.roll(value, jf - 2, 0), value)
            lhs_ref[row, index * 256 : index * 256 + 128] = here[cells].astype(BF)
            lhs_ref[row, index * 256 + 128 : index * 256 + 256] = beside[cells].astype(BF)
        spots.append(start)
        start += size
    result = jnp.dot(lhs_ref[0:start, :], w2_ref[...], preferred_element_type=F32)
    pooled = jnp.maximum(result[:, 0:128], result[:, 128:256])
    pooled = jnp.maximum(pooled, pltpu.roll(pooled, 64, 1))
    pooled = jnp.maximum(pooled + b2_ref[...], 0.0)
    keep_cols = inside_columns(pos_ref, block, limits, second_ref.shape[1], 1)
    for (at, first, size), spot in zip(tiles, spots):
        cells = slice(first, first + size)
        keep = keep_cols[cells] * inside_rows(pos_ref, block, limits, at - 1)
        second_ref[at, cells, :] = (pooled[spot : spot + size] * keep).astype(BF).astype(F32)


def second_tiles(block, js, late, split):
    early, rest, whole = [], [], []
    for at in range(block + 2):
        if split and GROUP <= at < block + 2 - GROUP:
            early += [(at, 0, late - PIECE), (at, late + 2 * PIECE, js - late - 2 * PIECE)]
            rest += [(at, late - PIECE, 3 * PIECE)]
        else:
            whole += [(at, 0, js)]
    return early, rest + whole


def convolve(
    sims_ref, maps, weights, scratch, score_ref, pos_ref, block, limits, padding, tiles
):
    w1_ref, b1_ref, w2_ref, b2_ref, w3_ref, b3_ref, w4_ref, b4_ref = weights
    first_ref, second_ref = maps
    y_ref, lhs2_ref, lhs3_ref = scratch
    _, _, jt = padding
    first_map(sims_ref, w1_ref, b1_ref, y_ref, first_ref, pos_ref, block, limits, tiles[0])
    second_map(first_ref, w2_ref, b2_ref, lhs2_ref, second_ref, pos_ref, block, limits, tiles[1])

    upper = lax.broadcasted_iota(jnp.int32, (jt, 128), 1) < 64
    for at in range(block // 2):
        row = slice(at * jt, (at + 1) * jt)
        rows = [second_ref.at[2 * at + down] for down in range(4)]
        for down in range(4):
            pair = jnp.where(upper, rows[down][0:jt, :], rows[down][1 : 1 + jt, :])
            lhs3_ref[row, down * 128 : (down + 1) * 128] = pair.astype(BF)
        for half in range(2):
            pair = jnp.where(
                upper, rows[2 * half][2 : 2 + jt, :], rows[2 * half + 1][2 : 2 + jt, :]
            )
            lhs3_ref[row, (4 + half) * 128 : (5 + half) * 128] = pair.astype(BF)
    third = jnp.dot(lhs3_ref[...], w3_ref[...], preferred_element_type=F32)
    third = jnp.maximum(third + b3_ref[...], 0.0).astype(BF)
    flat = lax.dot_general(
        w4_ref[...], third, (((1,), (1,)), ((), ())), preferred_element_type=F32
    )
    flat = flat[0:8] + b4_ref[0]
    for at in range(block // 2):
        score_ref[2 * at : 2 * at + 2, :] = flat[0:2, at * jt : at * jt + block]


def pad_cells(cells):
    js = -(-(cells + 2) // 8) * 8
    return (max(-(-(cells + 4) // 8) * 8, js), js, -(-cells // 16) * 16)


def convolve_scratch(block, padding, tiles):
    _, _, jt = padding
    return [
        pltpu.VMEM((sum(size for _, _, size in tiles[0]), 256), BF),
        pltpu.VMEM((sum(size for _, _, size in tiles[1]), 512), BF),
        pltpu.VMEM((block // 2 * jt, 768), BF),
    ]


def place(pos_ref, sims_ref, sources, segments):
    for source, row, size, shard, cell in segments:
        if source < len(sources):
            rows = slice(3 + cell, 3 + cell + size)
            sims_ref[pos_ref[2 + shard], rows, 0 : sources[source].shape[1]] = sources[source][
                row : row + size, :
            ]


def place_edges(pos_ref, sims_ref, starts, segments, table, edge, side):
    for source, row, size, shard, cell in segments:
        for at in range(0, size, 8):
            start = starts[source] + row + at
            count = min(8, size - at)
            lane = start // 8 * EDGE
            sims_ref[pos_ref[table + shard], 3 + cell + at : 3 + cell + at + count, side] = edge[
                start % 8 : start % 8 + count, lane : lane + EDGE
            ]


def assemble_kernel(segments, tiles, block, limits, pos_ref, *refs):
    sources, refs = refs[:-9], refs[-9:]
    w1_ref, b1_ref, w2_ref, b2_ref, sims_ref, first_ref, second_ref, y_ref, lhs_ref = refs
    sims_ref[...] = jnp.zeros_like(sims_ref)
    place(pos_ref, sims_ref, sources, segments)
    first_map(sims_ref, w1_ref, b1_ref, y_ref, first_ref, pos_ref, block, limits, tiles[0])
    if tiles[1]:
        second_map(first_ref, w2_ref, b2_ref, lhs_ref, second_ref, pos_ref, block, limits, tiles[1])


def assembled(position, sources, segments, weights, tiles, block, limits):
    smem = pl.BlockSpec(memory_space=pltpu.SMEM)
    vmem = pl.BlockSpec(memory_space=pltpu.VMEM)
    frames = sources[0].shape[1]
    jf, js, jt = pad_cells(block)
    return pl.pallas_call(
        functools.partial(assemble_kernel, segments, tiles, block, limits),
        in_specs=[smem] + [vmem for _ in sources] + [vmem] * 4,
        out_specs=[vmem] * 3,
        out_shape=[
            jax.ShapeDtypeStruct((PHASES, block + 24, 2 * frames), F32),
            jax.ShapeDtypeStruct((block + 2 * HALO, jf, 128), F32),
            jax.ShapeDtypeStruct((block + 2, max(js, jt + 8), 128), F32),
        ],
        scratch_shapes=[
            pltpu.VMEM((max(8, sum(size for _, _, size in part)), lanes), BF)
            for part, lanes in zip(tiles, (256, 512))
        ],
        compiler_params=pltpu.CompilerParams(vmem_limit_bytes=GRANT),
        cost_estimate=pl.CostEstimate(
            flops=1_000_000_000, bytes_accessed=500_000, transcendentals=0
        ),
        name="assemble",
    )(position, *sources, *weights)


def network_kernel(limits, padding, starts, segments, tiles, pos_ref, len_ref, *refs):
    (_, _, _, late_ref, core_ref, chip_ref), refs = refs[:6], refs[6:]
    weights, outs, scratch = refs[:8], refs[8:13], refs[13:]
    score_ref, peak_ref, sims_ref, *maps = outs
    block = score_ref.shape[0]
    last = len(starts) - 1
    place(
        pos_ref, sims_ref, [late_ref], [(0, *rest) for source, *rest in segments if source == last]
    )
    lanes = sims_ref.shape[2]
    above, below = slice(lanes - EDGE, lanes), slice(lanes // 2, lanes // 2 + EDGE)

    ends = (pos_ref[0] == 0) | (pos_ref[0] == limits[0] // block - 1)
    core, chip = core_ref[...], jnp.where(ends, 0.0, chip_ref[...])

    def edges(core_side, chip_side):
        place_edges(pos_ref, sims_ref, starts, segments, 6, core, core_side)
        place_edges(pos_ref, sims_ref, starts, segments, 10, chip, chip_side)

    pl.when(pos_ref[0] % 2 == 0)(lambda: edges(below, above))
    pl.when(pos_ref[0] % 2 == 1)(lambda: edges(above, below))
    convolve(
        sims_ref, maps, weights, scratch, score_ref, pos_ref, block, limits, padding, tiles
    )

    score = score_ref[...]
    videos = len_ref.shape[0]
    column = pos_ref[1] * block + lax.broadcasted_iota(jnp.int32, (block, block), 1)
    slot = lax.broadcasted_iota(jnp.int32, (block, 128), 1)
    start = jnp.int32(0)
    peaks = jnp.zeros((block, 128), F32)
    for video in range(videos):
        end = start + len_ref[video]
        member = (column >= start) & (column < end)
        best = jnp.max(jnp.where(member, score, -jnp.inf), axis=1, keepdims=True)
        peaks = jnp.where(slot == video, best, peaks)
        start = end
    peak_ref[...] = jnp.transpose(peaks)[0:videos]


def network(
    position, lengths, maps, late, edges, starts, segments, tiles, weights, block, limits
):
    smem = pl.BlockSpec(memory_space=pltpu.SMEM)
    vmem = pl.BlockSpec(memory_space=pltpu.VMEM)
    padding = pad_cells(block)
    arrays = [*maps, late, *edges]
    score, peaks, *_ = pl.pallas_call(
        functools.partial(network_kernel, limits, padding, starts, segments, tiles),
        in_specs=[smem, smem] + [vmem] * len(arrays) + [vmem] * 7 + [smem],
        out_specs=[vmem] * 5,
        out_shape=[
            jax.ShapeDtypeStruct((block, block), F32),
            jax.ShapeDtypeStruct((lengths.shape[0], block), F32),
            *[jax.ShapeDtypeStruct(array.shape, F32) for array in maps],
        ],
        scratch_shapes=convolve_scratch(block, padding, tiles),
        input_output_aliases={2: 2, 3: 3, 4: 4},
        cost_estimate=pl.CostEstimate(
            flops=6_000_000_000, bytes_accessed=4_000_000, transcendentals=0
        ),
        compiler_params=pltpu.CompilerParams(vmem_limit_bytes=GRANT),
        name="network",
    )(position, lengths, *arrays, *weights)
    return score, peaks


def weights_kernel(w1_ref, b1_ref, w2_ref, b2_ref, w3_ref, b3_ref, w4_ref, *outs):
    f1_ref, o1_ref, f2_ref, o2_ref, f3_ref, o3_ref, f4_ref = outs
    c1, c2, c3 = w1_ref.shape[2], w2_ref.shape[3], w3_ref.shape[3]
    rows = lax.broadcasted_iota(jnp.int32, (256, 16 * c1), 0)
    lane = lax.broadcasted_iota(jnp.int32, (256, 16 * c1), 1) // c1
    terms = 6 * WINDOW
    third = rows >= 2 * terms
    valid = rows < 3 * terms
    rows = rows - jnp.where(third, 2 * terms, jnp.where(rows >= terms, terms, 0))
    along = jnp.zeros_like(rows)
    for offset in range(1, 6):
        along = along + jnp.where(rows >= offset * WINDOW, 1, 0)
    down = rows - along * WINDOW - 2 * ((lane // 2) % 2) - lane // 8
    along = along - 2 * (lane % 2) - (lane // 4) % 2
    taps = []
    for di in range(3):
        for dj in range(3):
            tap = jnp.concatenate([w1_ref[di, dj : dj + 1, :]] * (128 // c1), axis=1)
            taps.append(jnp.concatenate([tap] * (16 * c1 // 128), axis=1))
    for member in range(GROUP):
        dense = jnp.zeros(rows.shape, F32)
        for di in range(3):
            for dj in range(3):
                here = (down == di + PHASES * member) & (along == dj) & valid
                dense = jnp.where(here, taps[3 * di + dj], dense)
        high = dense.astype(BF).astype(F32)
        at = slice(member * 16 * c1, (member + 1) * 16 * c1)
        f1_ref[:, at] = jnp.where(third, dense - high, high).astype(BF)
    o1_ref[...] = jnp.concatenate([b1_ref[...]] * (128 // c1), axis=1)
    o2_ref[...] = jnp.concatenate([b2_ref[...]] * (128 // c2), axis=1)
    f2_ref[...] = jnp.zeros_like(f2_ref)
    reach = ((0, 1), (2, -1))
    for index in range(16):
        row_kind, col_kind, sr, sc = (index >> 3) & 1, (index >> 2) & 1, (index >> 1) & 1, index & 1
        for phase in range(4):
            di = reach[row_kind][sr] - phase // 2 + 1
            dj = reach[col_kind][sc] - phase % 2 + 1
            if 0 <= di <= 2 and 0 <= dj <= 2:
                f2_ref[index * c1 : (index + 1) * c1, phase * c2 : (phase + 1) * c2] = w2_ref[
                    di, dj
                ]
    f3_ref[...] = jnp.zeros_like(f3_ref)
    order = [(row, col) for row in range(4) for col in range(2)] + [(row, 2) for row in range(4)]
    for index, (row, dj) in enumerate(order):
        for output in range(2):
            if 0 <= row - output <= 2:
                f3_ref[index * c2 : (index + 1) * c2, output * c3 : (output + 1) * c3] = w3_ref[
                    row - output, dj
                ]
    o3_ref[...] = jnp.concatenate([b3_ref[...]] * 2, axis=1)
    fourth = jnp.concatenate([w4_ref[...].astype(F32)] * 2, axis=1)
    half = lax.broadcasted_iota(jnp.int32, f4_ref.shape, 1) // c3
    output = lax.broadcasted_iota(jnp.int32, f4_ref.shape, 0)
    f4_ref[...] = jnp.where(half == output, fourth, 0.0).astype(BF)


def network_weights(w1, b1, w2, b2, w3, b3, w4, b4):
    c1, c2, c3 = w1.shape[2], w2.shape[2], w3.shape[2]
    shapes = [
        ((256, GROUP * 16 * c1), BF),
        ((1, 128), F32),
        ((16 * c1, 4 * c2), BF),
        ((1, 128), F32),
        ((12 * c2, 2 * c3), BF),
        ((1, 2 * c3), F32),
        ((16, 2 * c3), BF),
    ]
    f1, o1, f2, o2, f3, o3, f4 = pl.pallas_call(
        weights_kernel,
        out_shape=[jax.ShapeDtypeStruct(shape, dtype) for shape, dtype in shapes],
        cost_estimate=pl.CostEstimate(flops=100_000_000, bytes_accessed=4_000_000, transcendentals=0),
        compiler_params=pltpu.CompilerParams(vmem_limit_bytes=GRANT),
        name="weights",
    )(
        w1,
        b1[None],
        jnp.transpose(w2, (0, 1, 3, 2)),
        b2[None],
        jnp.transpose(w3, (0, 1, 3, 2)),
        b3[None],
        w4[None],
    )
    return (f1, o1, f2, o2, f3, o3, f4, b4)


def body(
    query_feats,
    ref_feats,
    pair_table,
    lengths,
    query_len,
    conv1_weight,
    conv1_bias,
    conv2_weight,
    conv2_bias,
    conv3_weight,
    conv3_bias,
    conv4_weight,
    conv4_bias,
):
    qry_index = lax.axis_index("qry")
    ref_index = lax.axis_index("ref")
    senders = lax.axis_size("qry")
    blocks = lax.axis_size("ref")
    frames, regions, channels = query_feats.shape
    rows = ref_feats.shape[0]
    block = frames // PHASES
    limits = (block * senders, block * blocks)
    count = rows // PIECE
    split = count >= 3 and senders == PHASES
    odd = qry_index % 2
    nearest = (qry_index + 2 * odd - 1) % senders
    entries = [qry_index, ref_index]
    for place in (qry_index, qry_index ^ 1, nearest):
        entries += [place ^ flip if split else flip for flip in range(PHASES)]
    position = jnp.stack([jnp.asarray(entry, jnp.int32) for entry in entries])
    query = jnp.transpose(query_feats, (1, 0, 2))
    own = jnp.transpose(ref_feats[:, 0], (1, 0, 2))
    chips = senders // 2
    across = [
        [(i, (i - 2 * step) % senders) for i in range(senders)] for step in range(1, chips)
    ]
    beside = [(i, i ^ 1) for i in range(senders)]

    if split:
        late = count // 2
        middle = [at for at in range(1, count - 1) if at != late]
        groups = [[0], [count - 1]] + [[at] for at in middle] + [[late]]
    else:
        groups = [list(range(count))]

    order = [at for group in groups for at in group]
    (piece,) = cut(own, order[:1])
    source, piece = lax.optimization_barrier((own, piece))
    whole = source.reshape(regions * rows, channels)
    cuts = [piece]
    if len(order) > 1:
        cuts += cut(source, order[1:])
    found = []
    for pairs in across:
        trips = []
        for piece in cuts:
            trips.append(shift(piece, "qry", pairs))
        found.append(trips)
    sibling = shift(whole, "qry", beside)
    weights = network_weights(
        conv1_weight,
        conv1_bias,
        conv2_weight,
        conv2_bias,
        conv3_weight,
        conv3_bias,
        conv4_weight,
        conv4_bias,
    )
    here, query = similarities(
        query, [whole, sibling], position, pair_table, fetch=True
    )
    sources, segments = [here], [(0, 0, rows, 0, 0), (0, rows, rows, 1, 0)]
    shard = 2
    last = []
    for pieces in found:
        pieces = list(pieces)
        for index, group in enumerate(groups):
            batch = []
            for at in group:
                piece = pieces.pop(0)
                batch += [piece, shift(piece, "qry", beside)]
            if split and index == len(groups) - 1:
                last = batch
                break
            here = similarities(query, batch, position, pair_table)[0]
            for order, at in enumerate(group):
                for half in range(2):
                    start = PIECE * (2 * order + half)
                    segments.append((len(sources), start, PIECE, shard + half, at * PIECE))
            sources.append(here)
        shard += 2
    if not split:
        tiles = [[None] * rows for _ in range(senders)]
        for source, row, size, place, cell in segments:
            for at in range(0, size, PIECE):
                tiles[place][cell + at] = sources[source][row + at : row + at + PIECE]
        tiles = [
            jnp.concatenate([part for part in parts if part is not None], axis=0)
            for parts in tiles
        ]
        sender = jnp.arange(senders, dtype=jnp.int32)
        step = (sender // 2 - qry_index // 2) % chips
        ordered = jnp.stack(tiles)[2 * step + ((sender % 2) ^ (qry_index % 2))]
        sims = ordered.reshape(senders // PHASES, PHASES, rows, frames).transpose(1, 2, 0, 3)
        sources = [sims.reshape(PHASES * block, frames)]
        segments = [(0, phase * block, block, phase, 0) for phase in range(PHASES)]

    def cells(low):
        parts = []
        for want in range(PHASES):
            for source, row, size, place, cell in segments:
                if place == want and cell <= low and low + HALO <= cell + size:
                    parts.append(sources[source][row + low - cell : row + low - cell + HALO])
        return jnp.concatenate(parts, axis=0)

    up = [(i, i + 1) for i in range(blocks - 1)]
    down = [(b, a) for a, b in up]
    right = shift(cells(0), "ref", down)
    left = shift(cells(block - HALO), "ref", up)
    for edge, cell in ((left, -HALO), (right, block)):
        segments += [(len(sources), HALO * k, HALO, k, cell) for k in range(PHASES)]
        sources.append(edge)
    jf, js, _ = pad_cells(block)
    spot = late * PIECE if split else 2 * PIECE
    firsts = first_tiles(block, frames, jf, spot)
    seconds = second_tiles(block, js, spot, split)
    maps = assembled(
        position, sources, segments, weights[:4], (firsts[0], seconds[0]), block, limits
    )
    if not split:
        firsts = first_tiles(block, 0, jf, spot)
    tiles = (firsts[1], seconds[1])
    if split:
        for half in range(2):
            segments.append((len(sources), PIECE * half, PIECE, 2 + half, late * PIECE))
        done, core, chip = similarities(query, last, position, pair_table, sources)
        sources.append(done)
    else:
        core, chip = edge_rows(position, sources)
        done = sources[-1]
    starts = [0]
    for source in sources[:-1]:
        starts.append(starts[-1] + source.shape[0])
    pairs = [(i, (i + 1) % senders) for i in range(1, senders, 2)]
    chip = shift(chip, "qry", pairs + [(b, a) for a, b in pairs])
    core = shift(core, "qry", beside)
    score_map, peaks = network(
        position,
        lengths,
        maps,
        done,
        (core, chip),
        starts,
        segments,
        tiles,
        weights,
        block,
        limits,
    )
    mine, other = peaks, shift(peaks, "qry", beside)
    peaks = jnp.where(odd == 1, jnp.stack([other, mine]), jnp.stack([mine, other]))

    def swap(array, flip_qry, flip_ref):
        pairs = [
            (q * blocks + r, (q ^ flip_qry) * blocks + (r ^ flip_ref))
            for q in range(senders)
            for r in range(blocks)
        ]
        return shift(array, ("qry", "ref"), pairs)

    bit = 1
    while bit < blocks:
        peaks = jnp.maximum(peaks, swap(peaks, 1, bit))
        bit *= 2
    first_row = (qry_index - odd) * block
    row_ids = first_row + jnp.arange(2 * block, dtype=jnp.int32).reshape(2, 1, block)
    total = jnp.sum(jnp.where(row_ids < query_len[0], peaks, 0.0), axis=(0, 2))
    bit = 2
    while bit < senders:
        total = total + swap(total, bit + 1, 0)
        bit *= 2
    return (score_map, total / query_len[0].astype(F32))


def solution(mesh):
    placed = (
        P(("groups", "qry"), None, None),
        P(("groups", "ref"), "qry", None, None),
        P("groups", None),
        P("groups"),
        P("groups"),
    ) + (P(),) * 8

    return jax.shard_map(
        body,
        mesh=mesh,
        in_specs=placed,
        out_specs=(P(("groups", "qry"), "ref"), P("groups")),
        check_vma=False,
    )
```

```python
import functools
import math

import jax
import jax.numpy as jnp
from jax import lax
from jax.experimental import pallas as pl
from jax.experimental.pallas import tpu as pltpu
from jax.sharding import PartitionSpec as P


GRANT = 20 * 1024 * 1024
PIECE = 8
PHASES = 4
HALO = 2
EDGE = 8
GROUP = 3
WINDOW = PHASES * GROUP + 2
BF = jnp.bfloat16
F32 = jnp.float32


def in_hbm(array):
    return pltpu.with_memory_space_constraint(array, pltpu.HBM)


def shift(array, axis, pairs):
    return lax.ppermute(array, axis, pairs)


def cut_kernel(order, source_ref, *refs):
    outs, sems = refs[:-1], refs[-1]
    copies = []
    for index, (at, out) in enumerate(zip(order, outs)):
        piece = source_ref.at[:, pl.ds(at * PIECE, PIECE), :]
        copies.append(pltpu.make_async_copy(piece, out, sems.at[index]))
    for copy in copies:
        copy.start()
    for copy in copies:
        copy.wait()


def cut(source, order):
    regions, _, channels = source.shape
    shape = (regions, PIECE, channels)
    pieces = pl.pallas_call(
        functools.partial(cut_kernel, order),
        in_specs=[pl.BlockSpec(memory_space=pltpu.HBM)],
        out_specs=[pl.BlockSpec(memory_space=pltpu.VMEM) for _ in order],
        out_shape=[jax.ShapeDtypeStruct(shape, source.dtype) for _ in order],
        scratch_shapes=[pltpu.SemaphoreType.DMA((len(order),))],
        compiler_params=pltpu.CompilerParams(vmem_limit_bytes=GRANT),
        cost_estimate=pl.CostEstimate(
            flops=0, bytes_accessed=4 * source.size, transcendentals=0
        ),
        name="cut",
    )(in_hbm(source))
    return [piece.reshape(regions * PIECE, channels) for piece in pieces]


def write_edges(pos_ref, arrays, core_ref, chip_ref, ready=None):
    total = jnp.concatenate(arrays, axis=0)
    frames = total.shape[1]
    eights = [total[at : at + 8] for at in range(0, total.shape[0], 8)]
    first = jnp.concatenate([eight[:, 0:EDGE] for eight in eights], axis=1)
    last = jnp.concatenate([eight[:, frames - EDGE : frames] for eight in eights], axis=1)
    even = pos_ref[0] % 2 == 0
    core, chip = jnp.where(even, last, first), jnp.where(even, first, last)
    if ready is not None:
        core = jnp.concatenate([ready[0], core], axis=1)
        chip = jnp.concatenate([ready[1], chip], axis=1)
    core_ref[...] = core
    chip_ref[...] = chip


def edge_shapes(columns):
    return [jax.ShapeDtypeStruct((8, columns // 8 * EDGE), F32)] * 2


def sims_kernel(scale, spans, others, fetch, pos_ref, table_ref, query_ref, *refs):
    pieces, refs = refs[: len(spans)], refs[len(spans) :]
    done, refs = refs[:others], refs[others:]
    out_ref = refs[0]
    if fetch:
        rows_ref, sems = refs[-2], refs[-1]
    regions, frames, channels = query_ref.shape
    width = 3 if regions % 3 == 0 else 1
    if fetch:
        copies, arriving = [], []
        start = 0
        for index, (span, piece) in enumerate(zip(spans, pieces)):
            rows = pl.ds(start, span * regions)
            copies.append(pltpu.make_async_copy(piece, rows_ref.at[rows, :], sems.at[index]))
            start += span * regions
        for copy in copies:
            copy.start()
        for step in range(regions // width):
            block = pl.ds(step * width, width)
            arriving.append(
                pltpu.make_async_copy(
                    query_ref.at[block], refs[1].at[block], sems.at[len(spans) + step]
                )
            )
        for copy in arriving:
            copy.start()
        query_ref = refs[1]
        for copy in copies:
            copy.wait()

    total = None
    for step in range(regions // width):
        if fetch:
            arriving[step].wait()
        rows = (
            rows_ref[...]
            if fetch
            else jnp.concatenate([piece[...] for piece in pieces], axis=0)
        )
        products = lax.dot_general(
            rows,
            query_ref[step * width : (step + 1) * width].reshape(-1, channels),
            (((1,), (1,)), ((), ())),
            preferred_element_type=F32,
        )
        parts = []
        start = 0
        for span in spans:
            best = products[start : start + span]
            for other in range(1, regions):
                best = jnp.maximum(
                    best, products[start + other * span : start + (other + 1) * span]
                )
            part = best[:, 0:frames]
            for other in range(1, width):
                part = part + best[:, other * frames : (other + 1) * frames]
            parts.append(part)
            start += span * regions
        part = jnp.concatenate(parts, axis=0)
        total = part if total is None else total + part
    active = table_ref[pos_ref[0], pos_ref[1]] == 1
    total = total * jnp.where(active, scale, 0.0).astype(F32)
    out_ref[...] = total
    if done:
        write_edges(pos_ref, [total], *refs[1:3], [ref[...] for ref in done])


def similarities(query, pieces, position, table, done=(), fetch=False):
    regions, frames, channels = query.shape
    spans = [piece.shape[0] // regions for piece in pieces]
    scale = 1.0 / (regions * math.sqrt(channels))
    rows = sum(spans)
    shapes = [jax.ShapeDtypeStruct((rows, frames), F32)]
    if done:
        shapes += edge_shapes(rows + done[0].shape[1] // EDGE * 8)
    steps = 0
    if fetch:
        shapes.append(pltpu.VMEM(query.shape, query.dtype))
        steps = regions
    smem = pl.BlockSpec(memory_space=pltpu.SMEM)
    vmem = pl.BlockSpec(memory_space=pltpu.VMEM)
    return pl.pallas_call(
        functools.partial(sims_kernel, scale, spans, len(done), fetch),
        in_specs=[smem, smem, pl.BlockSpec(memory_space=pltpu.HBM) if fetch else vmem]
        + [pl.BlockSpec(memory_space=pltpu.HBM) if fetch else vmem for _ in pieces]
        + [vmem for _ in done],
        out_specs=[vmem for _ in shapes],
        out_shape=shapes,
        scratch_shapes=[
            pltpu.VMEM((rows * regions, channels), BF),
            pltpu.SemaphoreType.DMA((len(pieces) + steps,)),
        ]
        if fetch
        else [],
        compiler_params=pltpu.CompilerParams(vmem_limit_bytes=GRANT),
        cost_estimate=pl.CostEstimate(
            flops=2 * rows * regions * regions * frames * channels,
            bytes_accessed=2 * channels * regions * rows,
            transcendentals=0,
        ),
        name="similarities",
    )(position, table, *(map(in_hbm, (query, *pieces)) if fetch else (query, *pieces)), *done)


def inside_columns(pos_ref, block, limits, count, halo):
    at = lax.broadcasted_iota(jnp.int32, (count, 128), 0) + (pos_ref[1] * block - halo)
    return jnp.where((at >= 0) & (at < limits[1]), 1.0, 0.0).astype(F32)


def inside_rows(pos_ref, block, limits, at):
    at = pos_ref[0] * block + at
    return jnp.where((at >= 0) & (at < limits[0]), 1.0, 0.0).astype(F32)


def first_map(sims_ref, w1_ref, b1_ref, y_ref, first_ref, pos_ref, block, limits, tiles):
    lanes = sims_ref.shape[2]
    sources = [(PHASES - 1, 0)] + [(phase, 1) for phase in range(PHASES)] + [(0, 2)]
    terms = len(sources) * WINDOW
    reach = PHASES * HALO + 1
    spots, start = [], 0
    for group, first, size in tiles:
        low = PHASES * GROUP * group - reach
        parts = []
        for phase, at in sources:
            base = sims_ref[phase, first + at : first + at + size, :]
            if low < 0:
                parts.append(base[:, lanes + low : lanes])
                parts.append(base[:, 0 : low + WINDOW])
            else:
                parts.append(base[:, low : low + WINDOW])
        window = jnp.concatenate(parts + [jnp.zeros((size, 128 - terms), F32)], axis=1)
        high = window.astype(BF).astype(F32)
        rest = pltpu.roll(window - high, terms, 1)
        again = pltpu.roll(high, 2 * terms - 128, 1)
        lane = lax.broadcasted_iota(jnp.int32, (size, 128), 1)
        row = slice(start, start + size)
        y_ref[row, 0:128] = jnp.where(lane < terms, high, rest).astype(BF)
        y_ref[row, 128:256] = jnp.where(lane < 2 * terms - 128, rest, again).astype(BF)
        spots.append(start)
        start += size

    keep_cols = inside_columns(pos_ref, block, limits, first_ref.shape[1], HALO)
    for member in range(GROUP):
        result = jnp.dot(
            y_ref[0:start, :],
            w1_ref[:, member * 512 : (member + 1) * 512],
            preferred_element_type=F32,
        )
        pooled = jnp.maximum(
            jnp.maximum(result[:, 0:128], result[:, 128:256]),
            jnp.maximum(result[:, 256:384], result[:, 384:512]),
        )
        pooled = jnp.maximum(pooled + b1_ref[...], 0.0)
        for (group, first, size), spot in zip(tiles, spots):
            at = group * GROUP + member
            keep = keep_cols[first : first + size] * inside_rows(
                pos_ref, block, limits, at - HALO
            )
            first_ref[at, first : first + size, :] = (
                (pooled[spot : spot + size] * keep).astype(BF).astype(F32)
            )


def first_tiles(block, frames, jf, late):
    groups = (block + 2 * HALO) // GROUP
    reach = PHASES * HALO + 1
    early, rest, whole = [], [], []
    for group in range(groups):
        low = PHASES * GROUP * group - reach
        if low >= 0 and low + WINDOW <= frames:
            early += [(group, 0, late)]
            rest += [(group, late, 2 * PIECE)]
        else:
            whole += [(group, 0, jf)]
    ends = [(group, late + 2 * PIECE, jf - late - 2 * PIECE) for group, _, _ in early]
    return early + ends, rest + whole


def second_map(first_ref, w2_ref, b2_ref, lhs_ref, second_ref, pos_ref, block, limits, tiles):
    jf = first_ref.shape[1]
    lane = lax.broadcasted_iota(jnp.int32, (jf, 128), 1)
    upper = lane < 64
    left = (lane // 32) % 2 == 0
    start, spots = 0, []
    for at, first, size in tiles:
        centre = first_ref[at + 1]
        across = jnp.where(upper, first_ref[at + 2], first_ref[at])
        row, cells = slice(start, start + size), slice(first, first + size)
        for index, value in enumerate((centre, across)):
            here = pltpu.roll(value, jf - 1, 0)
            beside = jnp.where(left, pltpu.roll(value, jf - 2, 0), value)
            lhs_ref[row, index * 256 : index * 256 + 128] = here[cells].astype(BF)
            lhs_ref[row, index * 256 + 128 : index * 256 + 256] = beside[cells].astype(BF)
        spots.append(start)
        start += size
    result = jnp.dot(lhs_ref[0:start, :], w2_ref[...], preferred_element_type=F32)
    pooled = jnp.maximum(result[:, 0:128], result[:, 128:256])
    pooled = jnp.maximum(pooled, pltpu.roll(pooled, 64, 1))
    pooled = jnp.maximum(pooled + b2_ref[...], 0.0)
    keep_cols = inside_columns(pos_ref, block, limits, second_ref.shape[1], 1)
    for (at, first, size), spot in zip(tiles, spots):
        cells = slice(first, first + size)
        keep = keep_cols[cells] * inside_rows(pos_ref, block, limits, at - 1)
        second_ref[at, cells, :] = (pooled[spot : spot + size] * keep).astype(BF).astype(F32)


def second_tiles(block, js, late, split):
    early, rest, whole = [], [], []
    for at in range(block + 2):
        if split and GROUP <= at < block + 2 - GROUP:
            early += [(at, 0, late - PIECE), (at, late + 2 * PIECE, js - late - 2 * PIECE)]
            rest += [(at, late - PIECE, 3 * PIECE)]
        else:
            whole += [(at, 0, js)]
    return early, rest + whole


def convolve(
    sims_ref, maps, weights, scratch, score_ref, pos_ref, block, limits, padding, tiles
):
    w1_ref, b1_ref, w2_ref, b2_ref, w3_ref, b3_ref, w4_ref, b4_ref = weights
    first_ref, second_ref = maps
    y_ref, lhs2_ref, lhs3_ref = scratch
    _, _, jt = padding
    first_map(sims_ref, w1_ref, b1_ref, y_ref, first_ref, pos_ref, block, limits, tiles[0])
    second_map(first_ref, w2_ref, b2_ref, lhs2_ref, second_ref, pos_ref, block, limits, tiles[1])

    upper = lax.broadcasted_iota(jnp.int32, (jt, 128), 1) < 64
    for at in range(block // 2):
        row = slice(at * jt, (at + 1) * jt)
        rows = [second_ref.at[2 * at + down] for down in range(4)]
        for down in range(4):
            pair = jnp.where(upper, rows[down][0:jt, :], rows[down][1 : 1 + jt, :])
            lhs3_ref[row, down * 128 : (down + 1) * 128] = pair.astype(BF)
        for half in range(2):
            pair = jnp.where(
                upper, rows[2 * half][2 : 2 + jt, :], rows[2 * half + 1][2 : 2 + jt, :]
            )
            lhs3_ref[row, (4 + half) * 128 : (5 + half) * 128] = pair.astype(BF)
    third = jnp.dot(lhs3_ref[...], w3_ref[...], preferred_element_type=F32)
    third = jnp.maximum(third + b3_ref[...], 0.0).astype(BF)
    flat = lax.dot_general(
        w4_ref[...], third, (((1,), (1,)), ((), ())), preferred_element_type=F32
    )
    flat = flat[0:8] + b4_ref[0]
    for at in range(block // 2):
        score_ref[2 * at : 2 * at + 2, :] = flat[0:2, at * jt : at * jt + block]


def pad_cells(cells):
    js = -(-(cells + 2) // 8) * 8
    return (max(-(-(cells + 4) // 8) * 8, js), js, -(-cells // 16) * 16)


def convolve_scratch(block, padding, tiles):
    _, _, jt = padding
    return [
        pltpu.VMEM((sum(size for _, _, size in tiles[0]), 256), BF),
        pltpu.VMEM((sum(size for _, _, size in tiles[1]), 512), BF),
        pltpu.VMEM((block // 2 * jt, 768), BF),
    ]


def place(pos_ref, sims_ref, sources, segments):
    for source, row, size, shard, cell in segments:
        if source < len(sources):
            rows = slice(3 + cell, 3 + cell + size)
            sims_ref[pos_ref[2 + shard], rows, 0 : sources[source].shape[1]] = sources[source][
                row : row + size, :
            ]


def place_edges(pos_ref, sims_ref, starts, segments, table, edge, side):
    for source, row, size, shard, cell in segments:
        for at in range(0, size, 8):
            start = starts[source] + row + at
            count = min(8, size - at)
            lane = start // 8 * EDGE
            sims_ref[pos_ref[table + shard], 3 + cell + at : 3 + cell + at + count, side] = edge[
                start % 8 : start % 8 + count, lane : lane + EDGE
            ]


def assemble_kernel(segments, tiles, block, limits, pos_ref, *refs):
    sources, refs = refs[:-11], refs[-11:]
    w1_ref, b1_ref, w2_ref, b2_ref, sims_ref, first_ref, second_ref, *rims, y_ref, lhs_ref = refs
    write_edges(pos_ref, [source[...] for source in sources], *rims)
    sims_ref[...] = jnp.zeros_like(sims_ref)
    place(pos_ref, sims_ref, sources, segments)
    first_map(sims_ref, w1_ref, b1_ref, y_ref, first_ref, pos_ref, block, limits, tiles[0])
    if tiles[1]:
        second_map(first_ref, w2_ref, b2_ref, lhs_ref, second_ref, pos_ref, block, limits, tiles[1])


def assembled(position, sources, segments, weights, tiles, block, limits):
    smem = pl.BlockSpec(memory_space=pltpu.SMEM)
    vmem = pl.BlockSpec(memory_space=pltpu.VMEM)
    frames = sources[0].shape[1]
    jf, js, jt = pad_cells(block)
    return pl.pallas_call(
        functools.partial(assemble_kernel, segments, tiles, block, limits),
        in_specs=[smem] + [vmem for _ in sources] + [vmem] * 4,
        out_specs=[vmem] * 5,
        out_shape=[
            jax.ShapeDtypeStruct((PHASES, block + 24, 2 * frames), F32),
            jax.ShapeDtypeStruct((block + 2 * HALO, jf, 128), F32),
            jax.ShapeDtypeStruct((block + 2, max(js, jt + 8), 128), F32),
        ]
        + edge_shapes(sum(source.shape[0] for source in sources)),
        scratch_shapes=[
            pltpu.VMEM((max(8, sum(size for _, _, size in part)), lanes), BF)
            for part, lanes in zip(tiles, (256, 512))
        ],
        compiler_params=pltpu.CompilerParams(vmem_limit_bytes=GRANT),
        cost_estimate=pl.CostEstimate(
            flops=1_000_000_000, bytes_accessed=500_000, transcendentals=0
        ),
        name="assemble",
    )(position, *sources, *weights)


def network_kernel(limits, padding, starts, segments, tiles, pos_ref, len_ref, *refs):
    (_, _, _, late_ref, core_ref, chip_ref), refs = refs[:6], refs[6:]
    weights, outs, scratch = refs[:8], refs[8:13], refs[13:]
    score_ref, peak_ref, sims_ref, *maps = outs
    block = score_ref.shape[0]
    last = len(starts) - 1
    place(
        pos_ref, sims_ref, [late_ref], [(0, *rest) for source, *rest in segments if source == last]
    )
    lanes = sims_ref.shape[2]
    above, below = slice(lanes - EDGE, lanes), slice(lanes // 2, lanes // 2 + EDGE)

    ends = (pos_ref[0] == 0) | (pos_ref[0] == limits[0] // block - 1)
    core, chip = core_ref[...], jnp.where(ends, 0.0, chip_ref[...])

    def edges(core_side, chip_side):
        place_edges(pos_ref, sims_ref, starts, segments, 6, core, core_side)
        place_edges(pos_ref, sims_ref, starts, segments, 10, chip, chip_side)

    pl.when(pos_ref[0] % 2 == 0)(lambda: edges(below, above))
    pl.when(pos_ref[0] % 2 == 1)(lambda: edges(above, below))
    convolve(
        sims_ref, maps, weights, scratch, score_ref, pos_ref, block, limits, padding, tiles
    )

    score = score_ref[...]
    videos = len_ref.shape[0]
    column = pos_ref[1] * block + lax.broadcasted_iota(jnp.int32, (block, block), 1)
    slot = lax.broadcasted_iota(jnp.int32, (block, 128), 1)
    start = jnp.int32(0)
    peaks = jnp.zeros((block, 128), F32)
    for video in range(videos):
        end = start + len_ref[video]
        member = (column >= start) & (column < end)
        best = jnp.max(jnp.where(member, score, -jnp.inf), axis=1, keepdims=True)
        peaks = jnp.where(slot == video, best, peaks)
        start = end
    peak_ref[...] = jnp.transpose(peaks)[0:videos]


def network(
    position, lengths, maps, late, edges, starts, segments, tiles, weights, block, limits
):
    smem = pl.BlockSpec(memory_space=pltpu.SMEM)
    vmem = pl.BlockSpec(memory_space=pltpu.VMEM)
    padding = pad_cells(block)
    arrays = [*maps, late, *edges]
    score, peaks, *_ = pl.pallas_call(
        functools.partial(network_kernel, limits, padding, starts, segments, tiles),
        in_specs=[smem, smem] + [vmem] * len(arrays) + [vmem] * 7 + [smem],
        out_specs=[vmem] * 5,
        out_shape=[
            jax.ShapeDtypeStruct((block, block), F32),
            jax.ShapeDtypeStruct((lengths.shape[0], block), F32),
            *[jax.ShapeDtypeStruct(array.shape, F32) for array in maps],
        ],
        scratch_shapes=convolve_scratch(block, padding, tiles),
        input_output_aliases={2: 2, 3: 3, 4: 4},
        cost_estimate=pl.CostEstimate(
            flops=6_000_000_000, bytes_accessed=4_000_000, transcendentals=0
        ),
        compiler_params=pltpu.CompilerParams(vmem_limit_bytes=GRANT),
        name="network",
    )(position, lengths, *arrays, *weights)
    return score, peaks


def weights_kernel(w1_ref, b1_ref, w2_ref, b2_ref, w3_ref, b3_ref, w4_ref, *outs):
    f1_ref, o1_ref, f2_ref, o2_ref, f3_ref, o3_ref, f4_ref = outs
    c1, c2, c3 = w1_ref.shape[2], w2_ref.shape[3], w3_ref.shape[3]
    rows = lax.broadcasted_iota(jnp.int32, (256, 16 * c1), 0)
    lane = lax.broadcasted_iota(jnp.int32, (256, 16 * c1), 1) // c1
    terms = 6 * WINDOW
    third = rows >= 2 * terms
    valid = rows < 3 * terms
    rows = rows - jnp.where(third, 2 * terms, jnp.where(rows >= terms, terms, 0))
    along = jnp.zeros_like(rows)
    for offset in range(1, 6):
        along = along + jnp.where(rows >= offset * WINDOW, 1, 0)
    down = rows - along * WINDOW - 2 * ((lane // 2) % 2) - lane // 8
    along = along - 2 * (lane % 2) - (lane // 4) % 2
    taps = []
    for di in range(3):
        for dj in range(3):
            tap = jnp.concatenate([w1_ref[di, dj : dj + 1, :]] * (128 // c1), axis=1)
            taps.append(jnp.concatenate([tap] * (16 * c1 // 128), axis=1))
    for member in range(GROUP):
        dense = jnp.zeros(rows.shape, F32)
        for di in range(3):
            for dj in range(3):
                here = (down == di + PHASES * member) & (along == dj) & valid
                dense = jnp.where(here, taps[3 * di + dj], dense)
        high = dense.astype(BF).astype(F32)
        at = slice(member * 16 * c1, (member + 1) * 16 * c1)
        f1_ref[:, at] = jnp.where(third, dense - high, high).astype(BF)
    o1_ref[...] = jnp.concatenate([b1_ref[...]] * (128 // c1), axis=1)
    o2_ref[...] = jnp.concatenate([b2_ref[...]] * (128 // c2), axis=1)
    f2_ref[...] = jnp.zeros_like(f2_ref)
    reach = ((0, 1), (2, -1))
    for index in range(16):
        row_kind, col_kind, sr, sc = (index >> 3) & 1, (index >> 2) & 1, (index >> 1) & 1, index & 1
        for phase in range(4):
            di = reach[row_kind][sr] - phase // 2 + 1
            dj = reach[col_kind][sc] - phase % 2 + 1
            if 0 <= di <= 2 and 0 <= dj <= 2:
                f2_ref[index * c1 : (index + 1) * c1, phase * c2 : (phase + 1) * c2] = w2_ref[
                    di, dj
                ]
    f3_ref[...] = jnp.zeros_like(f3_ref)
    order = [(row, col) for row in range(4) for col in range(2)] + [(row, 2) for row in range(4)]
    for index, (row, dj) in enumerate(order):
        for output in range(2):
            if 0 <= row - output <= 2:
                f3_ref[index * c2 : (index + 1) * c2, output * c3 : (output + 1) * c3] = w3_ref[
                    row - output, dj
                ]
    o3_ref[...] = jnp.concatenate([b3_ref[...]] * 2, axis=1)
    fourth = jnp.concatenate([w4_ref[...].astype(F32)] * 2, axis=1)
    half = lax.broadcasted_iota(jnp.int32, f4_ref.shape, 1) // c3
    output = lax.broadcasted_iota(jnp.int32, f4_ref.shape, 0)
    f4_ref[...] = jnp.where(half == output, fourth, 0.0).astype(BF)


def network_weights(w1, b1, w2, b2, w3, b3, w4, b4):
    c1, c2, c3 = w1.shape[2], w2.shape[2], w3.shape[2]
    shapes = [
        ((256, GROUP * 16 * c1), BF),
        ((1, 128), F32),
        ((16 * c1, 4 * c2), BF),
        ((1, 128), F32),
        ((12 * c2, 2 * c3), BF),
        ((1, 2 * c3), F32),
        ((16, 2 * c3), BF),
    ]
    f1, o1, f2, o2, f3, o3, f4 = pl.pallas_call(
        weights_kernel,
        out_shape=[jax.ShapeDtypeStruct(shape, dtype) for shape, dtype in shapes],
        cost_estimate=pl.CostEstimate(flops=100_000_000, bytes_accessed=4_000_000, transcendentals=0),
        compiler_params=pltpu.CompilerParams(vmem_limit_bytes=GRANT),
        name="weights",
    )(
        w1,
        b1[None],
        jnp.transpose(w2, (0, 1, 3, 2)),
        b2[None],
        jnp.transpose(w3, (0, 1, 3, 2)),
        b3[None],
        w4[None],
    )
    return (f1, o1, f2, o2, f3, o3, f4, b4)


def body(
    query_feats,
    ref_feats,
    pair_table,
    lengths,
    query_len,
    conv1_weight,
    conv1_bias,
    conv2_weight,
    conv2_bias,
    conv3_weight,
    conv3_bias,
    conv4_weight,
    conv4_bias,
):
    qry_index = lax.axis_index("qry")
    ref_index = lax.axis_index("ref")
    senders = lax.axis_size("qry")
    blocks = lax.axis_size("ref")
    frames, regions, channels = query_feats.shape
    rows = ref_feats.shape[0]
    block = frames // PHASES
    limits = (block * senders, block * blocks)
    count = rows // PIECE
    split = count >= 3 and senders == PHASES
    odd = qry_index % 2
    nearest = (qry_index + 2 * odd - 1) % senders
    entries = [qry_index, ref_index]
    for place in (qry_index, qry_index ^ 1, nearest):
        entries += [place ^ flip if split else flip for flip in range(PHASES)]
    position = jnp.stack([jnp.asarray(entry, jnp.int32) for entry in entries])
    query = jnp.transpose(query_feats, (1, 0, 2))
    own = jnp.transpose(ref_feats[:, 0], (1, 0, 2))
    chips = senders // 2
    across = [
        [(i, (i - 2 * step) % senders) for i in range(senders)] for step in range(1, chips)
    ]
    beside = [(i, i ^ 1) for i in range(senders)]

    if split:
        late = count // 2
        middle = [at for at in range(1, count - 1) if at != late]
        groups = [[0], [count - 1]] + [[at] for at in middle] + [[late]]
    else:
        groups = [list(range(count))]

    order = [at for group in groups for at in group]
    (piece,) = cut(own, order[:1])
    source, piece = lax.optimization_barrier((own, piece))
    whole = source.reshape(regions * rows, channels)
    cuts = [piece]
    if len(order) > 1:
        cuts += cut(source, order[1:])
    found = []
    for pairs in across:
        trips = []
        for piece in cuts:
            trips.append(shift(piece, "qry", pairs))
        found.append(trips)
    sibling = shift(whole, "qry", beside)
    weights = network_weights(
        conv1_weight,
        conv1_bias,
        conv2_weight,
        conv2_bias,
        conv3_weight,
        conv3_bias,
        conv4_weight,
        conv4_bias,
    )
    here, query = similarities(
        query, [whole, sibling], position, pair_table, fetch=True
    )
    sources, segments = [here], [(0, 0, rows, 0, 0), (0, rows, rows, 1, 0)]
    shard = 2
    last = []
    for pieces in found:
        pieces = list(pieces)
        for index, group in enumerate(groups):
            batch = []
            for at in group:
                piece = pieces.pop(0)
                batch += [piece, shift(piece, "qry", beside)]
            if split and index == len(groups) - 1:
                last = batch
                break
            here = similarities(query, batch, position, pair_table)[0]
            for order, at in enumerate(group):
                for half in range(2):
                    start = PIECE * (2 * order + half)
                    segments.append((len(sources), start, PIECE, shard + half, at * PIECE))
            sources.append(here)
        shard += 2
    if not split:
        tiles = [[None] * rows for _ in range(senders)]
        for source, row, size, place, cell in segments:
            for at in range(0, size, PIECE):
                tiles[place][cell + at] = sources[source][row + at : row + at + PIECE]
        tiles = [
            jnp.concatenate([part for part in parts if part is not None], axis=0)
            for parts in tiles
        ]
        sender = jnp.arange(senders, dtype=jnp.int32)
        step = (sender // 2 - qry_index // 2) % chips
        ordered = jnp.stack(tiles)[2 * step + ((sender % 2) ^ (qry_index % 2))]
        sims = ordered.reshape(senders // PHASES, PHASES, rows, frames).transpose(1, 2, 0, 3)
        sources = [sims.reshape(PHASES * block, frames)]
        segments = [(0, phase * block, block, phase, 0) for phase in range(PHASES)]

    def cells(low):
        parts = []
        for want in range(PHASES):
            for source, row, size, place, cell in segments:
                if place == want and cell <= low and low + HALO <= cell + size:
                    parts.append(sources[source][row + low - cell : row + low - cell + HALO])
        return jnp.concatenate(parts, axis=0)

    up = [(i, i + 1) for i in range(blocks - 1)]
    down = [(b, a) for a, b in up]
    right = shift(cells(0), "ref", down)
    left = shift(cells(block - HALO), "ref", up)
    for edge, cell in ((left, -HALO), (right, block)):
        segments += [(len(sources), HALO * k, HALO, k, cell) for k in range(PHASES)]
        sources.append(edge)
    jf, js, _ = pad_cells(block)
    spot = late * PIECE if split else 2 * PIECE
    firsts = first_tiles(block, frames, jf, spot)
    seconds = second_tiles(block, js, spot, split)
    *maps, core, chip = assembled(
        position, sources, segments, weights[:4], (firsts[0], seconds[0]), block, limits
    )
    if not split:
        firsts = first_tiles(block, 0, jf, spot)
    tiles = (firsts[1], seconds[1])
    if split:
        for half in range(2):
            segments.append((len(sources), PIECE * half, PIECE, 2 + half, late * PIECE))
        done, core, chip = similarities(
            query, last, position, pair_table, (core, chip)
        )
        sources.append(done)
    else:
        done = sources[-1]
    starts = [0]
    for source in sources[:-1]:
        starts.append(starts[-1] + source.shape[0])
    pairs = [(i, (i + 1) % senders) for i in range(1, senders, 2)]
    chip = shift(chip, "qry", pairs + [(b, a) for a, b in pairs])
    core = shift(core, "qry", beside)
    score_map, peaks = network(
        position,
        lengths,
        maps,
        done,
        (core, chip),
        starts,
        segments,
        tiles,
        weights,
        block,
        limits,
    )
    mine, other = peaks, shift(peaks, "qry", beside)
    peaks = jnp.where(odd == 1, jnp.stack([other, mine]), jnp.stack([mine, other]))

    def swap(array, flip_qry, flip_ref):
        pairs = [
            (q * blocks + r, (q ^ flip_qry) * blocks + (r ^ flip_ref))
            for q in range(senders)
            for r in range(blocks)
        ]
        return shift(array, ("qry", "ref"), pairs)

    bit = 1
    while bit < blocks:
        peaks = jnp.maximum(peaks, swap(peaks, 1, bit))
        bit *= 2
    first_row = (qry_index - odd) * block
    row_ids = first_row + jnp.arange(2 * block, dtype=jnp.int32).reshape(2, 1, block)
    total = jnp.sum(jnp.where(row_ids < query_len[0], peaks, 0.0), axis=(0, 2))
    bit = 2
    while bit < senders:
        total = total + swap(total, bit + 1, 0)
        bit *= 2
    return (score_map, total / query_len[0].astype(F32))


def solution(mesh):
    placed = (
        P(("groups", "qry"), None, None),
        P(("groups", "ref"), "qry", None, None),
        P("groups", None),
        P("groups"),
        P("groups"),
    ) + (P(),) * 8

    return jax.shard_map(
        body,
        mesh=mesh,
        in_specs=placed,
        out_specs=(P(("groups", "qry"), "ref"), P("groups")),
        check_vma=False,
    )
```
